32 devices in a mesh: freq: 8 (over z, y), tm: 4 (over x, core).
Axes of the slice: x: 2, y: 2, z: 4, core: 2. Of those that a mesh axis runs over, the one named last changes fastest.
Arguments:
- visibility: bfloat16 [8, 4, 8, 4096], P('freq', 'tm'), may hold values from -6 to 6
- model_visibility: bfloat16 [8, 4, 8, 4096], P('freq', 'tm'), may hold values from -6 to 6
- keep_mask: int32 [8, 4, 4096], P('freq', 'tm'), may hold values 0 or 1
- gains_in: float32 [8, 8, 512], P('freq'), may hold values from -6 to 6
- consensus_in: float32 [8, 8, 512], P('freq'), may hold values from -6 to 6
- dual_in: float32 [8, 8, 512], P('freq'), may hold values from -4 to 4
- penalty: float32 [512], replicated, may hold values from 30 to 600
- channel_index: int32 [8], P('freq'), may hold values from 0 to 7, each once
- first_station: int32 [4096], replicated, may hold values from 0 to 511, as said below
- second_station: int32 [4096], replicated, may hold values from 0 to 511
Outputs:
- gains_out: float32 [8, 8, 512], P('freq', None, 'tm')
- consensus_out: float32 [8, 8, 512], P('freq', None, 'tm')
- dual_out: float32 [8, 8, 512], P('freq', None, 'tm')
The draws below stay inside these ranges and needn't reach their ends.
Inputs may be any that keep to these rules, and one draw needn't show every extreme that they name: first_station and second_station of a baseline differ; station numbers repeat over baselines. channel_index holds each channel number once.
All inputs are finite; a program needn't handle non-finite values. No bound on the sum of `keep_mask` on one device may be relied on, other than what follows from the above.
Results may differ from the reference program's by a relative error of at most 0.0003.
Values sent between devices are 32-bit elements; how exact they have to be, the bound alone decides.
No kernel may reach another device: no remote copies, remote signals or barrier semaphores. Data moves between devices by JAX's collectives and lax.ppermute only.
A program may use at most 64 MiB of HBM per device.

```python
import math
import jax
import jax.numpy as jnp
from jax import lax

STATION_COUNT = 512
BASELINE_COUNT = 4096
SWEEPS = 2
CHANNEL_COUNT = 8
TIME_SLOT_COUNT = 4


def station_pairs(key):
    pair_key = jax.random.fold_in(key, 11)
    leading_key, key_shift = jax.random.split(pair_key)
    leading_entry = jax.random.randint(leading_key, (BASELINE_COUNT,), 0, STATION_COUNT)
    start_shift = jax.random.randint(key_shift, (BASELINE_COUNT,), 1, STATION_COUNT)
    time_slots = jnp.arange(BASELINE_COUNT)
    leading_entry = jnp.where(time_slots == 0, STATION_COUNT - 1, jnp.where(time_slots == 1, 0, leading_entry))
    start_shift = jnp.where(time_slots == 0, 1, jnp.where(time_slots == 1, STATION_COUNT - 1, start_shift))
    second = (leading_entry + start_shift) % STATION_COUNT
    return (leading_entry.astype(jnp.int32), second.astype(jnp.int32))


def draw_first_station(key, part):
    return station_pairs(key)[0]


def draw_second_station(key, part):
    return station_pairs(key)[1]


def plant(values, key, least, largest):
    longest = values.shape.index(max(values.shape))
    spots = []
    for shift in (0, 1):
        where = [jax.random.randint(jax.random.fold_in(key, axis), (), 0, length) for axis, length in enumerate(values.shape)]
        where[longest] = (where[longest] + shift) % values.shape[longest]
        spots.append(tuple(where))
    return values.at[spots[0]].set(least).at[spots[1]].set(largest)


def shard_levels(key, shape, shards, least, largest):
    level, own = 1.0, jax.random.fold_in(key, 6)
    for axis_at, parts in shards:
        steps = jnp.exp(jax.random.uniform(jax.random.fold_in(own, axis_at), (parts,), jnp.float32, least / len(shards), largest / len(shards)))
        level = level * jnp.repeat(steps, shape[axis_at] // parts).reshape([-1 if axis == axis_at else 1 for axis in range(len(shape))])
    return level


def scatter_about(stream_key, shape, width, limit, cuts=(), kind=jnp.bfloat16):
    gain = shard_levels(stream_key, shape, cuts, -0.22, 0.18) if cuts else 1.0
    values = jax.random.normal(stream_key, shape, jnp.float32) * width * gain
    return jnp.minimum(jnp.maximum(values, -limit), limit).astype(kind)


def setup_inputs(seed: int = 0) -> dict:
    splits = jax.random.split(jax.random.key(seed), 11)
    visibility = scatter_about(splits[0], (CHANNEL_COUNT, TIME_SLOT_COUNT, 8, BASELINE_COUNT), 1.0, 6.0, ((0, 8), (1, 4)))
    model_visibility = scatter_about(splits[1], (CHANNEL_COUNT, TIME_SLOT_COUNT, 8, BASELINE_COUNT), 0.7, 6.0, ((0, 8), (1, 4)))
    keep_mask = plant((jax.random.randint(splits[2], (CHANNEL_COUNT, TIME_SLOT_COUNT, BASELINE_COUNT), 0, 4) < 3).astype(jnp.int32), jax.random.fold_in(splits[2], 1), 0, 1)
    gains_in = scatter_about(splits[3], (CHANNEL_COUNT, 8, STATION_COUNT), 0.7, 6.0, ((0, 8),), jnp.float32)
    consensus_in = scatter_about(splits[4], (CHANNEL_COUNT, 8, STATION_COUNT), 0.7, 6.0, ((0, 8),), jnp.float32)
    dual_in = scatter_about(splits[5], (CHANNEL_COUNT, 8, STATION_COUNT), 0.3, 4.0, ((0, 8),), jnp.float32)
    penalty = jnp.clip(jnp.exp(jax.random.uniform(splits[6], (STATION_COUNT,), jnp.float32, math.log(30.0), math.log(600.0))), 30.0, 600.0)
    channel_index = jax.random.permutation(splits[7], CHANNEL_COUNT).astype(jnp.int32)
    first_station = draw_first_station(jax.random.fold_in(splits[10], 71), 0)
    second_station = draw_second_station(jax.random.fold_in(splits[10], 71), 0)
    return {"visibility": visibility, "model_visibility": model_visibility, "keep_mask": keep_mask, "gains_in": gains_in, "consensus_in": consensus_in, "dual_in": dual_in, "penalty": penalty, "channel_index": channel_index, "first_station": first_station, "second_station": second_station}


def entries(array, axis):
    return [(lax.index_in_dim(array, 2 * index, axis, False), lax.index_in_dim(array, 2 * index + 1, axis, False)) for index in range(4)]

def stack_jones(matrix, axis):
    return jnp.stack([matrix[index][part] for index in range(4) for part in range(2)], axis=axis)

def complex_mul(leading_entry, second):
    return (leading_entry[0] * second[0] - leading_entry[1] * second[1], leading_entry[0] * second[1] + leading_entry[1] * second[0])

def complex_add(leading_entry, second):
    return (leading_entry[0] + second[0], leading_entry[1] + second[1])

def matrix_mul(leading_entry, second):
    return [complex_add(complex_mul(leading_entry[0], second[0]), complex_mul(leading_entry[1], second[2])), complex_add(complex_mul(leading_entry[0], second[1]), complex_mul(leading_entry[1], second[3])), complex_add(complex_mul(leading_entry[2], second[0]), complex_mul(leading_entry[3], second[2])), complex_add(complex_mul(leading_entry[2], second[1]), complex_mul(leading_entry[3], second[3]))]

def adjoint(matrix):
    return [(matrix[0][0], -matrix[0][1]), (matrix[2][0], -matrix[2][1]), (matrix[1][0], -matrix[1][1]), (matrix[3][0], -matrix[3][1])]

def weighted(matrix, weight):
    return [(entry[0] * weight, entry[1] * weight) for entry in matrix]

def normal_sums(vis_block, model_block, flag_block, gains, first_station, second_station):
    stations = gains.shape[2]
    gains_first = jnp.take(gains, first_station, axis=2)[:, None]
    gains_second = jnp.take(gains, second_station, axis=2)[:, None]
    observed = entries(vis_block.astype(jnp.float32), 2)
    modelled = entries(model_block.astype(jnp.float32), 2)
    weight = flag_block.astype(jnp.float32)
    left = matrix_mul(modelled, adjoint(entries(gains_second, 2)))
    right = matrix_mul(adjoint(modelled), adjoint(entries(gains_first, 2)))
    num_first = weighted(matrix_mul(observed, adjoint(left)), weight)
    den_first = weighted(matrix_mul(left, adjoint(left)), weight)
    num_second = weighted(matrix_mul(adjoint(observed), adjoint(right)), weight)
    den_second = weighted(matrix_mul(right, adjoint(right)), weight)
    term_first = jnp.sum(jnp.concatenate([stack_jones(num_first, 1), stack_jones(den_first, 1)], axis=1), axis=2)
    term_second = jnp.sum(jnp.concatenate([stack_jones(num_second, 1), stack_jones(den_second, 1)], axis=1), axis=2)
    totals = jnp.zeros((gains.shape[0], 16, stations), jnp.float32)
    totals = totals.at[:, :, first_station].add(term_first)
    return totals.at[:, :, second_station].add(term_second)

def solve_jones(totals, gains_old, consensus, dual, penalty):
    numer = entries(totals[:, :8], 1)
    denom = entries(totals[:, 8:], 1)
    target = entries(consensus - dual, 1)
    rhs_side = [(numer[index][0] + penalty * target[index][0], numer[index][1] + penalty * target[index][1]) for index in range(4)]
    regular = [(denom[0][0] + penalty, denom[0][1]), denom[1], denom[2], (denom[3][0] + penalty, denom[3][1])]
    determ = complex_add(complex_mul(regular[0], regular[3]), complex_mul((-regular[1][0], -regular[1][1]), regular[2]))
    magnitude = determ[0] * determ[0] + determ[1] * determ[1]
    recip = (determ[0] / magnitude, -determ[1] / magnitude)
    inverse = [complex_mul(regular[3], recip), complex_mul((-regular[1][0], -regular[1][1]), recip), complex_mul((-regular[2][0], -regular[2][1]), recip), complex_mul(regular[0], recip)]
    solved = stack_jones(matrix_mul(rhs_side, inverse), 1)
    return 0.5 * (solved + gains_old)

def legendre(position):
    square = position * position
    return jnp.stack([jnp.ones_like(position), position, 1.5 * square - 0.5, (2.5 * square - 1.5) * position], axis=-1)

def channel_basis(index, total):
    return legendre(2.0 * index.astype(jnp.float32) / (total - 1.0) - 1.0)

def poly_fit(moments, total):
    basis_all = channel_basis(jnp.arange(total, dtype=jnp.int32), float(total))
    gram = jnp.dot(basis_all.T, basis_all, precision=lax.Precision.HIGHEST)
    factor = jnp.linalg.cholesky(gram)
    flat = moments.reshape(4, -1)
    middle = lax.linalg.triangular_solve(factor, flat, left_side=True, lower=True)
    coeffs = lax.linalg.triangular_solve(factor, middle, left_side=True, lower=True, transpose_a=True)
    return coeffs.reshape(moments.shape)

def reference(visibility, model_visibility, keep_mask, gains_in, consensus_in, dual_in, penalty, channel_index, first_station, second_station):

    def per_channel(items):
        vis_block, model_block, flag_block, gains, consensus, dual = [item[None] for item in items]
        for sweep_index in range(SWEEPS):
            totals = normal_sums(vis_block, model_block, flag_block, gains, first_station, second_station)
            gains = solve_jones(totals, gains, consensus, dual, penalty)
        return gains[0]
    gains_out = lax.map(per_channel, (visibility, model_visibility, keep_mask, gains_in, consensus_in, dual_in))
    basis = channel_basis(channel_index, float(CHANNEL_COUNT))
    moments = jnp.einsum('fk,fjs->kjs', basis, gains_out + dual_in, precision=lax.Precision.HIGHEST)
    coeffs = poly_fit(moments, CHANNEL_COUNT)
    consensus_out = jnp.einsum('fk,kjs->fjs', basis, coeffs, precision=lax.Precision.HIGHEST)
    dual_out = dual_in + gains_out - consensus_out
    return (gains_out, consensus_out, dual_out)
```

```python
import jax
import jax.numpy as jnp
import numpy as np
from jax import lax
from jax.experimental import pallas as pl
from jax.experimental.pallas import tpu as pltpu
from jax.sharding import PartitionSpec as P

SWEEPS = 2
LANES = 128
SUBS = 8
LO = 256
ROWS = 16
SPLITS = 2
PRODS = 48


def vmem():
    return pl.BlockSpec(memory_space=pltpu.VMEM)


def smem():
    return pl.BlockSpec(memory_space=pltpu.SMEM)


def split_bf16(value):
    parts = []
    for index in range(SPLITS):
        part = value.astype(jnp.bfloat16)
        parts.append(part)
        if index + 1 < SPLITS:
            value = value - part.astype(jnp.float32)
    return parts


def mul_conj(a, b):
    return (a[0] * b[0] + a[1] * b[1], a[1] * b[0] - a[0] * b[1])


def widen_kernel(vis_ref, model_ref, keep_ref, out_ref):
    tiles = vis_ref.shape[1] // LANES
    for tile in range(tiles):
        lanes = pl.ds(tile * LANES, LANES)
        keep = keep_ref[:, lanes].astype(jnp.float32)
        out_ref[pl.ds(tile * SUBS, SUBS), :] = vis_ref[:, lanes].astype(jnp.float32)
        out_ref[pl.ds((tiles + tile) * SUBS, SUBS), :] = (
            model_ref[:, lanes].astype(jnp.float32) * keep
        )


def slot_products(slot_ref, group, tiles):
    def load(part, component):
        start = (part * tiles + group * SUBS) * SUBS + component
        return slot_ref[pl.ds(start, SUBS, stride=SUBS), :]

    seen = [(load(0, 2 * e), load(0, 2 * e + 1)) for e in range(4)]
    model = [(load(1, 2 * e), load(1, 2 * e + 1)) for e in range(4)]
    rows = []
    for v in range(4):
        for m in range(4):
            rows.extend(mul_conj(seen[v], model[m]))
    rows.extend(entry[0] * entry[0] + entry[1] * entry[1] for entry in model)
    for left, right in ((0, 1), (2, 3), (0, 2), (1, 3)):
        rows.extend(mul_conj(model[left], model[right]))
    a = mul_conj(model[0], model[3])
    b = mul_conj(model[1], model[2])
    rows.extend((a[0] + b[0], a[0] - b[0], a[1] + b[1], a[1] - b[1]))
    return rows


def add_products(slot_refs, before_ref, out_ref):
    tiles = slot_refs[0].shape[0] // (2 * SUBS)
    for group in range(tiles // SUBS):
        at = pl.ds(group * SUBS, SUBS)
        total = None
        for slot_ref in slot_refs:
            rows = slot_products(slot_ref, group, tiles)
            total = rows if total is None else [x + y for x, y in zip(total, rows)]
        for index, row in enumerate(total):
            if before_ref is not None:
                row = row + before_ref[index, at, :]
            out_ref[index, at, :] = row


def tables_kernel(count, *refs):
    first_ref, second_ref = refs[:2]
    slot_refs = refs[2 : 2 + count]
    hot_ref, prod_ref = refs[2 + count :]
    baselines = first_ref.shape[1]
    step = 512
    for part, station_ref in enumerate((first_ref, second_ref)):
        for start in range(0, baselines, step):
            offset = station_ref[:, pl.ds(start, step)] & (LO - 1)
            row = lax.broadcasted_iota(jnp.int32, (LO, step), 0)
            hot_ref[:, pl.ds(part * baselines + start, step)] = jnp.where(
                row == offset, 1.0, 0.0
            ).astype(jnp.bfloat16)
    add_products(slot_refs, None, prod_ref)


def more_kernel(slot_ref, before_ref, out_ref):
    add_products([slot_ref], before_ref, out_ref)


def gram_rows(gain):
    entry = [(gain[2 * e : 2 * e + 1], gain[2 * e + 1 : 2 * e + 2]) for e in range(4)]
    h00 = sum(part * part for part in entry[0] + entry[2])
    h11 = sum(part * part for part in entry[1] + entry[3])
    top = mul_conj(entry[1], entry[0])
    low = mul_conj(entry[3], entry[2])
    zero = jnp.zeros((ROWS - 12, gain.shape[1]), jnp.float32)
    return jnp.concatenate([gain, h00, h11, top[0] + low[0], top[1] + low[1], zero], axis=0)


def baseline_terms(prod, gain_second, gain_first):
    def num(gain, swap):
        out = []
        for i in range(2):
            for l in range(2):
                real = imag = None
                for j in range(2):
                    for k in range(2):
                        if swap:
                            index = 4 * (2 * j + i) + 2 * k + l
                        else:
                            index = 4 * (2 * i + j) + 2 * l + k
                        tr, ti = prod(2 * index), prod(2 * index + 1)
                        gr, gi = gain[2 * (2 * j + k)], gain[2 * (2 * j + k) + 1]
                        if swap:
                            addr, addi = tr * gr + ti * gi, tr * gi - ti * gr
                        else:
                            addr, addi = tr * gr - ti * gi, tr * gi + ti * gr
                        real = addr if real is None else real + addr
                        imag = addi if imag is None else imag + addi
                out.extend((real, imag))
        return out

    n00, n01, n10, n11, pr, pi, qr, qi, rr, ri, sr, si, apr, amr, api, ami = (
        prod(32 + index) for index in range(16)
    )
    h00, h11, hr, hi = gain_second[8:12]
    den_first = [
        n00 * h00 + n01 * h11 + 2.0 * (pr * hr - pi * hi),
        n10 * h00 + n11 * h11 + 2.0 * (qr * hr - qi * hi),
        rr * h00 + sr * h11 + apr * hr - ami * hi,
        ri * h00 + si * h11 + api * hr + amr * hi,
    ]
    h00, h11, hr, hi = gain_first[8:12]
    den_second = [
        n00 * h00 + n10 * h11 + 2.0 * (rr * hr + ri * hi),
        n01 * h00 + n11 * h11 + 2.0 * (sr * hr + si * hi),
        pr * h00 + qr * h11 + apr * hr + api * hi,
        amr * hi - pi * h00 - qi * h11 - ami * hr,
    ]
    return num(gain_second, False) + den_first, num(gain_first, True) + den_second


def solve(total, gain, target, penalty):
    def row(array, index):
        return array[index : index + 1]

    rhs = [
        tuple(
            row(total, 2 * e + part) + penalty * row(target, 2 * e + part) for part in range(2)
        )
        for e in range(4)
    ]
    r00, r11 = row(total, 8) + penalty, row(total, 9) + penalty
    r01 = (row(total, 10), row(total, 11))
    scale = 1.0 / (r00 * r11 - (r01[0] * r01[0] + r01[1] * r01[1]))
    out = []
    for i in range(2):
        a, b = rhs[2 * i], rhs[2 * i + 1]
        cross = mul_conj(b, r01)
        out.extend(((a[part] * r11 - cross[part]) * scale for part in range(2)))
        out.append((b[0] * r00 - (a[0] * r01[0] - a[1] * r01[1])) * scale)
        out.append((b[1] * r00 - (a[0] * r01[1] + a[1] * r01[0])) * scale)
    return 0.5 * (jnp.concatenate(out, axis=0) + gain)


def sweeps_kernel(
    place_ref,
    channel_ref,
    first_ref,
    second_ref,
    gains_ref,
    consensus_ref,
    dual_ref,
    penalty_ref,
    hot_ref,
    before_ref,
    *rest,
):
    count = len(rest) - 7
    slot_refs = rest[:count]
    gain_out_ref, send_ref, prod_ref, seen_ref, term_ref, lhs_ref, full_ref = rest[count:]
    baselines = first_ref.shape[1]
    stations = gains_ref.shape[1]
    blocks = stations // LO
    tiles = baselines // LANES
    add_products(slot_refs, before_ref, prod_ref)
    term_ref[...] = jnp.zeros(term_ref.shape, jnp.float32)
    block_of = [ref[...] >> 8 for ref in (first_ref, second_ref)]
    gains = [gains_ref[:, pl.ds(h * LO, LO)] for h in range(blocks)]
    target = [
        consensus_ref[:, pl.ds(h * LO, LO)] - dual_ref[:, pl.ds(h * LO, LO)]
        for h in range(blocks)
    ]
    penalty = [penalty_ref[:, pl.ds(h * LO, LO)] for h in range(blocks)]
    for _ in range(SWEEPS):
        table = jnp.concatenate([gram_rows(gain) for gain in gains], axis=0)
        table = jnp.concatenate(split_bf16(table), axis=0)
        for part in range(2):
            found = jnp.dot(
                table,
                hot_ref[:, pl.ds(part * baselines, baselines)],
                preferred_element_type=jnp.float32,
            )
            high = blocks * ROWS
            found = sum(found[index * high : (index + 1) * high] for index in range(SPLITS))
            chosen = found[:ROWS]
            for h in range(1, blocks):
                chosen = jnp.where(
                    block_of[part] == h, found[h * ROWS : (h + 1) * ROWS], chosen
                )
            for tile in range(tiles):
                seen_ref[part, pl.ds(tile * ROWS, ROWS), :] = chosen[
                    :, tile * LANES : (tile + 1) * LANES
                ]
        for group in range(tiles // SUBS):
            start = group * SUBS * ROWS

            def prod(index):
                return prod_ref[index, pl.ds(group * SUBS, SUBS), :]

            gain_first, gain_second = (
                [seen_ref[part, pl.ds(start + j, SUBS, stride=ROWS), :] for j in range(12)]
                for part in range(2)
            )
            for part, rows in enumerate(baseline_terms(prod, gain_second, gain_first)):
                for j, row in enumerate(rows):
                    term_ref[part, pl.ds(start + j, SUBS, stride=ROWS), :] = row
        for part in range(2):
            for tile in range(tiles):
                lanes = slice(tile * LANES, (tile + 1) * LANES)
                block = block_of[part][:, lanes]
                value = term_ref[part, pl.ds(tile * ROWS, ROWS), :]
                rows = []
                for h in range(blocks):
                    rows.append(split_bf16(jnp.where(block == h, value, 0.0)))
                for index in range(SPLITS):
                    for h in range(blocks):
                        lhs_ref[
                            pl.ds((index * blocks + h) * ROWS, ROWS),
                            pl.ds(part * baselines + tile * LANES, LANES),
                        ] = rows[h][index]
        summed = lax.dot_general(
            lhs_ref[...],
            hot_ref[...],
            (((1,), (1,)), ((), ())),
            preferred_element_type=jnp.float32,
        )
        high = blocks * ROWS
        summed = sum(summed[index * high : (index + 1) * high] for index in range(SPLITS))
        gains = [
            solve(summed[h * ROWS : (h + 1) * ROWS], gains[h], target[h], penalty[h])
            for h in range(blocks)
        ]
    for h in range(blocks):
        full_ref[:, pl.ds(h * LO, LO)] = gains[h]
    width = gain_out_ref.shape[1]
    own = pl.ds(pl.multiple_of(place_ref[0] * width, width), width)
    part = full_ref[:, own]
    gain_out_ref[...] = part
    channels = send_ref.shape[0]
    mark = jnp.full((SUBS, width), channel_ref[0].astype(jnp.float32))
    combined = part + dual_ref[:, own]
    for channel in range(channels):
        send_ref[channel, :SUBS, :] = combined
        send_ref[channel, SUBS:, :] = mark


def legendre(position):
    square = position * position
    return [None, position, 1.5 * square - 0.5, (2.5 * square - 1.5) * position]


def fit_kernel(gram_factor, place_ref, channel_ref, parts_ref, gain_ref, dual_ref, *out_refs):
    consensus_ref, dual_out_ref = out_refs
    channels = parts_ref.shape[0]
    width = gain_ref.shape[1]
    scale = float(channels) - 1.0

    def basis(channel):
        return legendre(2.0 * channel / scale - 1.0)

    moments = [None] * 4
    for channel in range(channels):
        value = parts_ref[channel, :SUBS, :]
        for k, weight in enumerate(basis(parts_ref[channel, SUBS:, :])):
            add = value if weight is None else weight * value
            moments[k] = add if moments[k] is None else moments[k] + add
    middle = []
    for k in range(4):
        rest = moments[k]
        for earlier in range(k):
            rest = rest - gram_factor[k][earlier] * middle[earlier]
        middle.append(rest * (1.0 / gram_factor[k][k]))
    coeffs = [None] * 4
    for k in reversed(range(4)):
        rest = middle[k]
        for later in range(k + 1, 4):
            rest = rest - gram_factor[later][k] * coeffs[later]
        coeffs[k] = rest * (1.0 / gram_factor[k][k])
    own = basis(jnp.full((SUBS, width), channel_ref[0].astype(jnp.float32)))
    fitted = coeffs[0]
    for k in range(1, 4):
        fitted = fitted + own[k] * coeffs[k]
    consensus_ref[...] = fitted
    start = pl.multiple_of(place_ref[0] * width, width)
    dual_out_ref[...] = dual_ref[:, pl.ds(start, width)] + gain_ref[...] - fitted


def gram_cholesky(channels):
    x = 2.0 * np.arange(channels, dtype=np.float64) / (channels - 1.0) - 1.0
    basis = np.stack([np.ones_like(x), x, 1.5 * x * x - 0.5, (2.5 * x * x - 1.5) * x], -1)
    factor = np.linalg.cholesky(basis.T @ basis)
    return [[float(value) for value in row] for row in factor]


def call(kernel, shapes, spaces, scratch=()):
    single = isinstance(shapes, jax.ShapeDtypeStruct)
    return pl.pallas_call(
        kernel,
        out_shape=shapes,
        in_specs=[smem() if space == "s" else vmem() for space in spaces],
        out_specs=vmem() if single else [vmem() for _ in shapes],
        scratch_shapes=list(scratch),
    )


def shards(
    visibility,
    model_visibility,
    keep_mask,
    gains_in,
    consensus_in,
    dual_in,
    penalty,
    channel_index,
    first_station,
    second_station,
):
    f32 = jnp.float32
    baselines = visibility.shape[3]
    stations = gains_in.shape[2]
    slots = lax.axis_size("tm")
    channels = lax.axis_size("freq")
    width = stations // slots
    tiles = baselines // LANES
    blocks = stations // LO
    shape = jax.ShapeDtypeStruct
    place = lax.axis_index("tm").astype(jnp.int32).reshape(1)

    def swap(array, step):
        return lax.ppermute(array, "tm", [(i, i ^ step) for i in range(slots)])

    own = call(widen_kernel, shape((2 * tiles * SUBS, LANES), f32), "vvv")(
        visibility.reshape(SUBS, baselines),
        model_visibility.reshape(SUBS, baselines),
        keep_mask.reshape(1, baselines),
    )
    held = [own]
    step = slots // 2
    while step:
        held += [swap(array, step) for array in held]
        step //= 2
    first = first_station.reshape(1, baselines)
    second = second_station.reshape(1, baselines)
    products = shape((PRODS, tiles, LANES), f32)
    half = slots // 2
    near = [held[0], held[half]]
    hot, summed = call(
        lambda *refs: tables_kernel(len(near), *refs),
        [shape((LO, 2 * baselines), jnp.bfloat16), products],
        "vv" + "v" * len(near),
    )(first, second, *near)
    far = [array for index, array in enumerate(held) if index not in (0, half)]
    for array in far[: half - 1]:
        summed = call(more_kernel, products, "vv")(array, summed)
    rest = far[half - 1 :]
    gains, consensus, dual = (
        array.reshape(SUBS, stations) for array in (gains_in, consensus_in, dual_in)
    )
    gain_part, send = call(
        sweeps_kernel,
        [shape((SUBS, width), f32), shape((channels, 2 * SUBS, width), f32)],
        "ss" + "v" * (8 + len(rest)),
        [
            pltpu.VMEM((PRODS, tiles, LANES), f32),
            pltpu.VMEM((2, tiles * ROWS, LANES), f32),
            pltpu.VMEM((2, tiles * ROWS, LANES), f32),
            pltpu.VMEM((SPLITS * blocks * ROWS, 2 * baselines), jnp.bfloat16),
            pltpu.VMEM((SUBS, stations), f32),
        ],
    )(
        place,
        channel_index,
        first,
        second,
        gains,
        consensus,
        dual,
        penalty.reshape(1, stations),
        hot,
        summed,
        *rest,
    )
    parts = lax.all_to_all(send, "freq", 0, 0)
    factor = gram_cholesky(channels)
    consensus_out, dual_out = call(
        lambda *refs: fit_kernel(factor, *refs),
        [shape((SUBS, width), f32), shape((SUBS, width), f32)],
        "ssvvv",
    )(place, channel_index, parts, gain_part, dual)
    return tuple(array[None] for array in (gain_part, consensus_out, dual_out))


def solution(mesh):
    placed = (
        P("freq", "tm", None, None),
        P("freq", "tm", None, None),
        P("freq", "tm", None),
        P("freq", None, None),
        P("freq", None, None),
        P("freq", None, None),
        P(),
        P("freq"),
        P(),
        P(),
    )
    return jax.shard_map(
        shards,
        mesh=mesh,
        in_specs=placed,
        out_specs=(P("freq", None, "tm"), P("freq", None, "tm"), P("freq", None, "tm")),
        check_vma=False,
    )
```

```python
import jax
import jax.numpy as jnp
import numpy as np
from jax import lax
from jax.experimental import pallas as pl
from jax.experimental.pallas import tpu as pltpu
from jax.sharding import PartitionSpec as P

SWEEPS = 2
LANES = 128
SUBS = 8
PRODS = 48
TERMS = 24
PACK = 16
F32 = jnp.float32
BF16 = jnp.bfloat16


def mul_conj(a, b):
    return (a[0] * b[0] + a[1] * b[1], a[1] * b[0] - a[0] * b[1])


def copy_in(pairs, sem):
    copies = [
        pltpu.make_async_copy(source, target, sem.at[index])
        for index, (source, target) in enumerate(pairs)
    ]
    for copy in copies:
        copy.start()
    return copies


def widen_kernel(vis_hbm, model_hbm, keep_hbm, out_ref, vis_ref, model_ref, keep_ref, sem):
    copies = copy_in(
        [(vis_hbm, vis_ref), (keep_hbm, keep_ref), (model_hbm, model_ref)], sem
    )
    tiles = vis_ref.shape[1] // LANES
    copies[0].wait()
    for tile in range(tiles):
        lanes = pl.ds(tile * LANES, LANES)
        out_ref[pl.ds(tile * SUBS, SUBS), :] = vis_ref[:, lanes].astype(F32)
    copies[1].wait()
    copies[2].wait()
    for tile in range(tiles):
        lanes = pl.ds(tile * LANES, LANES)
        out_ref[pl.ds((tiles + tile) * SUBS, SUBS), :] = model_ref[:, lanes].astype(
            F32
        ) * keep_ref[:, lanes].astype(F32)


def slot_products(slot_ref, group, tiles):
    def load(part, component):
        start = (part * tiles + group * SUBS) * SUBS + component
        return slot_ref[pl.ds(start, SUBS, stride=SUBS), :]

    seen = [(load(0, 2 * e), load(0, 2 * e + 1)) for e in range(4)]
    model = [(load(1, 2 * e), load(1, 2 * e + 1)) for e in range(4)]
    rows = []
    for v in range(4):
        for m in range(4):
            rows.extend(mul_conj(seen[v], model[m]))
    rows.extend(entry[0] * entry[0] + entry[1] * entry[1] for entry in model)
    for left, right in ((0, 1), (2, 3), (0, 2), (1, 3)):
        rows.extend(mul_conj(model[left], model[right]))
    a = mul_conj(model[0], model[3])
    b = mul_conj(model[1], model[2])
    rows.extend((a[0] + b[0], a[0] - b[0], a[1] + b[1], a[1] - b[1]))
    return rows


def add_products(slot_refs, before_ref, out_ref):
    tiles = slot_refs[0].shape[0] // (2 * SUBS)
    for group in range(tiles // SUBS):
        at = pl.ds(group * SUBS, SUBS)
        total = None
        for slot_ref in slot_refs:
            rows = slot_products(slot_ref, group, tiles)
            total = rows if total is None else [x + y for x, y in zip(total, rows)]
        for index, row in enumerate(total):
            if before_ref is not None:
                row = row + before_ref[index, at, :]
            out_ref[index, at, :] = row


def gather_gains(gains, station_refs, seen_ref):
    blocks = gains[0].shape[0]
    tables = [
        [jnp.broadcast_to(gain[h : h + 1], (SUBS, LANES)) for h in range(blocks)]
        for gain in gains
    ]
    for part, station_ref in enumerate(station_refs):
        for group in range(station_ref.shape[0] // SUBS):
            at = pl.ds(group * SUBS, SUBS)
            station = station_ref[at, :]
            offset, block = station & (LANES - 1), station >> 7
            inside = [block == h for h in range(blocks)]
            for j, table in enumerate(tables):
                value = None
                for h in range(blocks):
                    found = jnp.take_along_axis(
                        table[h], offset, axis=1, mode="promise_in_bounds"
                    )
                    value = found if value is None else jnp.where(inside[h], found, value)
                seen_ref[part, j, at, :] = value


def tables_kernel(count, *refs):
    slot_refs, channel_ref = refs[:count], refs[count]
    station_hbms, array_hbms = refs[count + 1 : count + 3], refs[count + 3 : count + 7]
    outs = refs[count + 7 : -5]
    hot_ref, mask_ref, prod_ref, seen_ref, state_ref, own_ref, first_ref, second_ref = outs
    gains_ref, consensus_ref, dual_ref, penalty_ref, sem = refs[-5:]
    station_refs = (first_ref, second_ref)
    copies = copy_in(
        list(
            zip(
                station_hbms + array_hbms,
                station_refs + (gains_ref, consensus_ref, dual_ref, penalty_ref),
            )
        ),
        sem,
    )
    add_products(slot_refs, None, prod_ref)
    for copy in copies:
        copy.wait()
    tiles = first_ref.shape[0]
    blocks = gains_ref.shape[1] // LANES
    for h in range(blocks):
        lanes = pl.ds(h * LANES, LANES)
        penalty = penalty_ref[:, lanes]
        gain = gains_ref[:, lanes]
        target = penalty * (consensus_ref[:, lanes] - dual_ref[:, lanes])
        for j in range(SUBS):
            state_ref[pl.ds(j * SUBS + h, 1), :] = gain[j : j + 1]
            state_ref[pl.ds((SUBS + j) * SUBS + h, 1), :] = target[j : j + 1]
        state_ref[pl.ds(2 * SUBS * SUBS + h, 1), :] = penalty
    gains = [state_ref[pl.ds(j * SUBS, blocks), :] for j in range(SUBS)]
    gather_gains(gains, station_refs, seen_ref)
    place = lax.axis_index("tm")
    own_ref[:SUBS, :] = dual_ref[:, pl.ds(pl.multiple_of(place * LANES, LANES), LANES)]
    own_ref[SUBS:, :] = jnp.full((SUBS, LANES), channel_ref[0].astype(F32))
    row = lax.broadcasted_iota(jnp.int32, (LANES, LANES), 0)
    lower = lax.broadcasted_iota(jnp.int32, (PACK, LANES), 0) >= SUBS
    for part, station_ref in enumerate(station_refs):
        for tile in range(tiles):
            station = station_ref[pl.ds(tile, 1), :]
            offset, block = station & (LANES - 1), station >> 7
            lanes = pl.ds((part * tiles + tile) * LANES, LANES)
            hot_ref[:, lanes] = jnp.where(row == offset, 1.0, 0.0).astype(BF16)
            wide = jnp.broadcast_to(block, (PACK, LANES))
            for h in range(blocks):
                mask_ref[pl.ds(h * PACK, PACK), lanes] = jnp.where(wide == h, 1.0, 0.0).astype(
                    BF16
                )
            for pair in range(blocks // 2):
                mine = jnp.where(lower, 2 * pair + 1, 2 * pair)
                mask_ref[pl.ds((blocks + pair) * PACK, PACK), lanes] = jnp.where(
                    wide == mine, 1.0, 0.0
                ).astype(BF16)


def more_kernel(slot_ref, before_ref, out_ref):
    add_products([slot_ref], before_ref, out_ref)


def gram(gain):
    entry = [(gain[2 * e], gain[2 * e + 1]) for e in range(4)]
    h00 = sum(part * part for part in entry[0] + entry[2])
    h11 = sum(part * part for part in entry[1] + entry[3])
    top = mul_conj(entry[1], entry[0])
    low = mul_conj(entry[3], entry[2])
    return h00, h11, top[0] + low[0], top[1] + low[1]


def baseline_terms(prod, gain_second, gain_first):
    def num(gain, swap):
        out = []
        for i in range(2):
            for l in range(2):
                real = imag = None
                for j in range(2):
                    for k in range(2):
                        if swap:
                            index = 4 * (2 * j + i) + 2 * k + l
                        else:
                            index = 4 * (2 * i + j) + 2 * l + k
                        tr, ti = prod(2 * index), prod(2 * index + 1)
                        gr, gi = gain[2 * (2 * j + k)], gain[2 * (2 * j + k) + 1]
                        if swap:
                            addr, addi = tr * gr + ti * gi, tr * gi - ti * gr
                        else:
                            addr, addi = tr * gr - ti * gi, tr * gi + ti * gr
                        real = addr if real is None else real + addr
                        imag = addi if imag is None else imag + addi
                out.extend((real, imag))
        return out

    n00, n01, n10, n11, pr, pi, qr, qi, rr, ri, sr, si, apr, amr, api, ami = (
        prod(32 + index) for index in range(16)
    )
    h00, h11, hr, hi = gram(gain_second)
    den_first = [
        n00 * h00 + n01 * h11 + 2.0 * (pr * hr - pi * hi),
        n10 * h00 + n11 * h11 + 2.0 * (qr * hr - qi * hi),
        rr * h00 + sr * h11 + apr * hr - ami * hi,
        ri * h00 + si * h11 + api * hr + amr * hi,
    ]
    h00, h11, hr, hi = gram(gain_first)
    den_second = [
        n00 * h00 + n10 * h11 + 2.0 * (rr * hr + ri * hi),
        n01 * h00 + n11 * h11 + 2.0 * (sr * hr + si * hi),
        pr * h00 + qr * h11 + apr * hr + api * hi,
        amr * hi - pi * h00 - qi * h11 - ami * hr,
    ]
    return num(gain_second, False) + den_first, num(gain_first, True) + den_second


def store_terms(prod_ref, seen_ref, term_ref):
    for group in range(prod_ref.shape[1] // SUBS):
        at = pl.ds(group * SUBS, SUBS)
        start = group * SUBS * TERMS
        gain_first, gain_second = (
            [seen_ref[part, j, at, :] for j in range(SUBS)] for part in range(2)
        )
        both = baseline_terms(lambda index: prod_ref[index, at, :], gain_second, gain_first)
        for part, rows in enumerate(both):
            for j, row in enumerate(rows):
                where, apart = (start + j, 8) if j < 8 else (start + 8 + j, 4)
                high = row.astype(BF16).astype(F32)
                term_ref[part, pl.ds(where, SUBS, stride=TERMS), :] = high
                term_ref[part, pl.ds(where + apart, SUBS, stride=TERMS), :] = row - high


def scatter_terms(term_ref, hot_ref, mask_ref, chunk):
    rows = mask_ref.shape[0]
    tiles = term_ref.shape[1] // TERMS
    blocks = rows * 2 // (3 * PACK)
    total = None
    for part in range(2):
        for start in range(0, tiles, chunk):
            columns = []
            for tile in range(start, start + chunk):
                lanes = pl.ds((part * tiles + tile) * LANES, LANES)
                num = term_ref[part, pl.ds(tile * TERMS, PACK), :].astype(BF16)
                den = term_ref[part, pl.ds(tile * TERMS + PACK, SUBS), :]
                den = jnp.concatenate([den, den], axis=0).astype(BF16)
                column = [
                    mask_ref[pl.ds(h * PACK, PACK), lanes] * (num if h < blocks else den)
                    for h in range(rows // PACK)
                ]
                columns.append(jnp.concatenate(column, axis=0))
            lanes = pl.ds((part * tiles + start) * LANES, chunk * LANES)
            add = lax.dot_general(
                jnp.concatenate(columns, axis=1),
                hot_ref[:, lanes],
                (((1,), (1,)), ((), ())),
                preferred_element_type=F32,
            )
            total = add if total is None else total + add
    return total


def solve(num, den, gain, target, penalty):
    rhs = [tuple(num[2 * e + part] + target[2 * e + part] for part in range(2)) for e in range(4)]
    r00, r11, r01 = den[0] + penalty, den[1] + penalty, (den[2], den[3])
    scale = 0.5 / (r00 * r11 - (r01[0] * r01[0] + r01[1] * r01[1]))
    out = []
    for i in range(2):
        a, b = rhs[2 * i], rhs[2 * i + 1]
        cross = mul_conj(b, r01)
        out.extend((a[part] * r11 - cross[part]) * scale for part in range(2))
        out.append((b[0] * r00 - (a[0] * r01[0] - a[1] * r01[1])) * scale)
        out.append((b[1] * r00 - (a[0] * r01[1] + a[1] * r01[0])) * scale)
    return [value + 0.5 * old for value, old in zip(out, gain)]


def sweeps_kernel(*refs):
    hot_ref, mask_ref, before_ref, found_ref, state_ref, own_ref, first_ref, second_ref = refs[:8]
    slot_refs = refs[8:-6]
    gain_out_ref, send_ref, prod_ref, seen_ref, term_ref, total_ref = refs[-6:]
    blocks = mask_ref.shape[0] * 2 // (3 * PACK)
    add_products(slot_refs, before_ref, prod_ref)
    gains = [state_ref[pl.ds(j * SUBS, blocks), :] for j in range(SUBS)]
    target = [state_ref[pl.ds((SUBS + j) * SUBS, blocks), :] for j in range(SUBS)]
    penalty = state_ref[pl.ds(2 * SUBS * SUBS, blocks), :]
    for sweep in range(SWEEPS):
        if sweep:
            gather_gains(gains, (first_ref, second_ref), seen_ref)
        store_terms(prod_ref, found_ref if sweep == 0 else seen_ref, term_ref)
        total_ref[...] = scatter_terms(term_ref, hot_ref, mask_ref, 4)

        def rows(start, stride):
            return total_ref[pl.ds(start, blocks, stride=stride), :]

        num = [rows(j, PACK) + rows(SUBS + j, PACK) for j in range(SUBS)]
        den = [
            rows(blocks * PACK + j, SUBS) + rows(blocks * PACK + 4 + j, SUBS) for j in range(4)
        ]
        gains = solve(num, den, gains, target, penalty)
    for j in range(SUBS):
        total_ref[pl.ds(j, blocks, stride=SUBS), :] = gains[j]
    place = lax.axis_index("tm")
    part = total_ref[pl.ds(pl.multiple_of(place * SUBS, SUBS), SUBS), :]
    gain_out_ref[...] = part
    combined, mark = part + own_ref[:SUBS, :], own_ref[SUBS:, :]
    for channel in range(send_ref.shape[0]):
        send_ref[channel, :SUBS, :] = combined
        send_ref[channel, SUBS:, :] = mark


def legendre(position):
    square = position * position
    return [None, position, 1.5 * square - 0.5, (2.5 * square - 1.5) * position]


def fit_kernel(
    gram_factor, parts_ref, send_ref, consensus_hbm, dual_hbm, consensus_ref, dual_ref, sem
):
    channels = parts_ref.shape[0]
    scale = float(channels) - 1.0

    def basis(channel):
        return legendre(2.0 * channel / scale - 1.0)

    moments = [None] * 4
    for channel in range(channels):
        value = parts_ref[channel, :SUBS, :]
        for k, weight in enumerate(basis(parts_ref[channel, SUBS:, :])):
            add = value if weight is None else weight * value
            moments[k] = add if moments[k] is None else moments[k] + add
    middle = []
    for k in range(4):
        rest = moments[k]
        for earlier in range(k):
            rest = rest - gram_factor[k][earlier] * middle[earlier]
        middle.append(rest * (1.0 / gram_factor[k][k]))
    coeffs = [None] * 4
    for k in reversed(range(4)):
        rest = middle[k]
        for later in range(k + 1, 4):
            rest = rest - gram_factor[later][k] * coeffs[later]
        coeffs[k] = rest * (1.0 / gram_factor[k][k])
    own = basis(send_ref[0, SUBS:, :])
    fitted = coeffs[0]
    for k in range(1, 4):
        fitted = fitted + own[k] * coeffs[k]
    consensus_ref[...] = fitted
    dual_ref[...] = send_ref[0, :SUBS, :] - fitted
    for copy in copy_in([(consensus_ref, consensus_hbm), (dual_ref, dual_hbm)], sem):
        copy.wait()


def gram_cholesky(channels):
    x = 2.0 * np.arange(channels, dtype=np.float64) / (channels - 1.0) - 1.0
    basis = np.stack([np.ones_like(x), x, 1.5 * x * x - 0.5, (2.5 * x * x - 1.5) * x], -1)
    factor = np.linalg.cholesky(basis.T @ basis)
    return [[float(value) for value in row] for row in factor]


SPACES = {"s": pltpu.SMEM, "v": pltpu.VMEM, "h": pltpu.HBM}


def call(kernel, shapes, spaces, scratch=(), limit=8, micros=0):
    cost = pl.CostEstimate(
        flops=int(micros * 1.0e9), transcendentals=0, bytes_accessed=int(micros * 3.0e6)
    )
    run = pl.pallas_call(
        kernel,
        out_shape=shapes,
        in_specs=[pl.BlockSpec(memory_space=SPACES[space]) for space in spaces],
        out_specs=[pl.BlockSpec(memory_space=shape.memory_space) for shape in shapes],
        scratch_shapes=list(scratch),
        compiler_params=pltpu.CompilerParams(vmem_limit_bytes=limit << 20),
        cost_estimate=cost if micros else None,
    )

    def placed(*args):
        return run(
            *(
                arg if space == "s" else pltpu.with_memory_space_constraint(arg, SPACES[space])
                for arg, space in zip(args, spaces, strict=True)
            )
        )

    return placed


def shards(
    visibility,
    model_visibility,
    keep_mask,
    gains_in,
    consensus_in,
    dual_in,
    penalty,
    channel_index,
    first_station,
    second_station,
):
    baselines = visibility.shape[3]
    stations = gains_in.shape[2]
    slots = lax.axis_size("tm")
    channels = lax.axis_size("freq")
    tiles = baselines // LANES
    blocks = stations // LANES
    assert blocks == slots and blocks % 2 == 0 and channel_index.shape == (1,)
    vmem = pltpu.VMEM

    def swap(array, step):
        return lax.ppermute(array, "tm", [(i, i ^ step) for i in range(slots)])

    (own,) = call(
        widen_kernel,
        [vmem((2 * tiles * SUBS, LANES), F32)],
        "hhh",
        [
            vmem((SUBS, baselines), BF16),
            vmem((SUBS, baselines), BF16),
            vmem((1, baselines), jnp.int32),
            pltpu.SemaphoreType.DMA((3,)),
        ],
    )(
        visibility.reshape(SUBS, baselines),
        model_visibility.reshape(SUBS, baselines),
        keep_mask.reshape(1, baselines),
    )
    far = []
    step = slots // 2
    while step > 1:
        far += [swap(array, step) for array in [own, *far]]
        step //= 2
    near = [own, swap(own, 1)]
    gains, consensus, dual = (
        array.reshape(SUBS, stations) for array in (gains_in, consensus_in, dual_in)
    )
    products = vmem((PRODS, tiles, LANES), F32)
    seen = vmem((2, SUBS, tiles, LANES), F32)
    station = vmem((tiles, LANES), jnp.int32)
    wide = vmem((SUBS, stations), F32)
    tables = call(
        lambda *refs: tables_kernel(len(near), *refs),
        [
            vmem((LANES, 2 * baselines), BF16),
            vmem((blocks * 3 * PACK // 2, 2 * baselines), BF16),
            products,
            seen,
            vmem(((2 * SUBS + 1) * SUBS, LANES), F32),
            vmem((2 * SUBS, LANES), F32),
            station,
            station,
        ],
        "v" * len(near) + "shhhhhh",
        [wide, wide, wide, vmem((1, stations), F32), pltpu.SemaphoreType.DMA((6,))],
        limit=16,
        micros=4,
    )(
        *near,
        channel_index,
        first_station.reshape(tiles, LANES),
        second_station.reshape(tiles, LANES),
        gains,
        consensus,
        dual,
        penalty.reshape(1, stations),
    )
    hot, mask, summed, found, state, own, first, second = tables
    far, state = lax.optimization_barrier((far, state))
    last = [swap(array, 1) for array in far]
    for array in far:
        (summed,) = call(more_kernel, [products], "vv", micros=1)(array, summed)
    gain_part, send = call(
        sweeps_kernel,
        [vmem((SUBS, LANES), F32), vmem((channels, 2 * SUBS, LANES), F32)],
        "v" * (8 + len(last)),
        [
            products,
            seen,
            vmem((2, tiles * TERMS, LANES), F32),
            vmem((blocks * 3 * PACK // 2, LANES), F32),
        ],
        limit=16,
    )(hot, mask, summed, found, state, own, first, second, *last)
    parts = lax.all_to_all(send, "freq", 0, 0)
    factor = gram_cholesky(channels)
    out = vmem((SUBS, LANES), F32)
    consensus_out, dual_out = call(
        lambda *refs: fit_kernel(factor, *refs),
        [pltpu.HBM(out.shape, F32)] * 2,
        "vv",
        [out, out, pltpu.SemaphoreType.DMA((2,))],
    )(parts, send)
    return tuple(array[None] for array in (gain_part, consensus_out, dual_out))


def solution(mesh):
    placed = (
        P("freq", "tm", None, None),
        P("freq", "tm", None, None),
        P("freq", "tm", None),
        P("freq", None, None),
        P("freq", None, None),
        P("freq", None, None),
        P(),
        P("freq"),
        P(),
        P(),
    )
    return jax.shard_map(
        shards,
        mesh=mesh,
        in_specs=placed,
        out_specs=(P("freq", None, "tm"), P("freq", None, "tm"), P("freq", None, "tm")),
        check_vma=False,
    )
```

```python
import jax
import jax.numpy as jnp
import numpy as np
from jax import lax
from jax.experimental import pallas as pl
from jax.experimental.pallas import tpu as pltpu
from jax.sharding import PartitionSpec as P

SWEEPS = 2
LANES = 128
SUBS = 8
PRODS = 48
TERMS = 24
PACK = 16
F32 = jnp.float32
BF16 = jnp.bfloat16


def mul_conj(a, b):
    return (a[0] * b[0] + a[1] * b[1], a[1] * b[0] - a[0] * b[1])


def copy_in(pairs, sem):
    copies = [
        pltpu.make_async_copy(source, target, sem.at[index])
        for index, (source, target) in enumerate(pairs)
    ]
    for copy in copies:
        copy.start()
    return copies


def widen_kernel(vis_hbm, model_hbm, keep_hbm, out_ref, vis_ref, model_ref, keep_ref, sem):
    copies = copy_in(
        [(vis_hbm, vis_ref), (keep_hbm, keep_ref), (model_hbm, model_ref)], sem
    )
    tiles = vis_ref.shape[1] // LANES
    copies[0].wait()
    for tile in range(tiles):
        lanes = pl.ds(tile * LANES, LANES)
        out_ref[pl.ds(tile * SUBS, SUBS), :] = vis_ref[:, lanes].astype(F32)
    copies[1].wait()
    copies[2].wait()
    for tile in range(tiles):
        lanes = pl.ds(tile * LANES, LANES)
        out_ref[pl.ds((tiles + tile) * SUBS, SUBS), :] = model_ref[:, lanes].astype(
            F32
        ) * keep_ref[:, lanes].astype(F32)


def slot_products(slot_ref, group, tiles):
    def load(part, component):
        start = (part * tiles + group * SUBS) * SUBS + component
        return slot_ref[pl.ds(start, SUBS, stride=SUBS), :]

    seen = [(load(0, 2 * e), load(0, 2 * e + 1)) for e in range(4)]
    model = [(load(1, 2 * e), load(1, 2 * e + 1)) for e in range(4)]
    rows = []
    for v in range(4):
        for m in range(4):
            rows.extend(mul_conj(seen[v], model[m]))
    rows.extend(entry[0] * entry[0] + entry[1] * entry[1] for entry in model)
    for left, right in ((0, 1), (2, 3), (0, 2), (1, 3)):
        rows.extend(mul_conj(model[left], model[right]))
    a = mul_conj(model[0], model[3])
    b = mul_conj(model[1], model[2])
    rows.extend((a[0] + b[0], a[0] - b[0], a[1] + b[1], a[1] - b[1]))
    return rows


def add_products(slot_refs, before_ref, out_ref, group):
    tiles = slot_refs[0].shape[0] // (2 * SUBS)
    at = pl.ds(group * SUBS, SUBS)
    total = None
    for slot_ref in slot_refs:
        rows = slot_products(slot_ref, group, tiles)
        total = rows if total is None else [x + y for x, y in zip(total, rows)]
    for index, row in enumerate(total):
        if before_ref is not None:
            row = row + before_ref[index, at, :]
            total[index] = row
        out_ref[index, at, :] = row
    return total


def gain_tables(gains):
    return [
        [jnp.broadcast_to(gain[h : h + 1], (SUBS, LANES)) for h in range(gain.shape[0])]
        for gain in gains
    ]


def gather_gains(tables, station_ref, group):
    station = station_ref[pl.ds(group * SUBS, SUBS), :]
    offset, block = station & (LANES - 1), station >> 7
    values = []
    for table in tables:
        value = None
        for h, row in enumerate(table):
            found = jnp.take_along_axis(row, offset, axis=1, mode="promise_in_bounds")
            value = found if value is None else jnp.where(block == h, found, value)
        values.append(value)
    return values


def tables_kernel(count, *refs):
    slot_refs, channel_ref = refs[:count], refs[count]
    station_hbms, array_hbms = refs[count + 1 : count + 3], refs[count + 3 : count + 7]
    outs = refs[count + 7 : -5]
    hot_ref, mask_ref, prod_ref, seen_ref, state_ref, own_ref, first_ref, second_ref = outs
    gains_ref, consensus_ref, dual_ref, penalty_ref, sem = refs[-5:]
    station_refs = (first_ref, second_ref)
    copies = copy_in(
        list(
            zip(
                station_hbms + array_hbms,
                station_refs + (gains_ref, consensus_ref, dual_ref, penalty_ref),
            )
        ),
        sem,
    )
    tiles = first_ref.shape[0]
    for group in range(tiles // SUBS):
        add_products(slot_refs, None, prod_ref, group)
    for copy in copies:
        copy.wait()
    blocks = gains_ref.shape[1] // LANES
    for h in range(blocks):
        lanes = pl.ds(h * LANES, LANES)
        penalty = penalty_ref[:, lanes]
        gain = gains_ref[:, lanes]
        target = penalty * (consensus_ref[:, lanes] - dual_ref[:, lanes])
        for j in range(SUBS):
            state_ref[pl.ds(j * SUBS + h, 1), :] = gain[j : j + 1]
            state_ref[pl.ds((SUBS + j) * SUBS + h, 1), :] = target[j : j + 1]
        state_ref[pl.ds(2 * SUBS * SUBS + h, 1), :] = penalty
    gains = [state_ref[pl.ds(j * SUBS, blocks), :] for j in range(SUBS)]
    tables = gain_tables(gains)
    for part, station_ref in enumerate(station_refs):
        for group in range(tiles // SUBS):
            for j, value in enumerate(gather_gains(tables, station_ref, group)):
                seen_ref[part, j, pl.ds(group * SUBS, SUBS), :] = value
    place = lax.axis_index("tm")
    own_ref[:SUBS, :] = dual_ref[:, pl.ds(pl.multiple_of(place * LANES, LANES), LANES)]
    own_ref[SUBS:, :] = jnp.full((SUBS, LANES), channel_ref[0].astype(F32))
    row = lax.broadcasted_iota(jnp.int32, (LANES, LANES), 0)
    lower = lax.broadcasted_iota(jnp.int32, (PACK, LANES), 0) >= SUBS
    for part, station_ref in enumerate(station_refs):
        for tile in range(tiles):
            station = station_ref[pl.ds(tile, 1), :]
            offset, block = station & (LANES - 1), station >> 7
            lanes = pl.ds((part * tiles + tile) * LANES, LANES)
            hot_ref[lanes, :] = jnp.where(row == offset, 1.0, 0.0).T.astype(BF16)
            wide = jnp.broadcast_to(block, (PACK, LANES))
            for h in range(blocks):
                mask_ref[pl.ds(h * PACK, PACK), lanes] = jnp.where(wide == h, 1.0, 0.0).astype(
                    BF16
                )
            for pair in range(blocks // 2):
                mine = jnp.where(lower, 2 * pair + 1, 2 * pair)
                mask_ref[pl.ds((blocks + pair) * PACK, PACK), lanes] = jnp.where(
                    wide == mine, 1.0, 0.0
                ).astype(BF16)


def more_kernel(slot_ref, before_ref, out_ref):
    for group in range(out_ref.shape[1] // SUBS):
        add_products([slot_ref], before_ref, out_ref, group)


def gram(gain):
    entry = [(gain[2 * e], gain[2 * e + 1]) for e in range(4)]
    h00 = sum(part * part for part in entry[0] + entry[2])
    h11 = sum(part * part for part in entry[1] + entry[3])
    top = mul_conj(entry[1], entry[0])
    low = mul_conj(entry[3], entry[2])
    return h00, h11, top[0] + low[0], top[1] + low[1]


def baseline_terms(prod, gain_second, gain_first):
    def num(gain, swap):
        out = []
        for i in range(2):
            for l in range(2):
                real = imag = None
                for j in range(2):
                    for k in range(2):
                        if swap:
                            index = 4 * (2 * j + i) + 2 * k + l
                        else:
                            index = 4 * (2 * i + j) + 2 * l + k
                        tr, ti = prod(2 * index), prod(2 * index + 1)
                        gr, gi = gain[2 * (2 * j + k)], gain[2 * (2 * j + k) + 1]
                        if swap:
                            addr, addi = tr * gr + ti * gi, tr * gi - ti * gr
                        else:
                            addr, addi = tr * gr - ti * gi, tr * gi + ti * gr
                        real = addr if real is None else real + addr
                        imag = addi if imag is None else imag + addi
                out.extend((real, imag))
        return out

    n00, n01, n10, n11, pr, pi, qr, qi, rr, ri, sr, si, apr, amr, api, ami = (
        prod(32 + index) for index in range(16)
    )
    h00, h11, hr, hi = gram(gain_second)
    den_first = [
        n00 * h00 + n01 * h11 + 2.0 * (pr * hr - pi * hi),
        n10 * h00 + n11 * h11 + 2.0 * (qr * hr - qi * hi),
        rr * h00 + sr * h11 + apr * hr - ami * hi,
        ri * h00 + si * h11 + api * hr + amr * hi,
    ]
    h00, h11, hr, hi = gram(gain_first)
    den_second = [
        n00 * h00 + n10 * h11 + 2.0 * (rr * hr + ri * hi),
        n01 * h00 + n11 * h11 + 2.0 * (sr * hr + si * hi),
        pr * h00 + qr * h11 + apr * hr + api * hi,
        amr * hi - pi * h00 - qi * h11 - ami * hr,
    ]
    return num(gain_second, False) + den_first, num(gain_first, True) + den_second


def store_terms(prod, gain_first, gain_second, group, term_ref):
    start = group * SUBS * TERMS
    for part, rows in enumerate(baseline_terms(prod, gain_second, gain_first)):
        for j, row in enumerate(rows):
            where, apart = (start + j, 8) if j < 8 else (start + 8 + j, 4)
            high = row.astype(BF16).astype(F32)
            term_ref[part, pl.ds(where, SUBS, stride=TERMS), :] = high
            term_ref[part, pl.ds(where + apart, SUBS, stride=TERMS), :] = row - high


def scatter_terms(term_ref, hot_ref, mask_ref, group, part):
    rows = mask_ref.shape[0]
    tiles = term_ref.shape[1] // TERMS
    blocks = rows * 2 // (3 * PACK)
    columns = []
    for tile in range(group * SUBS, (group + 1) * SUBS):
        lanes = pl.ds((part * tiles + tile) * LANES, LANES)
        num = term_ref[part, pl.ds(tile * TERMS, PACK), :].astype(BF16)
        den = term_ref[part, pl.ds(tile * TERMS + PACK, SUBS), :]
        den = jnp.concatenate([den, den], axis=0).astype(BF16)
        column = [
            mask_ref[pl.ds(h * PACK, PACK), lanes] * (num if h < blocks else den)
            for h in range(rows // PACK)
        ]
        columns.append(jnp.concatenate(column, axis=0))
    at = pl.ds((part * tiles + group * SUBS) * LANES, SUBS * LANES)
    return jnp.dot(
        jnp.concatenate(columns, axis=1), hot_ref[at, :], preferred_element_type=F32
    )


def solve(num, den, gain, target, penalty):
    rhs = [tuple(num[2 * e + part] + target[2 * e + part] for part in range(2)) for e in range(4)]
    r00, r11, r01 = den[0] + penalty, den[1] + penalty, (den[2], den[3])
    scale = 0.5 / (r00 * r11 - (r01[0] * r01[0] + r01[1] * r01[1]))
    out = []
    for i in range(2):
        a, b = rhs[2 * i], rhs[2 * i + 1]
        cross = mul_conj(b, r01)
        out.extend((a[part] * r11 - cross[part]) * scale for part in range(2))
        out.append((b[0] * r00 - (a[0] * r01[0] - a[1] * r01[1])) * scale)
        out.append((b[1] * r00 - (a[0] * r01[1] + a[1] * r01[0])) * scale)
    return [value + 0.5 * old for value, old in zip(out, gain)]


def own_place():
    return lax.axis_index("tm")


def sweeps_kernel(*refs):
    hot_ref, mask_ref, before_ref, found_ref, state_ref, own_ref, first_ref, second_ref = refs[:8]
    slot_refs = refs[8:-5]
    gain_out_ref, send_ref, prod_ref, term_ref, total_ref = refs[-5:]
    blocks = mask_ref.shape[0] * 2 // (3 * PACK)
    groups = first_ref.shape[0] // SUBS
    gains = [state_ref[pl.ds(j * SUBS, blocks), :] for j in range(SUBS)]
    target = [state_ref[pl.ds((SUBS + j) * SUBS, blocks), :] for j in range(SUBS)]
    penalty = state_ref[pl.ds(2 * SUBS * SUBS, blocks), :]
    for sweep in range(SWEEPS):
        tables = gain_tables(gains) if sweep else None
        total = None
        for group in range(groups):
            at = pl.ds(group * SUBS, SUBS)
            if sweep:
                gain_first, gain_second = (
                    gather_gains(tables, ref, group) for ref in (first_ref, second_ref)
                )
            else:
                add_products(slot_refs, before_ref, prod_ref, group)
                gain_first, gain_second = (
                    [found_ref[part, j, at, :] for j in range(SUBS)] for part in range(2)
                )
            store_terms(
                lambda index: prod_ref[index, at, :], gain_first, gain_second, group, term_ref
            )
            for part in range(2):
                add = scatter_terms(term_ref, hot_ref, mask_ref, group, part)
                total = add if total is None else total + add
        total_ref[...] = total

        def rows(start, stride):
            return total_ref[pl.ds(start, blocks, stride=stride), :]

        num = [rows(j, PACK) + rows(SUBS + j, PACK) for j in range(SUBS)]
        den = [
            rows(blocks * PACK + j, SUBS) + rows(blocks * PACK + 4 + j, SUBS) for j in range(4)
        ]
        gains = solve(num, den, gains, target, penalty)
    for j in range(SUBS):
        total_ref[pl.ds(j, blocks, stride=SUBS), :] = gains[j]
    place = own_place()
    part = total_ref[pl.ds(pl.multiple_of(place * SUBS, SUBS), SUBS), :]
    gain_out_ref[...] = part
    combined, mark = part + own_ref[:SUBS, :], own_ref[SUBS:, :]
    for channel in range(send_ref.shape[0]):
        send_ref[channel, :SUBS, :] = combined
        send_ref[channel, SUBS:, :] = mark


def legendre(position):
    square = position * position
    return [None, position, 1.5 * square - 0.5, (2.5 * square - 1.5) * position]


def fit(gram_factor, parts, send):
    scale = float(parts.shape[0]) - 1.0

    def basis(channel):
        return legendre(2.0 * channel / scale - 1.0)

    value = parts[:, :SUBS]
    moments = [
        jnp.sum(value if weight is None else weight * value, axis=0)
        for weight in basis(parts[:, SUBS:])
    ]
    middle = []
    for k in range(4):
        rest = moments[k]
        for earlier in range(k):
            rest = rest - gram_factor[k][earlier] * middle[earlier]
        middle.append(rest * (1.0 / gram_factor[k][k]))
    coeffs = [None] * 4
    for k in reversed(range(4)):
        rest = middle[k]
        for later in range(k + 1, 4):
            rest = rest - gram_factor[later][k] * coeffs[later]
        coeffs[k] = rest * (1.0 / gram_factor[k][k])
    own = basis(send[0, SUBS:])
    fitted = coeffs[0]
    for k in range(1, 4):
        fitted = fitted + own[k] * coeffs[k]
    return fitted, send[0, :SUBS] - fitted


def gram_cholesky(channels):
    x = 2.0 * np.arange(channels, dtype=np.float64) / (channels - 1.0) - 1.0
    basis = np.stack([np.ones_like(x), x, 1.5 * x * x - 0.5, (2.5 * x * x - 1.5) * x], -1)
    factor = np.linalg.cholesky(basis.T @ basis)
    return [[float(value) for value in row] for row in factor]


SPACES = {"s": pltpu.SMEM, "v": pltpu.VMEM, "h": pltpu.HBM}


def call(kernel, shapes, spaces, scratch=(), limit=8, micros=0):
    cost = pl.CostEstimate(
        flops=int(micros * 1.0e9), transcendentals=0, bytes_accessed=int(micros * 3.0e6)
    )
    run = pl.pallas_call(
        kernel,
        out_shape=shapes,
        in_specs=[pl.BlockSpec(memory_space=SPACES[space]) for space in spaces],
        out_specs=[pl.BlockSpec(memory_space=shape.memory_space) for shape in shapes],
        scratch_shapes=list(scratch),
        compiler_params=pltpu.CompilerParams(vmem_limit_bytes=limit << 20),
        cost_estimate=cost if micros else None,
    )

    def placed(*args):
        return run(
            *(
                arg if space == "s" else pltpu.with_memory_space_constraint(arg, SPACES[space])
                for arg, space in zip(args, spaces, strict=True)
            )
        )

    return placed


def shards(
    visibility,
    model_visibility,
    keep_mask,
    gains_in,
    consensus_in,
    dual_in,
    penalty,
    channel_index,
    first_station,
    second_station,
):
    baselines = visibility.shape[3]
    stations = gains_in.shape[2]
    slots = lax.axis_size("tm")
    channels = lax.axis_size("freq")
    tiles = baselines // LANES
    blocks = stations // LANES
    assert blocks == slots and blocks % 2 == 0 and channel_index.shape == (1,)
    vmem = pltpu.VMEM

    def swap(array, step):
        return lax.ppermute(array, "tm", [(i, i ^ step) for i in range(slots)])

    (own,) = call(
        widen_kernel,
        [vmem((2 * tiles * SUBS, LANES), F32)],
        "hhh",
        [
            vmem((SUBS, baselines), BF16),
            vmem((SUBS, baselines), BF16),
            vmem((1, baselines), jnp.int32),
            pltpu.SemaphoreType.DMA((3,)),
        ],
    )(
        visibility.reshape(SUBS, baselines),
        model_visibility.reshape(SUBS, baselines),
        keep_mask.reshape(1, baselines),
    )
    far = []
    step = slots // 2
    while step > 1:
        far += [swap(array, step) for array in [own, *far]]
        step //= 2
    near = [own, swap(own, 1)]
    gains, consensus, dual = (
        array.reshape(SUBS, stations) for array in (gains_in, consensus_in, dual_in)
    )
    products = vmem((PRODS, tiles, LANES), F32)
    seen = vmem((2, SUBS, tiles, LANES), F32)
    station = vmem((tiles, LANES), jnp.int32)
    wide = vmem((SUBS, stations), F32)
    tables = call(
        lambda *refs: tables_kernel(len(near), *refs),
        [
            vmem((2 * baselines, LANES), BF16),
            vmem((blocks * 3 * PACK // 2, 2 * baselines), BF16),
            products,
            seen,
            vmem(((2 * SUBS + 1) * SUBS, LANES), F32),
            vmem((2 * SUBS, LANES), F32),
            station,
            station,
        ],
        "v" * len(near) + "shhhhhh",
        [wide, wide, wide, vmem((1, stations), F32), pltpu.SemaphoreType.DMA((6,))],
        limit=16,
        micros=4,
    )(
        *near,
        channel_index,
        first_station.reshape(tiles, LANES),
        second_station.reshape(tiles, LANES),
        gains,
        consensus,
        dual,
        penalty.reshape(1, stations),
    )
    hot, mask, summed, found, state, own, first, second = tables
    far, state = lax.optimization_barrier((far, state))
    last = [swap(array, 1) for array in far]
    for array in far:
        (summed,) = call(more_kernel, [products], "vv", micros=1)(array, summed)
    gain_part, send = call(
        sweeps_kernel,
        [vmem((SUBS, LANES), F32), vmem((channels, 2 * SUBS, LANES), F32)],
        "v" * (8 + len(last)),
        [
            products,
            vmem((2, tiles * TERMS, LANES), F32),
            vmem((blocks * 3 * PACK // 2, LANES), F32),
        ],
        limit=16,
    )(hot, mask, summed, found, state, own, first, second, *last)
    parts = lax.all_to_all(send, "freq", 0, 0)
    consensus_out, dual_out = fit(gram_cholesky(channels), parts, send)
    return tuple(array[None] for array in (gain_part, consensus_out, dual_out))


def solution(mesh):
    placed = (
        P("freq", "tm", None, None),
        P("freq", "tm", None, None),
        P("freq", "tm", None),
        P("freq", None, None),
        P("freq", None, None),
        P("freq", None, None),
        P(),
        P("freq"),
        P(),
        P(),
    )
    return jax.shard_map(
        shards,
        mesh=mesh,
        in_specs=placed,
        out_specs=(P("freq", None, "tm"), P("freq", None, "tm"), P("freq", None, "tm")),
        check_vma=False,
    )
```

```python
import jax
import jax.numpy as jnp
import numpy as np
from jax import lax
from jax.experimental import pallas as pl
from jax.experimental.pallas import tpu as pltpu
from jax.sharding import PartitionSpec as P

SWEEPS = 2
LANES = 128
SUBS = 8
PRODS = 48
TERMS = 24
PACK = 16
F32 = jnp.float32
BF16 = jnp.bfloat16


def mul_conj(a, b):
    return (a[0] * b[0] + a[1] * b[1], a[1] * b[0] - a[0] * b[1])


def copy_in(pairs, sem):
    copies = [
        pltpu.make_async_copy(source, target, sem.at[index])
        for index, (source, target) in enumerate(pairs)
    ]
    for copy in copies:
        copy.start()
    return copies


def widen_kernel(vis_hbm, model_hbm, keep_hbm, out_ref, vis_ref, model_ref, keep_ref, sem):
    copies = copy_in(
        [(vis_hbm, vis_ref), (keep_hbm, keep_ref), (model_hbm, model_ref)], sem
    )
    tiles = vis_ref.shape[1] // LANES
    copies[0].wait()
    for tile in range(tiles):
        lanes = pl.ds(tile * LANES, LANES)
        out_ref[pl.ds(tile * SUBS, SUBS), :] = vis_ref[:, lanes].astype(F32)
    copies[1].wait()
    copies[2].wait()
    for tile in range(tiles):
        lanes = pl.ds(tile * LANES, LANES)
        out_ref[pl.ds((tiles + tile) * SUBS, SUBS), :] = model_ref[:, lanes].astype(
            F32
        ) * keep_ref[:, lanes].astype(F32)


def slot_products(slot_ref, group, tiles):
    def load(part, component):
        start = (part * tiles + group * SUBS) * SUBS + component
        return slot_ref[pl.ds(start, SUBS, stride=SUBS), :]

    seen = [(load(0, 2 * e), load(0, 2 * e + 1)) for e in range(4)]
    model = [(load(1, 2 * e), load(1, 2 * e + 1)) for e in range(4)]
    rows = []
    for v in range(4):
        for m in range(4):
            rows.extend(mul_conj(seen[v], model[m]))
    rows.extend(entry[0] * entry[0] + entry[1] * entry[1] for entry in model)
    for left, right in ((0, 1), (2, 3), (0, 2), (1, 3)):
        rows.extend(mul_conj(model[left], model[right]))
    a = mul_conj(model[0], model[3])
    b = mul_conj(model[1], model[2])
    rows.extend((a[0] + b[0], a[0] - b[0], a[1] + b[1], a[1] - b[1]))
    return rows


def add_products(slot_refs, before_ref, out_ref, group):
    tiles = slot_refs[0].shape[0] // (2 * SUBS)
    at = pl.ds(group * SUBS, SUBS)
    total = None
    for slot_ref in slot_refs:
        rows = slot_products(slot_ref, group, tiles)
        total = rows if total is None else [x + y for x, y in zip(total, rows)]
    for index, row in enumerate(total):
        if before_ref is not None:
            row = row + before_ref[index, at, :]
            total[index] = row
        out_ref[index, at, :] = row
    return total


def gain_tables(gains):
    return [
        [jnp.broadcast_to(gain[h : h + 1], (SUBS, LANES)) for h in range(gain.shape[0])]
        for gain in gains
    ]


def gather_gains(tables, station_ref, group):
    station = station_ref[pl.ds(group * SUBS, SUBS), :]
    offset, block = station & (LANES - 1), station >> 7
    values = []
    for table in tables:
        value = None
        for h, row in enumerate(table):
            found = jnp.take_along_axis(row, offset, axis=1, mode="promise_in_bounds")
            value = found if value is None else jnp.where(block == h, found, value)
        values.append(value)
    return values


def tables_kernel(count, *refs):
    slot_refs, channel_ref = refs[:count], refs[count]
    station_hbms, array_hbms = refs[count + 1 : count + 3], refs[count + 3 : count + 7]
    outs = refs[count + 7 : -5]
    hot_ref, mask_ref, prod_ref, seen_ref, state_ref, own_ref, first_ref, second_ref = outs
    gains_ref, consensus_ref, dual_ref, penalty_ref, sem = refs[-5:]
    station_refs = (first_ref, second_ref)
    copies = copy_in(
        list(
            zip(
                station_hbms + array_hbms,
                station_refs + (gains_ref, consensus_ref, dual_ref, penalty_ref),
            )
        ),
        sem,
    )
    tiles = first_ref.shape[0]
    for group in range(tiles // SUBS):
        add_products(slot_refs, None, prod_ref, group)
    for copy in copies:
        copy.wait()
    blocks = gains_ref.shape[1] // LANES
    for h in range(blocks):
        lanes = pl.ds(h * LANES, LANES)
        penalty = penalty_ref[:, lanes]
        gain = gains_ref[:, lanes]
        target = penalty * (consensus_ref[:, lanes] - dual_ref[:, lanes])
        for j in range(SUBS):
            state_ref[pl.ds(j * SUBS + h, 1), :] = gain[j : j + 1]
            state_ref[pl.ds((SUBS + j) * SUBS + h, 1), :] = target[j : j + 1]
        state_ref[pl.ds(2 * SUBS * SUBS + h, 1), :] = penalty
    gains = [state_ref[pl.ds(j * SUBS, blocks), :] for j in range(SUBS)]
    tables = gain_tables(gains)
    for part, station_ref in enumerate(station_refs):
        for group in range(tiles // SUBS):
            for j, value in enumerate(gather_gains(tables, station_ref, group)):
                seen_ref[part, j, pl.ds(group * SUBS, SUBS), :] = value
    place = lax.axis_index("tm")
    own_ref[:SUBS, :] = dual_ref[:, pl.ds(pl.multiple_of(place * LANES, LANES), LANES)]
    own_ref[SUBS:, :] = jnp.full((SUBS, LANES), channel_ref[0].astype(F32))
    row = lax.broadcasted_iota(jnp.int32, (LANES, LANES), 0)
    lower = lax.broadcasted_iota(jnp.int32, (PACK, LANES), 0) >= SUBS
    for part, station_ref in enumerate(station_refs):
        for tile in range(tiles):
            station = station_ref[pl.ds(tile, 1), :]
            offset, block = station & (LANES - 1), station >> 7
            lanes = pl.ds((part * tiles + tile) * LANES, LANES)
            hot_ref[lanes, :] = jnp.where(row == offset, 1.0, 0.0).T.astype(BF16)
            wide = jnp.broadcast_to(block, (PACK, LANES))
            for h in range(blocks):
                mask_ref[pl.ds(h * PACK, PACK), lanes] = jnp.where(wide == h, 1.0, 0.0).astype(
                    BF16
                )
            for pair in range(blocks // 2):
                mine = jnp.where(lower, 2 * pair + 1, 2 * pair)
                mask_ref[pl.ds((blocks + pair) * PACK, PACK), lanes] = jnp.where(
                    wide == mine, 1.0, 0.0
                ).astype(BF16)


def more_kernel(before_ref, *refs):
    for group in range(before_ref.shape[1] // SUBS):
        add_products(refs[:-1], before_ref, refs[-1], group)


def gram(gain):
    entry = [(gain[2 * e], gain[2 * e + 1]) for e in range(4)]
    h00 = sum(part * part for part in entry[0] + entry[2])
    h11 = sum(part * part for part in entry[1] + entry[3])
    top = mul_conj(entry[1], entry[0])
    low = mul_conj(entry[3], entry[2])
    return h00, h11, top[0] + low[0], top[1] + low[1]


def baseline_terms(prod, gain_second, gain_first):
    def num(gain, swap):
        out = []
        for i in range(2):
            for l in range(2):
                real = imag = None
                for j in range(2):
                    for k in range(2):
                        if swap:
                            index = 4 * (2 * j + i) + 2 * k + l
                        else:
                            index = 4 * (2 * i + j) + 2 * l + k
                        tr, ti = prod(2 * index), prod(2 * index + 1)
                        gr, gi = gain[2 * (2 * j + k)], gain[2 * (2 * j + k) + 1]
                        if swap:
                            addr, addi = tr * gr + ti * gi, tr * gi - ti * gr
                        else:
                            addr, addi = tr * gr - ti * gi, tr * gi + ti * gr
                        real = addr if real is None else real + addr
                        imag = addi if imag is None else imag + addi
                out.extend((real, imag))
        return out

    n00, n01, n10, n11, pr, pi, qr, qi, rr, ri, sr, si, apr, amr, api, ami = (
        prod(32 + index) for index in range(16)
    )
    h00, h11, hr, hi = gram(gain_second)
    den_first = [
        n00 * h00 + n01 * h11 + 2.0 * (pr * hr - pi * hi),
        n10 * h00 + n11 * h11 + 2.0 * (qr * hr - qi * hi),
        rr * h00 + sr * h11 + apr * hr - ami * hi,
        ri * h00 + si * h11 + api * hr + amr * hi,
    ]
    h00, h11, hr, hi = gram(gain_first)
    den_second = [
        n00 * h00 + n10 * h11 + 2.0 * (rr * hr + ri * hi),
        n01 * h00 + n11 * h11 + 2.0 * (sr * hr + si * hi),
        pr * h00 + qr * h11 + apr * hr + api * hi,
        amr * hi - pi * h00 - qi * h11 - ami * hr,
    ]
    return num(gain_second, False) + den_first, num(gain_first, True) + den_second


def store_terms(prod, gain_first, gain_second, group, term_ref):
    start = group * SUBS * TERMS
    for part, rows in enumerate(baseline_terms(prod, gain_second, gain_first)):
        for j, row in enumerate(rows):
            where, apart = (start + j, 8) if j < 8 else (start + 8 + j, 4)
            high = row.astype(BF16).astype(F32)
            term_ref[part, pl.ds(where, SUBS, stride=TERMS), :] = high
            term_ref[part, pl.ds(where + apart, SUBS, stride=TERMS), :] = row - high


def scatter_terms(term_ref, hot_ref, mask_ref, group, part):
    rows = mask_ref.shape[0]
    tiles = term_ref.shape[1] // TERMS
    blocks = rows * 2 // (3 * PACK)
    columns = []
    for tile in range(group * SUBS, (group + 1) * SUBS):
        lanes = pl.ds((part * tiles + tile) * LANES, LANES)
        num = term_ref[part, pl.ds(tile * TERMS, PACK), :].astype(BF16)
        den = term_ref[part, pl.ds(tile * TERMS + PACK, SUBS), :]
        den = jnp.concatenate([den, den], axis=0).astype(BF16)
        column = [
            mask_ref[pl.ds(h * PACK, PACK), lanes] * (num if h < blocks else den)
            for h in range(rows // PACK)
        ]
        columns.append(jnp.concatenate(column, axis=0))
    at = pl.ds((part * tiles + group * SUBS) * LANES, SUBS * LANES)
    return jnp.dot(
        jnp.concatenate(columns, axis=1), hot_ref[at, :], preferred_element_type=F32
    )


def solve(num, den, gain, target, penalty):
    rhs = [tuple(num[2 * e + part] + target[2 * e + part] for part in range(2)) for e in range(4)]
    r00, r11, r01 = den[0] + penalty, den[1] + penalty, (den[2], den[3])
    scale = 0.5 / (r00 * r11 - (r01[0] * r01[0] + r01[1] * r01[1]))
    out = []
    for i in range(2):
        a, b = rhs[2 * i], rhs[2 * i + 1]
        cross = mul_conj(b, r01)
        out.extend((a[part] * r11 - cross[part]) * scale for part in range(2))
        out.append((b[0] * r00 - (a[0] * r01[0] - a[1] * r01[1])) * scale)
        out.append((b[1] * r00 - (a[0] * r01[1] + a[1] * r01[0])) * scale)
    return [value + 0.5 * old for value, old in zip(out, gain)]


def own_place():
    return lax.axis_index("tm")


def sweeps_kernel(*refs):
    hot_ref, mask_ref, before_ref, found_ref, state_ref, own_ref, first_ref, second_ref = refs[:8]
    slot_refs = refs[8:-5]
    gain_out_ref, send_ref, prod_ref, term_ref, total_ref = refs[-5:]
    blocks = mask_ref.shape[0] * 2 // (3 * PACK)
    groups = first_ref.shape[0] // SUBS
    gains = [state_ref[pl.ds(j * SUBS, blocks), :] for j in range(SUBS)]
    target = [state_ref[pl.ds((SUBS + j) * SUBS, blocks), :] for j in range(SUBS)]
    penalty = state_ref[pl.ds(2 * SUBS * SUBS, blocks), :]
    for sweep in range(SWEEPS):
        tables = gain_tables(gains) if sweep else None
        total = None
        for group in range(groups):
            at = pl.ds(group * SUBS, SUBS)
            if sweep:
                gain_first, gain_second = (
                    gather_gains(tables, ref, group) for ref in (first_ref, second_ref)
                )
            else:
                add_products(slot_refs, before_ref, prod_ref, group)
                gain_first, gain_second = (
                    [found_ref[part, j, at, :] for j in range(SUBS)] for part in range(2)
                )
            store_terms(
                lambda index: prod_ref[index, at, :], gain_first, gain_second, group, term_ref
            )
            for part in range(2):
                add = scatter_terms(term_ref, hot_ref, mask_ref, group, part)
                total = add if total is None else total + add
        total_ref[...] = total

        def rows(start, stride):
            return total_ref[pl.ds(start, blocks, stride=stride), :]

        num = [rows(j, PACK) + rows(SUBS + j, PACK) for j in range(SUBS)]
        den = [
            rows(blocks * PACK + j, SUBS) + rows(blocks * PACK + 4 + j, SUBS) for j in range(4)
        ]
        gains = solve(num, den, gains, target, penalty)
    for j in range(SUBS):
        total_ref[pl.ds(j, blocks, stride=SUBS), :] = gains[j]
    place = own_place()
    part = total_ref[pl.ds(pl.multiple_of(place * SUBS, SUBS), SUBS), :]
    gain_out_ref[...] = part
    combined, mark = part + own_ref[:SUBS, :], own_ref[SUBS:, :]
    for channel in range(send_ref.shape[0]):
        send_ref[channel, :SUBS, :] = combined
        send_ref[channel, SUBS:, :] = mark


def legendre(position):
    square = position * position
    return [None, position, 1.5 * square - 0.5, (2.5 * square - 1.5) * position]


def fit(gram_factor, parts, send):
    scale = float(parts.shape[0]) - 1.0

    def basis(channel):
        return legendre(2.0 * channel / scale - 1.0)

    value = parts[:, :SUBS]
    moments = [
        jnp.sum(value if weight is None else weight * value, axis=0)
        for weight in basis(parts[:, SUBS:])
    ]
    middle = []
    for k in range(4):
        rest = moments[k]
        for earlier in range(k):
            rest = rest - gram_factor[k][earlier] * middle[earlier]
        middle.append(rest * (1.0 / gram_factor[k][k]))
    coeffs = [None] * 4
    for k in reversed(range(4)):
        rest = middle[k]
        for later in range(k + 1, 4):
            rest = rest - gram_factor[later][k] * coeffs[later]
        coeffs[k] = rest * (1.0 / gram_factor[k][k])
    own = basis(send[0, SUBS:])
    fitted = coeffs[0]
    for k in range(1, 4):
        fitted = fitted + own[k] * coeffs[k]
    return fitted, send[0, :SUBS] - fitted


def gram_cholesky(channels):
    x = 2.0 * np.arange(channels, dtype=np.float64) / (channels - 1.0) - 1.0
    basis = np.stack([np.ones_like(x), x, 1.5 * x * x - 0.5, (2.5 * x * x - 1.5) * x], -1)
    factor = np.linalg.cholesky(basis.T @ basis)
    return [[float(value) for value in row] for row in factor]


SPACES = {"s": pltpu.SMEM, "v": pltpu.VMEM, "h": pltpu.HBM}


def call(kernel, shapes, spaces, scratch=(), limit=8, micros=0):
    cost = pl.CostEstimate(
        flops=int(micros * 1.0e9), transcendentals=0, bytes_accessed=int(micros * 3.0e6)
    )
    run = pl.pallas_call(
        kernel,
        out_shape=shapes,
        in_specs=[pl.BlockSpec(memory_space=SPACES[space]) for space in spaces],
        out_specs=[pl.BlockSpec(memory_space=shape.memory_space) for shape in shapes],
        scratch_shapes=list(scratch),
        compiler_params=pltpu.CompilerParams(vmem_limit_bytes=limit << 20),
        cost_estimate=cost if micros else None,
    )

    def placed(*args):
        return run(
            *(
                arg if space == "s" else pltpu.with_memory_space_constraint(arg, SPACES[space])
                for arg, space in zip(args, spaces, strict=True)
            )
        )

    return placed


def shards(
    visibility,
    model_visibility,
    keep_mask,
    gains_in,
    consensus_in,
    dual_in,
    penalty,
    channel_index,
    first_station,
    second_station,
):
    baselines = visibility.shape[3]
    stations = gains_in.shape[2]
    slots = lax.axis_size("tm")
    channels = lax.axis_size("freq")
    tiles = baselines // LANES
    blocks = stations // LANES
    assert blocks == slots and blocks % 2 == 0 and channel_index.shape == (1,)
    vmem = pltpu.VMEM

    def swap(array, step):
        return lax.ppermute(array, "tm", [(i, i ^ step) for i in range(slots)])

    (own,) = call(
        widen_kernel,
        [vmem((2 * tiles * SUBS, LANES), F32)],
        "hhh",
        [
            vmem((SUBS, baselines), BF16),
            vmem((SUBS, baselines), BF16),
            vmem((1, baselines), jnp.int32),
            pltpu.SemaphoreType.DMA((3,)),
        ],
    )(
        visibility.reshape(SUBS, baselines),
        model_visibility.reshape(SUBS, baselines),
        keep_mask.reshape(1, baselines),
    )
    far = []
    step = slots // 2
    while step > 1:
        far += [swap(array, step) for array in [own, *far]]
        step //= 2
    gains, consensus, dual = (
        array.reshape(SUBS, stations) for array in (gains_in, consensus_in, dual_in)
    )
    products = vmem((PRODS, tiles, LANES), F32)
    seen = vmem((2, SUBS, tiles, LANES), F32)
    station = vmem((tiles, LANES), jnp.int32)
    wide = vmem((SUBS, stations), F32)
    tables = call(
        lambda *refs: tables_kernel(1, *refs),
        [
            vmem((2 * baselines, LANES), BF16),
            vmem((blocks * 3 * PACK // 2, 2 * baselines), BF16),
            products,
            seen,
            vmem(((2 * SUBS + 1) * SUBS, LANES), F32),
            vmem((2 * SUBS, LANES), F32),
            station,
            station,
        ],
        "vshhhhhh",
        [wide, wide, wide, vmem((1, stations), F32), pltpu.SemaphoreType.DMA((6,))],
        limit=16,
        micros=4,
    )(
        own,
        channel_index,
        first_station.reshape(tiles, LANES),
        second_station.reshape(tiles, LANES),
        gains,
        consensus,
        dual,
        penalty.reshape(1, stations),
    )
    hot, mask, summed, found, state, marks, first, second = tables
    own, state = lax.optimization_barrier((own, state))
    near = swap(own, 1)
    far, state = lax.optimization_barrier((far, state))
    last = [swap(array, 1) for array in far]
    (summed,) = call(more_kernel, [products], "v" * (2 + len(far)), micros=1)(
        summed, near, *far
    )
    gain_part, send = call(
        sweeps_kernel,
        [vmem((SUBS, LANES), F32), vmem((channels, 2 * SUBS, LANES), F32)],
        "v" * (8 + len(last)),
        [
            products,
            vmem((2, tiles * TERMS, LANES), F32),
            vmem((blocks * 3 * PACK // 2, LANES), F32),
        ],
        limit=16,
    )(hot, mask, summed, found, state, marks, first, second, *last)
    parts = lax.all_to_all(send, "freq", 0, 0)
    consensus_out, dual_out = fit(gram_cholesky(channels), parts, send)
    return tuple(array[None] for array in (gain_part, consensus_out, dual_out))


def solution(mesh):
    placed = (
        P("freq", "tm", None, None),
        P("freq", "tm", None, None),
        P("freq", "tm", None),
        P("freq", None, None),
        P("freq", None, None),
        P("freq", None, None),
        P(),
        P("freq"),
        P(),
        P(),
    )
    return jax.shard_map(
        shards,
        mesh=mesh,
        in_specs=placed,
        out_specs=(P("freq", None, "tm"), P("freq", None, "tm"), P("freq", None, "tm")),
        check_vma=False,
    )
```

```python
import jax
import jax.numpy as jnp
import numpy as np
from jax import lax
from jax.experimental import pallas as pl
from jax.experimental.pallas import tpu as pltpu
from jax.sharding import PartitionSpec as P

SWEEPS = 2
LANES = 128
SUBS = 8
PRODS = 48
TERMS = 24
PACK = 16
F32 = jnp.float32
BF16 = jnp.bfloat16


def mul_conj(a, b):
    return (a[0] * b[0] + a[1] * b[1], a[1] * b[0] - a[0] * b[1])


def copy_in(pairs, sem):
    copies = [
        pltpu.make_async_copy(source, target, sem.at[index])
        for index, (source, target) in enumerate(pairs)
    ]
    for copy in copies:
        copy.start()
    return copies


def widen_kernel(vis_hbm, model_hbm, keep_hbm, *refs):
    vis_ref, model_ref, keep_ref, sem = refs[-4:]
    copies = copy_in(
        [(vis_hbm, vis_ref), (keep_hbm, keep_ref), (model_hbm, model_ref)], sem
    )
    for copy in copies:
        copy.wait()
    start = 0
    for out_ref in refs[:-4]:
        tiles = out_ref.shape[0] // (2 * SUBS)
        for tile in range(tiles):
            lanes = pl.ds((start + tile) * LANES, LANES)
            out_ref[pl.ds(tile * SUBS, SUBS), :] = vis_ref[:, lanes].astype(F32)
            out_ref[pl.ds((tiles + tile) * SUBS, SUBS), :] = model_ref[:, lanes].astype(
                F32
            ) * keep_ref[:, lanes].astype(F32)
        start += tiles


def slot_products(slot_ref, group, tiles):
    def load(part, component):
        start = (part * tiles + group * SUBS) * SUBS + component
        return slot_ref[pl.ds(start, SUBS, stride=SUBS), :]

    seen = [(load(0, 2 * e), load(0, 2 * e + 1)) for e in range(4)]
    model = [(load(1, 2 * e), load(1, 2 * e + 1)) for e in range(4)]
    rows = []
    for v in range(4):
        for m in range(4):
            rows.extend(mul_conj(seen[v], model[m]))
    rows.extend(entry[0] * entry[0] + entry[1] * entry[1] for entry in model)
    for left, right in ((0, 1), (2, 3), (0, 2), (1, 3)):
        rows.extend(mul_conj(model[left], model[right]))
    a = mul_conj(model[0], model[3])
    b = mul_conj(model[1], model[2])
    rows.extend((a[0] + b[0], a[0] - b[0], a[1] + b[1], a[1] - b[1]))
    return rows


def add_products(slot_refs, before_ref, out_ref, group):
    tiles = slot_refs[0].shape[0] // (2 * SUBS)
    at = pl.ds(group * SUBS, SUBS)
    total = None
    for slot_ref in slot_refs:
        rows = slot_products(slot_ref, group, tiles)
        total = rows if total is None else [x + y for x, y in zip(total, rows)]
    for index, row in enumerate(total):
        if before_ref is not None:
            row = row + before_ref[index, at, :]
            total[index] = row
        out_ref[index, at, :] = row
    return total


def gain_tables(gains):
    return [
        [jnp.broadcast_to(gain[h : h + 1], (SUBS, LANES)) for h in range(gain.shape[0])]
        for gain in gains
    ]


def gather_gains(tables, station_ref, group):
    station = station_ref[pl.ds(group * SUBS, SUBS), :]
    offset, block = station & (LANES - 1), station >> 7
    values = []
    for table in tables:
        value = None
        for h, row in enumerate(table):
            found = jnp.take_along_axis(row, offset, axis=1, mode="promise_in_bounds")
            value = found if value is None else jnp.where(block == h, found, value)
        values.append(value)
    return values


def tables_kernel(count, *refs):
    slot_refs, channel_ref = refs[:count], refs[count]
    station_hbms, array_hbms = refs[count + 1 : count + 3], refs[count + 3 : count + 7]
    prod_refs = refs[count + 7 : 2 * count + 7]
    outs = refs[2 * count + 7 : -5]
    hot_ref, mask_ref, seen_ref, state_ref, own_ref, first_ref, second_ref = outs
    gains_ref, consensus_ref, dual_ref, penalty_ref, sem = refs[-5:]
    station_refs = (first_ref, second_ref)
    copies = copy_in(
        list(
            zip(
                station_hbms + array_hbms,
                station_refs + (gains_ref, consensus_ref, dual_ref, penalty_ref),
            )
        ),
        sem,
    )
    tiles = first_ref.shape[0]
    for slot_ref, prod_ref in zip(slot_refs, prod_refs, strict=True):
        for group in range(prod_ref.shape[1] // SUBS):
            add_products([slot_ref], None, prod_ref, group)
    for copy in copies:
        copy.wait()
    blocks = gains_ref.shape[1] // LANES
    for h in range(blocks):
        lanes = pl.ds(h * LANES, LANES)
        penalty = penalty_ref[:, lanes]
        gain = gains_ref[:, lanes]
        target = penalty * (consensus_ref[:, lanes] - dual_ref[:, lanes])
        for j in range(SUBS):
            state_ref[pl.ds(j * SUBS + h, 1), :] = gain[j : j + 1]
            state_ref[pl.ds((SUBS + j) * SUBS + h, 1), :] = target[j : j + 1]
        state_ref[pl.ds(2 * SUBS * SUBS + h, 1), :] = penalty
    gains = [state_ref[pl.ds(j * SUBS, blocks), :] for j in range(SUBS)]
    tables = gain_tables(gains)
    for part, station_ref in enumerate(station_refs):
        for group in range(tiles // SUBS):
            for j, value in enumerate(gather_gains(tables, station_ref, group)):
                seen_ref[part, j, pl.ds(group * SUBS, SUBS), :] = value
    place = lax.axis_index("tm")
    own_ref[:SUBS, :] = dual_ref[:, pl.ds(pl.multiple_of(place * LANES, LANES), LANES)]
    own_ref[SUBS:, :] = jnp.full((SUBS, LANES), channel_ref[0].astype(F32))
    row = lax.broadcasted_iota(jnp.int32, (LANES, LANES), 0)
    lower = lax.broadcasted_iota(jnp.int32, (PACK, LANES), 0) >= SUBS
    for part, station_ref in enumerate(station_refs):
        for tile in range(tiles):
            station = station_ref[pl.ds(tile, 1), :]
            offset, block = station & (LANES - 1), station >> 7
            lanes = pl.ds((part * tiles + tile) * LANES, LANES)
            hot_ref[lanes, :] = jnp.where(row == offset, 1.0, 0.0).T.astype(BF16)
            wide = jnp.broadcast_to(block, (PACK, LANES))
            for h in range(blocks):
                mask_ref[pl.ds(h * PACK, PACK), lanes] = jnp.where(wide == h, 1.0, 0.0).astype(
                    BF16
                )
            for pair in range(blocks // 2):
                mine = jnp.where(lower, 2 * pair + 1, 2 * pair)
                mask_ref[pl.ds((blocks + pair) * PACK, PACK), lanes] = jnp.where(
                    wide == mine, 1.0, 0.0
                ).astype(BF16)


def more_kernel(before_ref, *refs):
    for group in range(before_ref.shape[1] // SUBS):
        add_products(refs[:-1], before_ref, refs[-1], group)


def gram(gain):
    entry = [(gain[2 * e], gain[2 * e + 1]) for e in range(4)]
    h00 = sum(part * part for part in entry[0] + entry[2])
    h11 = sum(part * part for part in entry[1] + entry[3])
    top = mul_conj(entry[1], entry[0])
    low = mul_conj(entry[3], entry[2])
    return h00, h11, top[0] + low[0], top[1] + low[1]


def baseline_terms(prod, gain_second, gain_first):
    def num(gain, swap):
        out = []
        for i in range(2):
            for l in range(2):
                real = imag = None
                for j in range(2):
                    for k in range(2):
                        if swap:
                            index = 4 * (2 * j + i) + 2 * k + l
                        else:
                            index = 4 * (2 * i + j) + 2 * l + k
                        tr, ti = prod(2 * index), prod(2 * index + 1)
                        gr, gi = gain[2 * (2 * j + k)], gain[2 * (2 * j + k) + 1]
                        if swap:
                            addr, addi = tr * gr + ti * gi, tr * gi - ti * gr
                        else:
                            addr, addi = tr * gr - ti * gi, tr * gi + ti * gr
                        real = addr if real is None else real + addr
                        imag = addi if imag is None else imag + addi
                out.extend((real, imag))
        return out

    n00, n01, n10, n11, pr, pi, qr, qi, rr, ri, sr, si, apr, amr, api, ami = (
        prod(32 + index) for index in range(16)
    )
    h00, h11, hr, hi = gram(gain_second)
    den_first = [
        n00 * h00 + n01 * h11 + 2.0 * (pr * hr - pi * hi),
        n10 * h00 + n11 * h11 + 2.0 * (qr * hr - qi * hi),
        rr * h00 + sr * h11 + apr * hr - ami * hi,
        ri * h00 + si * h11 + api * hr + amr * hi,
    ]
    h00, h11, hr, hi = gram(gain_first)
    den_second = [
        n00 * h00 + n10 * h11 + 2.0 * (rr * hr + ri * hi),
        n01 * h00 + n11 * h11 + 2.0 * (sr * hr + si * hi),
        pr * h00 + qr * h11 + apr * hr + api * hi,
        amr * hi - pi * h00 - qi * h11 - ami * hr,
    ]
    return num(gain_second, False) + den_first, num(gain_first, True) + den_second


def store_terms(prod, gain_first, gain_second, group, term_ref):
    start = group * SUBS * TERMS
    for part, rows in enumerate(baseline_terms(prod, gain_second, gain_first)):
        for j, row in enumerate(rows):
            where, apart = (start + j, 8) if j < 8 else (start + 8 + j, 4)
            high = row.astype(BF16).astype(F32)
            term_ref[part, pl.ds(where, SUBS, stride=TERMS), :] = high
            term_ref[part, pl.ds(where + apart, SUBS, stride=TERMS), :] = row - high


def scatter_terms(term_ref, hot_ref, mask_ref, group, start, part):
    rows = mask_ref.shape[0]
    tiles = hot_ref.shape[0] // (2 * LANES)
    blocks = rows * 2 // (3 * PACK)
    columns = []
    for tile in range(group * SUBS, (group + 1) * SUBS):
        lanes = pl.ds((part * tiles + start + tile) * LANES, LANES)
        num = term_ref[part, pl.ds(tile * TERMS, PACK), :].astype(BF16)
        den = term_ref[part, pl.ds(tile * TERMS + PACK, SUBS), :]
        den = jnp.concatenate([den, den], axis=0).astype(BF16)
        column = [
            mask_ref[pl.ds(h * PACK, PACK), lanes] * (num if h < blocks else den)
            for h in range(rows // PACK)
        ]
        columns.append(jnp.concatenate(column, axis=0))
    at = pl.ds((part * tiles + start + group * SUBS) * LANES, SUBS * LANES)
    return jnp.dot(
        jnp.concatenate(columns, axis=1), hot_ref[at, :], preferred_element_type=F32
    )


def piece_totals(prod_ref, gains_of, term_ref, hot_ref, mask_ref, start, total):
    for group in range(prod_ref.shape[1] // SUBS):
        at = pl.ds(group * SUBS, SUBS)
        gain_first, gain_second = (gains_of(part, start // SUBS + group) for part in range(2))
        store_terms(
            lambda index: prod_ref[index, at, :], gain_first, gain_second, group, term_ref
        )
        for part in range(2):
            add = scatter_terms(term_ref, hot_ref, mask_ref, group, start, part)
            total = add if total is None else total + add
    return total


def found_gains(found_ref):
    return lambda part, group: [
        found_ref[part, j, pl.ds(group * SUBS, SUBS), :] for j in range(SUBS)
    ]


def piece_kernel(start, hot_ref, mask_ref, found_ref, before_ref, *refs):
    slot_refs = refs[:-3]
    prod_ref, total_ref, term_ref = refs[-3:]
    for group in range(prod_ref.shape[1] // SUBS):
        add_products(slot_refs, before_ref, prod_ref, group)
    total_ref[...] = piece_totals(
        prod_ref, found_gains(found_ref), term_ref, hot_ref, mask_ref, start, None
    )


def solve(num, den, gain, target, penalty):
    rhs = [tuple(num[2 * e + part] + target[2 * e + part] for part in range(2)) for e in range(4)]
    r00, r11, r01 = den[0] + penalty, den[1] + penalty, (den[2], den[3])
    scale = 0.5 / (r00 * r11 - (r01[0] * r01[0] + r01[1] * r01[1]))
    out = []
    for i in range(2):
        a, b = rhs[2 * i], rhs[2 * i + 1]
        cross = mul_conj(b, r01)
        out.extend((a[part] * r11 - cross[part]) * scale for part in range(2))
        out.append((b[0] * r00 - (a[0] * r01[0] - a[1] * r01[1])) * scale)
        out.append((b[1] * r00 - (a[0] * r01[1] + a[1] * r01[0])) * scale)
    return [value + 0.5 * old for value, old in zip(out, gain)]


def own_place():
    return lax.axis_index("tm")


def sweeps_kernel(counts, *refs):
    pieces, slots = counts
    hot_ref, mask_ref, found_ref, state_ref, own_ref, first_ref, second_ref = refs[:7]
    prod_refs, partial_refs = refs[7 : 6 + pieces], refs[6 + pieces : 5 + 2 * pieces]
    before_ref, slot_refs = refs[5 + 2 * pieces], refs[6 + 2 * pieces : 6 + 2 * pieces + slots]
    gain_out_ref, send_ref, last_ref, total_ref = refs[6 + 2 * pieces + slots : -pieces]
    term_refs = refs[-pieces:]
    blocks = mask_ref.shape[0] * 2 // (3 * PACK)
    gains = [state_ref[pl.ds(j * SUBS, blocks), :] for j in range(SUBS)]
    target = [state_ref[pl.ds((SUBS + j) * SUBS, blocks), :] for j in range(SUBS)]
    penalty = state_ref[pl.ds(2 * SUBS * SUBS, blocks), :]
    for group in range(last_ref.shape[1] // SUBS):
        add_products(slot_refs, before_ref, last_ref, group)
    prod_refs = (*prod_refs, last_ref)
    for sweep in range(SWEEPS):
        total = None
        if sweep:
            tables = gain_tables(gains)

            def gains_of(part, group, tables=tables):
                return gather_gains(tables, (first_ref, second_ref)[part], group)

        else:
            gains_of = found_gains(found_ref)
            for partial_ref in partial_refs:
                total = partial_ref[...] if total is None else total + partial_ref[...]
        start = 0
        for prod_ref, term_ref in zip(prod_refs, term_refs, strict=True):
            if sweep or prod_ref is last_ref:
                total = piece_totals(
                    prod_ref, gains_of, term_ref, hot_ref, mask_ref, start, total
                )
            start += prod_ref.shape[1]
        total_ref[...] = total

        def rows(start, stride):
            return total_ref[pl.ds(start, blocks, stride=stride), :]

        num = [rows(j, PACK) + rows(SUBS + j, PACK) for j in range(SUBS)]
        den = [
            rows(blocks * PACK + j, SUBS) + rows(blocks * PACK + 4 + j, SUBS) for j in range(4)
        ]
        gains = solve(num, den, gains, target, penalty)
    for j in range(SUBS):
        total_ref[pl.ds(j, blocks, stride=SUBS), :] = gains[j]
    place = own_place()
    part = total_ref[pl.ds(pl.multiple_of(place * SUBS, SUBS), SUBS), :]
    gain_out_ref[...] = part
    combined, mark = part + own_ref[:SUBS, :], own_ref[SUBS:, :]
    for channel in range(send_ref.shape[0]):
        send_ref[channel, :SUBS, :] = combined
        send_ref[channel, SUBS:, :] = mark


def legendre(position):
    square = position * position
    return [None, position, 1.5 * square - 0.5, (2.5 * square - 1.5) * position]


def fit(gram_factor, parts, send):
    scale = float(parts.shape[0]) - 1.0

    def basis(channel):
        return legendre(2.0 * channel / scale - 1.0)

    value = parts[:, :SUBS]
    moments = [
        jnp.sum(value if weight is None else weight * value, axis=0)
        for weight in basis(parts[:, SUBS:])
    ]
    middle = []
    for k in range(4):
        rest = moments[k]
        for earlier in range(k):
            rest = rest - gram_factor[k][earlier] * middle[earlier]
        middle.append(rest * (1.0 / gram_factor[k][k]))
    coeffs = [None] * 4
    for k in reversed(range(4)):
        rest = middle[k]
        for later in range(k + 1, 4):
            rest = rest - gram_factor[later][k] * coeffs[later]
        coeffs[k] = rest * (1.0 / gram_factor[k][k])
    own = basis(send[0, SUBS:])
    fitted = coeffs[0]
    for k in range(1, 4):
        fitted = fitted + own[k] * coeffs[k]
    return fitted, send[0, :SUBS] - fitted


def gram_cholesky(channels):
    x = 2.0 * np.arange(channels, dtype=np.float64) / (channels - 1.0) - 1.0
    basis = np.stack([np.ones_like(x), x, 1.5 * x * x - 0.5, (2.5 * x * x - 1.5) * x], -1)
    factor = np.linalg.cholesky(basis.T @ basis)
    return [[float(value) for value in row] for row in factor]


SPACES = {"s": pltpu.SMEM, "v": pltpu.VMEM, "h": pltpu.HBM}


def call(kernel, shapes, spaces, scratch=(), limit=8, micros=0):
    cost = pl.CostEstimate(
        flops=int(micros * 1.0e9), transcendentals=0, bytes_accessed=int(micros * 3.0e6)
    )
    run = pl.pallas_call(
        kernel,
        out_shape=shapes,
        in_specs=[pl.BlockSpec(memory_space=SPACES[space]) for space in spaces],
        out_specs=[pl.BlockSpec(memory_space=shape.memory_space) for shape in shapes],
        scratch_shapes=list(scratch),
        compiler_params=pltpu.CompilerParams(vmem_limit_bytes=limit << 20),
        cost_estimate=cost if micros else None,
    )

    def placed(*args):
        return run(
            *(
                arg if space == "s" else pltpu.with_memory_space_constraint(arg, SPACES[space])
                for arg, space in zip(args, spaces, strict=True)
            )
        )

    return placed


def shards(
    visibility,
    model_visibility,
    keep_mask,
    gains_in,
    consensus_in,
    dual_in,
    penalty,
    channel_index,
    first_station,
    second_station,
):
    baselines = visibility.shape[3]
    stations = gains_in.shape[2]
    slots = lax.axis_size("tm")
    channels = lax.axis_size("freq")
    tiles = baselines // LANES
    blocks = stations // LANES
    assert blocks == slots and blocks % 2 == 0 and channel_index.shape == (1,)
    vmem = pltpu.VMEM

    def swap(array, step):
        return lax.ppermute(array, "tm", [(i, i ^ step) for i in range(slots)])

    sizes = [tiles // 2, tiles // 2]
    pieces = call(
        widen_kernel,
        [vmem((2 * size * SUBS, LANES), F32) for size in sizes],
        "hhh",
        [
            vmem((SUBS, baselines), BF16),
            vmem((SUBS, baselines), BF16),
            vmem((1, baselines), jnp.int32),
            pltpu.SemaphoreType.DMA((3,)),
        ],
    )(
        visibility.reshape(SUBS, baselines),
        model_visibility.reshape(SUBS, baselines),
        keep_mask.reshape(1, baselines),
    )
    far = []
    for piece in pieces:
        got = []
        step = slots // 2
        while step > 1:
            got += [swap(array, step) for array in [piece, *got]]
            step //= 2
        far.append(got)
    gains, consensus, dual = (
        array.reshape(SUBS, stations) for array in (gains_in, consensus_in, dual_in)
    )
    products = [vmem((PRODS, size, LANES), F32) for size in sizes]
    terms = [vmem((2, size * TERMS, LANES), F32) for size in sizes]
    seen = vmem((2, SUBS, tiles, LANES), F32)
    station = vmem((tiles, LANES), jnp.int32)
    wide = vmem((SUBS, stations), F32)
    totals = vmem((blocks * 3 * PACK // 2, LANES), F32)
    count = len(sizes)
    tables = call(
        lambda *refs: tables_kernel(count, *refs),
        [
            *products,
            vmem((2 * baselines, LANES), BF16),
            vmem((blocks * 3 * PACK // 2, 2 * baselines), BF16),
            seen,
            vmem(((2 * SUBS + 1) * SUBS, LANES), F32),
            vmem((2 * SUBS, LANES), F32),
            station,
            station,
        ],
        "v" * count + "shhhhhh",
        [wide, wide, wide, vmem((1, stations), F32), pltpu.SemaphoreType.DMA((6,))],
        limit=16,
        micros=1,
    )(
        *pieces,
        channel_index,
        first_station.reshape(tiles, LANES),
        second_station.reshape(tiles, LANES),
        gains,
        consensus,
        dual,
        penalty.reshape(1, stations),
    )
    summed = list(tables[:count])
    hot, mask, found, state, own, first, second = tables[count:]
    pieces, state = lax.optimization_barrier((pieces, state))
    near = [swap(piece, 1) for piece in pieces]
    far[0], state = lax.optimization_barrier((far[0], state))
    last = [[swap(array, 1) for array in far[0]]]
    (summed[0],) = call(more_kernel, [products[0]], "v" * (2 + len(far[0])), micros=0.001)(
        summed[0], near[0], *far[0]
    )
    far[1], last[0], found = lax.optimization_barrier((far[1], last[0], found))
    last.append([swap(array, 1) for array in far[1]])
    (summed[1],) = call(more_kernel, [products[1]], "v" * (2 + len(far[1])), micros=0.001)(
        summed[1], near[1], *far[1]
    )
    summed[0], partial = call(
        lambda *refs: piece_kernel(0, *refs),
        [products[0], totals],
        "v" * (4 + len(last[0])),
        [terms[0]],
        limit=16,
        micros=0.001,
    )(hot, mask, found, summed[0], *last[0])
    gain_part, send = call(
        lambda *refs: sweeps_kernel((count, len(last[1])), *refs),
        [vmem((SUBS, LANES), F32), vmem((channels, 2 * SUBS, LANES), F32)],
        "v" * (10 + len(last[1])),
        [products[1], totals, *terms],
        limit=16,
    )(
        hot,
        mask,
        found,
        state,
        own,
        first,
        second,
        summed[0],
        partial,
        summed[1],
        *last[1],
    )
    parts = lax.all_to_all(send, "freq", 0, 0)
    consensus_out, dual_out = fit(gram_cholesky(channels), parts, send)
    return tuple(array[None] for array in (gain_part, consensus_out, dual_out))


def solution(mesh):
    placed = (
        P("freq", "tm", None, None),
        P("freq", "tm", None, None),
        P("freq", "tm", None),
        P("freq", None, None),
        P("freq", None, None),
        P("freq", None, None),
        P(),
        P("freq"),
        P(),
        P(),
    )
    return jax.shard_map(
        shards,
        mesh=mesh,
        in_specs=placed,
        out_specs=(P("freq", None, "tm"), P("freq", None, "tm"), P("freq", None, "tm")),
        check_vma=False,
    )
```

```python
import jax
import jax.numpy as jnp
import numpy as np
from jax import lax
from jax.experimental import pallas as pl
from jax.experimental.pallas import tpu as pltpu
from jax.sharding import PartitionSpec as P

SWEEPS = 2
LANES = 128
SUBS = 8
PRODS = 48
TERMS = 24
PACK = 16
F32 = jnp.float32
BF16 = jnp.bfloat16


def mul_conj(a, b):
    return (a[0] * b[0] + a[1] * b[1], a[1] * b[0] - a[0] * b[1])


def copy_in(pairs, sem):
    copies = [
        pltpu.make_async_copy(source, target, sem.at[index])
        for index, (source, target) in enumerate(pairs)
    ]
    for copy in copies:
        copy.start()
    return copies


def widen_kernel(vis_hbm, model_hbm, keep_hbm, *refs):
    vis_ref, model_ref, keep_ref, sem = refs[-4:]
    copies = copy_in(
        [(vis_hbm, vis_ref), (keep_hbm, keep_ref), (model_hbm, model_ref)], sem
    )
    for copy in copies:
        copy.wait()
    start = 0
    for out_ref in refs[:-4]:
        tiles = out_ref.shape[0] // (2 * SUBS)
        for tile in range(tiles):
            lanes = pl.ds((start + tile) * LANES, LANES)
            out_ref[pl.ds(tile * SUBS, SUBS), :] = vis_ref[:, lanes].astype(F32)
            out_ref[pl.ds((tiles + tile) * SUBS, SUBS), :] = model_ref[:, lanes].astype(
                F32
            ) * keep_ref[:, lanes].astype(F32)
        start += tiles


def slot_products(slot_ref, group, tiles):
    def load(part, component):
        start = (part * tiles + group * SUBS) * SUBS + component
        return slot_ref[pl.ds(start, SUBS, stride=SUBS), :]

    seen = [(load(0, 2 * e), load(0, 2 * e + 1)) for e in range(4)]
    model = [(load(1, 2 * e), load(1, 2 * e + 1)) for e in range(4)]
    rows = []
    for v in range(4):
        for m in range(4):
            rows.extend(mul_conj(seen[v], model[m]))
    rows.extend(entry[0] * entry[0] + entry[1] * entry[1] for entry in model)
    for left, right in ((0, 1), (2, 3), (0, 2), (1, 3)):
        rows.extend(mul_conj(model[left], model[right]))
    a = mul_conj(model[0], model[3])
    b = mul_conj(model[1], model[2])
    rows.extend((a[0] + b[0], a[0] - b[0], a[1] + b[1], a[1] - b[1]))
    return rows


def add_products(slot_refs, before_ref, out_ref, group):
    tiles = slot_refs[0].shape[0] // (2 * SUBS)
    at = pl.ds(group * SUBS, SUBS)
    total = None
    for slot_ref in slot_refs:
        rows = slot_products(slot_ref, group, tiles)
        total = rows if total is None else [x + y for x, y in zip(total, rows)]
    for index, row in enumerate(total):
        if before_ref is not None:
            row = row + before_ref[index, at, :]
            total[index] = row
        out_ref[index, at, :] = row
    return total


def gain_tables(gains):
    return [
        [jnp.broadcast_to(gain[h : h + 1], (SUBS, LANES)) for h in range(gain.shape[0])]
        for gain in gains
    ]


def gather_gains(tables, station_ref, group):
    station = station_ref[pl.ds(group * SUBS, SUBS), :]
    offset, block = station & (LANES - 1), station >> 7
    values = []
    for table in tables:
        value = None
        for h, row in enumerate(table):
            found = jnp.take_along_axis(row, offset, axis=1, mode="promise_in_bounds")
            value = found if value is None else jnp.where(block == h, found, value)
        values.append(value)
    return values


def tables_kernel(count, *refs):
    slot_refs, channel_ref = refs[:count], refs[count]
    station_hbms, array_hbms = refs[count + 1 : count + 3], refs[count + 3 : count + 7]
    prod_refs = refs[count + 7 : 2 * count + 7]
    outs = refs[2 * count + 7 : -5]
    hot_ref, mask_ref, seen_ref, state_ref, own_ref, first_ref, second_ref = outs
    gains_ref, consensus_ref, dual_ref, penalty_ref, sem = refs[-5:]
    station_refs = (first_ref, second_ref)
    copies = copy_in(
        list(
            zip(
                station_hbms + array_hbms,
                station_refs + (gains_ref, consensus_ref, dual_ref, penalty_ref),
            )
        ),
        sem,
    )
    tiles = first_ref.shape[0]
    for slot_ref, prod_ref in zip(slot_refs, prod_refs, strict=True):
        for group in range(prod_ref.shape[1] // SUBS):
            add_products([slot_ref], None, prod_ref, group)
    for copy in copies:
        copy.wait()
    blocks = gains_ref.shape[1] // LANES
    for h in range(blocks):
        lanes = pl.ds(h * LANES, LANES)
        penalty = penalty_ref[:, lanes]
        gain = gains_ref[:, lanes]
        target = penalty * (consensus_ref[:, lanes] - dual_ref[:, lanes])
        for j in range(SUBS):
            state_ref[pl.ds(j * SUBS + h, 1), :] = gain[j : j + 1]
            state_ref[pl.ds((SUBS + j) * SUBS + h, 1), :] = target[j : j + 1]
        state_ref[pl.ds(2 * SUBS * SUBS + h, 1), :] = penalty
    gains = [state_ref[pl.ds(j * SUBS, blocks), :] for j in range(SUBS)]
    tables = gain_tables(gains)
    for part, station_ref in enumerate(station_refs):
        for group in range(tiles // SUBS):
            for j, value in enumerate(gather_gains(tables, station_ref, group)):
                seen_ref[part, j, pl.ds(group * SUBS, SUBS), :] = value
    place = lax.axis_index("tm")
    own_ref[:SUBS, :] = dual_ref[:, pl.ds(pl.multiple_of(place * LANES, LANES), LANES)]
    own_ref[SUBS:, :] = jnp.full((SUBS, LANES), channel_ref[0].astype(F32))
    row = lax.broadcasted_iota(jnp.int32, (LANES, LANES), 0)
    lower = lax.broadcasted_iota(jnp.int32, (PACK, LANES), 0) >= SUBS
    for part, station_ref in enumerate(station_refs):
        for tile in range(tiles):
            station = station_ref[pl.ds(tile, 1), :]
            offset, block = station & (LANES - 1), station >> 7
            lanes = pl.ds((part * tiles + tile) * LANES, LANES)
            hot_ref[lanes, :] = jnp.where(row == offset, 1.0, 0.0).T.astype(BF16)
            wide = jnp.broadcast_to(block, (PACK, LANES))
            for h in range(blocks):
                mask_ref[pl.ds(h * PACK, PACK), lanes] = jnp.where(wide == h, 1.0, 0.0).astype(
                    BF16
                )
            for pair in range(blocks // 2):
                mine = jnp.where(lower, 2 * pair + 1, 2 * pair)
                mask_ref[pl.ds((blocks + pair) * PACK, PACK), lanes] = jnp.where(
                    wide == mine, 1.0, 0.0
                ).astype(BF16)


def more_kernel(before_ref, *refs):
    for group in range(before_ref.shape[1] // SUBS):
        add_products(refs[:-1], before_ref, refs[-1], group)


def gram(gain):
    entry = [(gain[2 * e], gain[2 * e + 1]) for e in range(4)]
    h00 = sum(part * part for part in entry[0] + entry[2])
    h11 = sum(part * part for part in entry[1] + entry[3])
    top = mul_conj(entry[1], entry[0])
    low = mul_conj(entry[3], entry[2])
    return h00, h11, top[0] + low[0], top[1] + low[1]


def baseline_terms(prod, gain_second, gain_first):
    def num(gain, swap):
        out = []
        for i in range(2):
            for l in range(2):
                real = imag = None
                for j in range(2):
                    for k in range(2):
                        if swap:
                            index = 4 * (2 * j + i) + 2 * k + l
                        else:
                            index = 4 * (2 * i + j) + 2 * l + k
                        tr, ti = prod(2 * index), prod(2 * index + 1)
                        gr, gi = gain[2 * (2 * j + k)], gain[2 * (2 * j + k) + 1]
                        if swap:
                            addr, addi = tr * gr + ti * gi, tr * gi - ti * gr
                        else:
                            addr, addi = tr * gr - ti * gi, tr * gi + ti * gr
                        real = addr if real is None else real + addr
                        imag = addi if imag is None else imag + addi
                out.extend((real, imag))
        return out

    n00, n01, n10, n11, pr, pi, qr, qi, rr, ri, sr, si, apr, amr, api, ami = (
        prod(32 + index) for index in range(16)
    )
    h00, h11, hr, hi = gram(gain_second)
    den_first = [
        n00 * h00 + n01 * h11 + 2.0 * (pr * hr - pi * hi),
        n10 * h00 + n11 * h11 + 2.0 * (qr * hr - qi * hi),
        rr * h00 + sr * h11 + apr * hr - ami * hi,
        ri * h00 + si * h11 + api * hr + amr * hi,
    ]
    h00, h11, hr, hi = gram(gain_first)
    den_second = [
        n00 * h00 + n10 * h11 + 2.0 * (rr * hr + ri * hi),
        n01 * h00 + n11 * h11 + 2.0 * (sr * hr + si * hi),
        pr * h00 + qr * h11 + apr * hr + api * hi,
        amr * hi - pi * h00 - qi * h11 - ami * hr,
    ]
    return num(gain_second, False) + den_first, num(gain_first, True) + den_second


def store_terms(prod, gain_first, gain_second, group, term_ref):
    start = group * SUBS * TERMS
    for part, rows in enumerate(baseline_terms(prod, gain_second, gain_first)):
        for j, row in enumerate(rows):
            where, apart = (start + j, 8) if j < 8 else (start + 8 + j, 4)
            high = row.astype(BF16).astype(F32)
            term_ref[part, pl.ds(where, SUBS, stride=TERMS), :] = high
            term_ref[part, pl.ds(where + apart, SUBS, stride=TERMS), :] = row - high


def scatter_terms(term_ref, hot_ref, mask_ref, group, start, part):
    rows = mask_ref.shape[0]
    tiles = hot_ref.shape[0] // (2 * LANES)
    blocks = rows * 2 // (3 * PACK)
    columns = []
    for tile in range(group * SUBS, (group + 1) * SUBS):
        lanes = pl.ds((part * tiles + start + tile) * LANES, LANES)
        num = term_ref[part, pl.ds(tile * TERMS, PACK), :].astype(BF16)
        den = term_ref[part, pl.ds(tile * TERMS + PACK, SUBS), :]
        den = jnp.concatenate([den, den], axis=0).astype(BF16)
        column = [
            mask_ref[pl.ds(h * PACK, PACK), lanes] * (num if h < blocks else den)
            for h in range(rows // PACK)
        ]
        columns.append(jnp.concatenate(column, axis=0))
    at = pl.ds((part * tiles + start + group * SUBS) * LANES, SUBS * LANES)
    return jnp.dot(
        jnp.concatenate(columns, axis=1), hot_ref[at, :], preferred_element_type=F32
    )


def piece_totals(prod_ref, gains_of, term_ref, hot_ref, mask_ref, start, total):
    for group in range(prod_ref.shape[1] // SUBS):
        at = pl.ds(group * SUBS, SUBS)
        gain_first, gain_second = (gains_of(part, start // SUBS + group) for part in range(2))
        store_terms(
            lambda index: prod_ref[index, at, :], gain_first, gain_second, group, term_ref
        )
        for part in range(2):
            add = scatter_terms(term_ref, hot_ref, mask_ref, group, start, part)
            total = add if total is None else total + add
    return total


def found_gains(found_ref):
    return lambda part, group: [
        found_ref[part, j, pl.ds(group * SUBS, SUBS), :] for j in range(SUBS)
    ]


def piece_kernel(start, hot_ref, mask_ref, found_ref, before_ref, *refs):
    slot_refs = refs[:-3]
    prod_ref, total_ref, term_ref = refs[-3:]
    for group in range(prod_ref.shape[1] // SUBS):
        add_products(slot_refs, before_ref, prod_ref, group)
    total_ref[...] = piece_totals(
        prod_ref, found_gains(found_ref), term_ref, hot_ref, mask_ref, start, None
    )


def solve(num, den, gain, target, penalty):
    rhs = [tuple(num[2 * e + part] + target[2 * e + part] for part in range(2)) for e in range(4)]
    r00, r11, r01 = den[0] + penalty, den[1] + penalty, (den[2], den[3])
    scale = 0.5 / (r00 * r11 - (r01[0] * r01[0] + r01[1] * r01[1]))
    out = []
    for i in range(2):
        a, b = rhs[2 * i], rhs[2 * i + 1]
        cross = mul_conj(b, r01)
        out.extend((a[part] * r11 - cross[part]) * scale for part in range(2))
        out.append((b[0] * r00 - (a[0] * r01[0] - a[1] * r01[1])) * scale)
        out.append((b[1] * r00 - (a[0] * r01[1] + a[1] * r01[0])) * scale)
    return [value + 0.5 * old for value, old in zip(out, gain)]


def own_place():
    return lax.axis_index("tm")


def sweeps_kernel(counts, *refs):
    pieces, slots = counts
    hot_ref, mask_ref, found_ref, state_ref, own_ref, first_ref, second_ref = refs[:7]
    prod_refs, partial_refs = refs[7 : 6 + pieces], refs[6 + pieces : 5 + 2 * pieces]
    before_ref, slot_refs = refs[5 + 2 * pieces], refs[6 + 2 * pieces : 6 + 2 * pieces + slots]
    gain_out_ref, sum_ref, send_ref, last_ref, total_ref = refs[6 + 2 * pieces + slots : -pieces]
    term_refs = refs[-pieces:]
    blocks = mask_ref.shape[0] * 2 // (3 * PACK)
    gains = [state_ref[pl.ds(j * SUBS, blocks), :] for j in range(SUBS)]
    target = [state_ref[pl.ds((SUBS + j) * SUBS, blocks), :] for j in range(SUBS)]
    penalty = state_ref[pl.ds(2 * SUBS * SUBS, blocks), :]
    for group in range(last_ref.shape[1] // SUBS):
        add_products(slot_refs, before_ref, last_ref, group)
    prod_refs = (*prod_refs, last_ref)
    for sweep in range(SWEEPS):
        total = None
        if sweep:
            tables = gain_tables(gains)

            def gains_of(part, group, tables=tables):
                return gather_gains(tables, (first_ref, second_ref)[part], group)

        else:
            gains_of = found_gains(found_ref)
            for partial_ref in partial_refs:
                total = partial_ref[...] if total is None else total + partial_ref[...]
        start = 0
        for prod_ref, term_ref in zip(prod_refs, term_refs, strict=True):
            if sweep or prod_ref is last_ref:
                total = piece_totals(
                    prod_ref, gains_of, term_ref, hot_ref, mask_ref, start, total
                )
            start += prod_ref.shape[1]
        total_ref[...] = total

        def rows(start, stride):
            return total_ref[pl.ds(start, blocks, stride=stride), :]

        num = [rows(j, PACK) + rows(SUBS + j, PACK) for j in range(SUBS)]
        den = [
            rows(blocks * PACK + j, SUBS) + rows(blocks * PACK + 4 + j, SUBS) for j in range(4)
        ]
        gains = solve(num, den, gains, target, penalty)
    for j in range(SUBS):
        total_ref[pl.ds(j, blocks, stride=SUBS), :] = gains[j]
    place = own_place()
    part = total_ref[pl.ds(pl.multiple_of(place * SUBS, SUBS), SUBS), :]
    gain_out_ref[...] = part
    combined, mark = part + own_ref[:SUBS, :], own_ref[SUBS:, :]
    sum_ref[...] = combined
    for channel in range(send_ref.shape[0]):
        send_ref[channel, :SUBS, :] = combined
        send_ref[channel, SUBS:, :] = mark


def legendre(position):
    square = position * position
    return [None, position, 1.5 * square - 0.5, (2.5 * square - 1.5) * position]


def fit_kernel(gram_factor, parts_ref, own_ref, gain_ref, sum_ref, *refs):
    gain_hbm, consensus_hbm, dual_hbm, consensus_ref, dual_ref, sem = refs
    gain_copy = pltpu.make_async_copy(gain_ref, gain_hbm, sem.at[0])
    gain_copy.start()
    channels = parts_ref.shape[0]
    scale = float(channels) - 1.0

    def basis(channel):
        return legendre(2.0 * channel / scale - 1.0)

    moments = [None] * 4
    for channel in range(channels):
        value = parts_ref[channel, :SUBS, :]
        for k, weight in enumerate(basis(parts_ref[channel, SUBS:, :])):
            add = value if weight is None else weight * value
            moments[k] = add if moments[k] is None else moments[k] + add
    middle = []
    for k in range(4):
        rest = moments[k]
        for earlier in range(k):
            rest = rest - gram_factor[k][earlier] * middle[earlier]
        middle.append(rest * (1.0 / gram_factor[k][k]))
    coeffs = [None] * 4
    for k in reversed(range(4)):
        rest = middle[k]
        for later in range(k + 1, 4):
            rest = rest - gram_factor[later][k] * coeffs[later]
        coeffs[k] = rest * (1.0 / gram_factor[k][k])
    own = basis(own_ref[SUBS:, :])
    fitted = coeffs[0]
    for k in range(1, 4):
        fitted = fitted + own[k] * coeffs[k]
    consensus_ref[...] = fitted
    dual_ref[...] = sum_ref[...] - fitted
    consensus_copy = pltpu.make_async_copy(consensus_ref, consensus_hbm, sem.at[1])
    dual_copy = pltpu.make_async_copy(dual_ref, dual_hbm, sem.at[2])
    consensus_copy.start()
    dual_copy.start()
    gain_copy.wait()
    consensus_copy.wait()
    dual_copy.wait()


def gram_cholesky(channels):
    x = 2.0 * np.arange(channels, dtype=np.float64) / (channels - 1.0) - 1.0
    basis = np.stack([np.ones_like(x), x, 1.5 * x * x - 0.5, (2.5 * x * x - 1.5) * x], -1)
    factor = np.linalg.cholesky(basis.T @ basis)
    return [[float(value) for value in row] for row in factor]


SPACES = {"s": pltpu.SMEM, "v": pltpu.VMEM, "h": pltpu.HBM}


def call(kernel, shapes, spaces, scratch=(), limit=8, micros=0):
    cost = pl.CostEstimate(
        flops=int(micros * 1.0e9), transcendentals=0, bytes_accessed=int(micros * 3.0e6)
    )
    run = pl.pallas_call(
        kernel,
        out_shape=shapes,
        in_specs=[pl.BlockSpec(memory_space=SPACES[space]) for space in spaces],
        out_specs=[pl.BlockSpec(memory_space=shape.memory_space) for shape in shapes],
        scratch_shapes=list(scratch),
        compiler_params=pltpu.CompilerParams(vmem_limit_bytes=limit << 20),
        cost_estimate=cost if micros else None,
    )

    def placed(*args):
        return run(
            *(
                arg if space == "s" else pltpu.with_memory_space_constraint(arg, SPACES[space])
                for arg, space in zip(args, spaces, strict=True)
            )
        )

    return placed


def shards(
    visibility,
    model_visibility,
    keep_mask,
    gains_in,
    consensus_in,
    dual_in,
    penalty,
    channel_index,
    first_station,
    second_station,
):
    baselines = visibility.shape[3]
    stations = gains_in.shape[2]
    slots = lax.axis_size("tm")
    channels = lax.axis_size("freq")
    tiles = baselines // LANES
    blocks = stations // LANES
    assert blocks == slots and blocks % 2 == 0 and channel_index.shape == (1,)
    vmem = pltpu.VMEM

    def swap(array, step):
        return lax.ppermute(array, "tm", [(i, i ^ step) for i in range(slots)])

    sizes = [tiles // 2, tiles // 2]
    pieces = call(
        widen_kernel,
        [vmem((2 * size * SUBS, LANES), F32) for size in sizes],
        "hhh",
        [
            vmem((SUBS, baselines), BF16),
            vmem((SUBS, baselines), BF16),
            vmem((1, baselines), jnp.int32),
            pltpu.SemaphoreType.DMA((3,)),
        ],
    )(
        visibility.reshape(SUBS, baselines),
        model_visibility.reshape(SUBS, baselines),
        keep_mask.reshape(1, baselines),
    )
    far = []
    for piece in pieces:
        got = []
        step = slots // 2
        while step > 1:
            got += [swap(array, step) for array in [piece, *got]]
            step //= 2
        far.append(got)
    gains, consensus, dual = (
        array.reshape(SUBS, stations) for array in (gains_in, consensus_in, dual_in)
    )
    products = [vmem((PRODS, size, LANES), F32) for size in sizes]
    terms = [vmem((2, size * TERMS, LANES), F32) for size in sizes]
    seen = vmem((2, SUBS, tiles, LANES), F32)
    station = vmem((tiles, LANES), jnp.int32)
    wide = vmem((SUBS, stations), F32)
    totals = vmem((blocks * 3 * PACK // 2, LANES), F32)
    count = len(sizes)
    tables = call(
        lambda *refs: tables_kernel(count, *refs),
        [
            *products,
            vmem((2 * baselines, LANES), BF16),
            vmem((blocks * 3 * PACK // 2, 2 * baselines), BF16),
            seen,
            vmem(((2 * SUBS + 1) * SUBS, LANES), F32),
            vmem((2 * SUBS, LANES), F32),
            station,
            station,
        ],
        "v" * count + "shhhhhh",
        [wide, wide, wide, vmem((1, stations), F32), pltpu.SemaphoreType.DMA((6,))],
        limit=16,
        micros=1,
    )(
        *pieces,
        channel_index,
        first_station.reshape(tiles, LANES),
        second_station.reshape(tiles, LANES),
        gains,
        consensus,
        dual,
        penalty.reshape(1, stations),
    )
    summed = list(tables[:count])
    hot, mask, found, state, own, first, second = tables[count:]
    pieces, state = lax.optimization_barrier((pieces, state))
    near = [swap(piece, 1) for piece in pieces]
    far[0], state = lax.optimization_barrier((far[0], state))
    last = [[swap(array, 1) for array in far[0]]]
    (summed[0],) = call(more_kernel, [products[0]], "v" * (2 + len(far[0])), micros=0.001)(
        summed[0], near[0], *far[0]
    )
    far[1], last[0], found = lax.optimization_barrier((far[1], last[0], found))
    last.append([swap(array, 1) for array in far[1]])
    (summed[1],) = call(more_kernel, [products[1]], "v" * (2 + len(far[1])), micros=0.001)(
        summed[1], near[1], *far[1]
    )
    summed[0], partial = call(
        lambda *refs: piece_kernel(0, *refs),
        [products[0], totals],
        "v" * (4 + len(last[0])),
        [terms[0]],
        limit=16,
        micros=0.001,
    )(hot, mask, found, summed[0], *last[0])
    part = vmem((SUBS, LANES), F32)
    gain_part, combined, send = call(
        lambda *refs: sweeps_kernel((count, len(last[1])), *refs),
        [part, part, vmem((channels, 2 * SUBS, LANES), F32)],
        "v" * (10 + len(last[1])),
        [products[1], totals, *terms],
        limit=16,
    )(
        hot,
        mask,
        found,
        state,
        own,
        first,
        second,
        summed[0],
        partial,
        summed[1],
        *last[1],
    )
    parts = lax.all_to_all(send, "freq", 0, 0)
    outs = call(
        lambda *refs: fit_kernel(gram_cholesky(channels), *refs),
        [pltpu.HBM((SUBS, LANES), F32)] * 3,
        "vvvv",
        [part, part, pltpu.SemaphoreType.DMA((3,))],
    )(parts, own, gain_part, combined)
    return tuple(array[None] for array in outs)


def solution(mesh):
    placed = (
        P("freq", "tm", None, None),
        P("freq", "tm", None, None),
        P("freq", "tm", None),
        P("freq", None, None),
        P("freq", None, None),
        P("freq", None, None),
        P(),
        P("freq"),
        P(),
        P(),
    )
    return jax.shard_map(
        shards,
        mesh=mesh,
        in_specs=placed,
        out_specs=(P("freq", None, "tm"), P("freq", None, "tm"), P("freq", None, "tm")),
        check_vma=False,
    )
```

```python
import jax
import jax.numpy as jnp
import numpy as np
from jax import lax
from jax.experimental import pallas as pl
from jax.experimental.pallas import tpu as pltpu
from jax.sharding import PartitionSpec as P

SWEEPS = 2
LANES = 128
SUBS = 8
PRODS = 48
TERMS = 24
SENT = 9
PACK = 16
F32 = jnp.float32
BF16 = jnp.bfloat16


def mul_conj(a, b):
    return (a[0] * b[0] + a[1] * b[1], a[1] * b[0] - a[0] * b[1])


def copy_in(pairs, sem):
    copies = [
        pltpu.make_async_copy(source, target, sem.at[index])
        for index, (source, target) in enumerate(pairs)
    ]
    for copy in copies:
        copy.start()
    return copies


def widen_kernel(vis_hbm, model_hbm, keep_hbm, *refs):
    vis_ref, model_ref, keep_ref, sem = refs[-4:]
    copies = copy_in(
        [(vis_hbm, vis_ref), (keep_hbm, keep_ref), (model_hbm, model_ref)], sem
    )
    for copy in copies:
        copy.wait()
    start = 0
    for out_ref in refs[:-4]:
        tiles = out_ref.shape[0] // (2 * SUBS)
        for tile in range(tiles):
            lanes = pl.ds((start + tile) * LANES, LANES)
            out_ref[pl.ds(tile * SUBS, SUBS), :] = vis_ref[:, lanes].astype(F32)
            out_ref[pl.ds((tiles + tile) * SUBS, SUBS), :] = model_ref[:, lanes].astype(
                F32
            ) * keep_ref[:, lanes].astype(F32)
        start += tiles


def slot_products(slot_ref, group, tiles):
    def load(part, component):
        start = (part * tiles + group * SUBS) * SUBS + component
        return slot_ref[pl.ds(start, SUBS, stride=SUBS), :]

    seen = [(load(0, 2 * e), load(0, 2 * e + 1)) for e in range(4)]
    model = [(load(1, 2 * e), load(1, 2 * e + 1)) for e in range(4)]
    rows = []
    for v in range(4):
        for m in range(4):
            rows.extend(mul_conj(seen[v], model[m]))
    rows.extend(entry[0] * entry[0] + entry[1] * entry[1] for entry in model)
    for left, right in ((0, 1), (2, 3), (0, 2), (1, 3)):
        rows.extend(mul_conj(model[left], model[right]))
    a = mul_conj(model[0], model[3])
    b = mul_conj(model[1], model[2])
    rows.extend((a[0] + b[0], a[0] - b[0], a[1] + b[1], a[1] - b[1]))
    return rows


def add_products(slot_refs, before_ref, out_ref, group):
    tiles = slot_refs[0].shape[0] // (2 * SUBS)
    at = pl.ds(group * SUBS, SUBS)
    total = None
    for slot_ref in slot_refs:
        rows = slot_products(slot_ref, group, tiles)
        total = rows if total is None else [x + y for x, y in zip(total, rows)]
    for index, row in enumerate(total):
        if before_ref is not None:
            row = row + before_ref[index, at, :]
            total[index] = row
        out_ref[index, at, :] = row
    return total


def gain_tables(gains):
    return [
        [jnp.broadcast_to(gain[h : h + 1], (SUBS, LANES)) for h in range(gain.shape[0])]
        for gain in gains
    ]


def gather_gains(tables, station_ref, group):
    station = station_ref[pl.ds(group * SUBS, SUBS), :]
    offset, block = station & (LANES - 1), station >> 7
    values = []
    for table in tables:
        value = None
        for h, row in enumerate(table):
            found = jnp.take_along_axis(row, offset, axis=1, mode="promise_in_bounds")
            value = found if value is None else jnp.where(block == h, found, value)
        values.append(value)
    return values


def tables_kernel(count, *refs):
    slot_refs, channel_ref = refs[:count], refs[count]
    station_hbms, array_hbms = refs[count + 1 : count + 3], refs[count + 3 : count + 7]
    prod_refs = refs[count + 7 : 2 * count + 7]
    outs = refs[2 * count + 7 : -5]
    hot_ref, mask_ref, seen_ref, state_ref, own_ref, first_ref, second_ref = outs
    gains_ref, consensus_ref, dual_ref, penalty_ref, sem = refs[-5:]
    station_refs = (first_ref, second_ref)
    copies = copy_in(
        list(
            zip(
                station_hbms + array_hbms,
                station_refs + (gains_ref, consensus_ref, dual_ref, penalty_ref),
            )
        ),
        sem,
    )
    tiles = first_ref.shape[0]
    for slot_ref, prod_ref in zip(slot_refs, prod_refs, strict=True):
        for group in range(prod_ref.shape[1] // SUBS):
            add_products([slot_ref], None, prod_ref, group)
    for copy in copies:
        copy.wait()
    blocks = gains_ref.shape[1] // LANES
    for h in range(blocks):
        lanes = pl.ds(h * LANES, LANES)
        penalty = penalty_ref[:, lanes]
        gain = gains_ref[:, lanes]
        target = penalty * (consensus_ref[:, lanes] - dual_ref[:, lanes])
        for j in range(SUBS):
            state_ref[pl.ds(j * SUBS + h, 1), :] = gain[j : j + 1]
            state_ref[pl.ds((SUBS + j) * SUBS + h, 1), :] = target[j : j + 1]
        state_ref[pl.ds(2 * SUBS * SUBS + h, 1), :] = penalty
    gains = [state_ref[pl.ds(j * SUBS, blocks), :] for j in range(SUBS)]
    tables = gain_tables(gains)
    for part, station_ref in enumerate(station_refs):
        for group in range(tiles // SUBS):
            for j, value in enumerate(gather_gains(tables, station_ref, group)):
                seen_ref[part, j, pl.ds(group * SUBS, SUBS), :] = value
    place = lax.axis_index("tm")
    own_ref[:SUBS, :] = dual_ref[:, pl.ds(pl.multiple_of(place * LANES, LANES), LANES)]
    own_ref[SUBS:, :] = jnp.full((SUBS, LANES), channel_ref[0].astype(F32))
    row = lax.broadcasted_iota(jnp.int32, (LANES, LANES), 0)
    lower = lax.broadcasted_iota(jnp.int32, (PACK, LANES), 0) >= SUBS
    for part, station_ref in enumerate(station_refs):
        for tile in range(tiles):
            station = station_ref[pl.ds(tile, 1), :]
            offset, block = station & (LANES - 1), station >> 7
            lanes = pl.ds((part * tiles + tile) * LANES, LANES)
            hot_ref[lanes, :] = jnp.where(row == offset, 1.0, 0.0).T.astype(BF16)
            wide = jnp.broadcast_to(block, (PACK, LANES))
            for h in range(blocks):
                mask_ref[pl.ds(h * PACK, PACK), lanes] = jnp.where(wide == h, 1.0, 0.0).astype(
                    BF16
                )
            for pair in range(blocks // 2):
                mine = jnp.where(lower, 2 * pair + 1, 2 * pair)
                mask_ref[pl.ds((blocks + pair) * PACK, PACK), lanes] = jnp.where(
                    wide == mine, 1.0, 0.0
                ).astype(BF16)


def more_kernel(before_ref, *refs):
    for group in range(before_ref.shape[1] // SUBS):
        add_products(refs[:-1], before_ref, refs[-1], group)


def gram(gain):
    entry = [(gain[2 * e], gain[2 * e + 1]) for e in range(4)]
    h00 = sum(part * part for part in entry[0] + entry[2])
    h11 = sum(part * part for part in entry[1] + entry[3])
    top = mul_conj(entry[1], entry[0])
    low = mul_conj(entry[3], entry[2])
    return h00, h11, top[0] + low[0], top[1] + low[1]


def baseline_terms(prod, gain_second, gain_first):
    def num(gain, swap):
        out = []
        for i in range(2):
            for l in range(2):
                real = imag = None
                for j in range(2):
                    for k in range(2):
                        if swap:
                            index = 4 * (2 * j + i) + 2 * k + l
                        else:
                            index = 4 * (2 * i + j) + 2 * l + k
                        tr, ti = prod(2 * index), prod(2 * index + 1)
                        gr, gi = gain[2 * (2 * j + k)], gain[2 * (2 * j + k) + 1]
                        if swap:
                            addr, addi = tr * gr + ti * gi, tr * gi - ti * gr
                        else:
                            addr, addi = tr * gr - ti * gi, tr * gi + ti * gr
                        real = addr if real is None else real + addr
                        imag = addi if imag is None else imag + addi
                out.extend((real, imag))
        return out

    n00, n01, n10, n11, pr, pi, qr, qi, rr, ri, sr, si, apr, amr, api, ami = (
        prod(32 + index) for index in range(16)
    )
    h00, h11, hr, hi = gram(gain_second)
    den_first = [
        n00 * h00 + n01 * h11 + 2.0 * (pr * hr - pi * hi),
        n10 * h00 + n11 * h11 + 2.0 * (qr * hr - qi * hi),
        rr * h00 + sr * h11 + apr * hr - ami * hi,
        ri * h00 + si * h11 + api * hr + amr * hi,
    ]
    h00, h11, hr, hi = gram(gain_first)
    den_second = [
        n00 * h00 + n10 * h11 + 2.0 * (rr * hr + ri * hi),
        n01 * h00 + n11 * h11 + 2.0 * (sr * hr + si * hi),
        pr * h00 + qr * h11 + apr * hr + api * hi,
        amr * hi - pi * h00 - qi * h11 - ami * hr,
    ]
    return num(gain_second, False) + den_first, num(gain_first, True) + den_second


def store_terms(prod, gain_first, gain_second, group, term_ref):
    start = group * SUBS * TERMS
    for part, rows in enumerate(baseline_terms(prod, gain_second, gain_first)):
        for j, row in enumerate(rows):
            where, apart = (start + j, 8) if j < 8 else (start + 8 + j, 4)
            high = row.astype(BF16).astype(F32)
            term_ref[part, pl.ds(where, SUBS, stride=TERMS), :] = high
            term_ref[part, pl.ds(where + apart, SUBS, stride=TERMS), :] = row - high


def scatter_terms(term_ref, hot_ref, mask_ref, group, start, part):
    rows = mask_ref.shape[0]
    tiles = hot_ref.shape[0] // (2 * LANES)
    blocks = rows * 2 // (3 * PACK)
    columns = []
    for tile in range(group * SUBS, (group + 1) * SUBS):
        lanes = pl.ds((part * tiles + start + tile) * LANES, LANES)
        num = term_ref[part, pl.ds(tile * TERMS, PACK), :].astype(BF16)
        den = term_ref[part, pl.ds(tile * TERMS + PACK, SUBS), :]
        den = jnp.concatenate([den, den], axis=0).astype(BF16)
        column = [
            mask_ref[pl.ds(h * PACK, PACK), lanes] * (num if h < blocks else den)
            for h in range(rows // PACK)
        ]
        columns.append(jnp.concatenate(column, axis=0))
    at = pl.ds((part * tiles + start + group * SUBS) * LANES, SUBS * LANES)
    return jnp.dot(
        jnp.concatenate(columns, axis=1), hot_ref[at, :], preferred_element_type=F32
    )


def piece_totals(prod_ref, gains_of, term_ref, hot_ref, mask_ref, start, total):
    for group in range(prod_ref.shape[1] // SUBS):
        at = pl.ds(group * SUBS, SUBS)
        gain_first, gain_second = (gains_of(part, start // SUBS + group) for part in range(2))
        store_terms(
            lambda index: prod_ref[index, at, :], gain_first, gain_second, group, term_ref
        )
        for part in range(2):
            add = scatter_terms(term_ref, hot_ref, mask_ref, group, start, part)
            total = add if total is None else total + add
    return total


def found_gains(found_ref):
    return lambda part, group: [
        found_ref[part, j, pl.ds(group * SUBS, SUBS), :] for j in range(SUBS)
    ]


def piece_kernel(start, hot_ref, mask_ref, found_ref, before_ref, *refs):
    slot_refs = refs[:-3]
    prod_ref, total_ref, term_ref = refs[-3:]
    for group in range(prod_ref.shape[1] // SUBS):
        add_products(slot_refs, before_ref, prod_ref, group)
    total_ref[...] = piece_totals(
        prod_ref, found_gains(found_ref), term_ref, hot_ref, mask_ref, start, None
    )


def solve(num, den, gain, target, penalty):
    rhs = [tuple(num[2 * e + part] + target[2 * e + part] for part in range(2)) for e in range(4)]
    r00, r11, r01 = den[0] + penalty, den[1] + penalty, (den[2], den[3])
    scale = 0.5 / (r00 * r11 - (r01[0] * r01[0] + r01[1] * r01[1]))
    out = []
    for i in range(2):
        a, b = rhs[2 * i], rhs[2 * i + 1]
        cross = mul_conj(b, r01)
        out.extend((a[part] * r11 - cross[part]) * scale for part in range(2))
        out.append((b[0] * r00 - (a[0] * r01[0] - a[1] * r01[1])) * scale)
        out.append((b[1] * r00 - (a[0] * r01[1] + a[1] * r01[0])) * scale)
    return [value + 0.5 * old for value, old in zip(out, gain)]


def own_place():
    return lax.axis_index("tm")


def sweeps_kernel(counts, *refs):
    pieces, slots = counts
    hot_ref, mask_ref, found_ref, state_ref, own_ref, first_ref, second_ref = refs[:7]
    prod_refs, partial_refs = refs[7 : 6 + pieces], refs[6 + pieces : 5 + 2 * pieces]
    before_ref, slot_refs = refs[5 + 2 * pieces], refs[6 + 2 * pieces : 6 + 2 * pieces + slots]
    gain_out_ref, sum_ref, send_ref, last_ref, total_ref = refs[6 + 2 * pieces + slots : -pieces]
    term_refs = refs[-pieces:]
    blocks = mask_ref.shape[0] * 2 // (3 * PACK)
    gains = [state_ref[pl.ds(j * SUBS, blocks), :] for j in range(SUBS)]
    target = [state_ref[pl.ds((SUBS + j) * SUBS, blocks), :] for j in range(SUBS)]
    penalty = state_ref[pl.ds(2 * SUBS * SUBS, blocks), :]
    for group in range(last_ref.shape[1] // SUBS):
        add_products(slot_refs, before_ref, last_ref, group)
    prod_refs = (*prod_refs, last_ref)
    for sweep in range(SWEEPS):
        total = None
        if sweep:
            tables = gain_tables(gains)

            def gains_of(part, group, tables=tables):
                return gather_gains(tables, (first_ref, second_ref)[part], group)

        else:
            gains_of = found_gains(found_ref)
            for partial_ref in partial_refs:
                total = partial_ref[...] if total is None else total + partial_ref[...]
        start = 0
        for prod_ref, term_ref in zip(prod_refs, term_refs, strict=True):
            if sweep or prod_ref is last_ref:
                total = piece_totals(
                    prod_ref, gains_of, term_ref, hot_ref, mask_ref, start, total
                )
            start += prod_ref.shape[1]
        total_ref[...] = total

        def rows(start, stride):
            return total_ref[pl.ds(start, blocks, stride=stride), :]

        num = [rows(j, PACK) + rows(SUBS + j, PACK) for j in range(SUBS)]
        den = [
            rows(blocks * PACK + j, SUBS) + rows(blocks * PACK + 4 + j, SUBS) for j in range(4)
        ]
        gains = solve(num, den, gains, target, penalty)
    for j in range(SUBS):
        total_ref[pl.ds(j, blocks, stride=SUBS), :] = gains[j]
    place = own_place()
    part = total_ref[pl.ds(pl.multiple_of(place * SUBS, SUBS), SUBS), :]
    gain_out_ref[...] = part
    combined, mark = part + own_ref[:SUBS, :], own_ref[SUBS:, :]
    sum_ref[...] = combined
    for channel in range(send_ref.shape[0] // SENT):
        send_ref[pl.ds(channel * SENT, SUBS), :] = combined
        send_ref[pl.ds(channel * SENT + SUBS, 1), :] = mark[:1]


def legendre(position):
    square = position * position
    return [None, position, 1.5 * square - 0.5, (2.5 * square - 1.5) * position]


def fit_kernel(gram_factor, parts_ref, own_ref, gain_ref, sum_ref, *refs):
    gain_hbm, consensus_hbm, dual_hbm, consensus_ref, dual_ref, sem = refs
    gain_copy = pltpu.make_async_copy(gain_ref, gain_hbm, sem.at[0])
    gain_copy.start()
    channels = parts_ref.shape[0] // SENT
    scale = float(channels) - 1.0

    def basis(channel):
        return legendre(2.0 * channel / scale - 1.0)

    moments = [None] * 4
    for channel in range(channels):
        value = parts_ref[pl.ds(channel * SENT, SUBS), :]
        for k, weight in enumerate(basis(parts_ref[pl.ds(channel * SENT + SUBS, 1), :])):
            add = value if weight is None else weight * value
            moments[k] = add if moments[k] is None else moments[k] + add
    middle = []
    for k in range(4):
        rest = moments[k]
        for earlier in range(k):
            rest = rest - gram_factor[k][earlier] * middle[earlier]
        middle.append(rest * (1.0 / gram_factor[k][k]))
    coeffs = [None] * 4
    for k in reversed(range(4)):
        rest = middle[k]
        for later in range(k + 1, 4):
            rest = rest - gram_factor[later][k] * coeffs[later]
        coeffs[k] = rest * (1.0 / gram_factor[k][k])
    own = basis(own_ref[SUBS:, :])
    fitted = coeffs[0]
    for k in range(1, 4):
        fitted = fitted + own[k] * coeffs[k]
    consensus_ref[...] = fitted
    dual_ref[...] = sum_ref[...] - fitted
    consensus_copy = pltpu.make_async_copy(consensus_ref, consensus_hbm, sem.at[1])
    dual_copy = pltpu.make_async_copy(dual_ref, dual_hbm, sem.at[2])
    consensus_copy.start()
    dual_copy.start()
    gain_copy.wait()
    consensus_copy.wait()
    dual_copy.wait()


def gram_cholesky(channels):
    x = 2.0 * np.arange(channels, dtype=np.float64) / (channels - 1.0) - 1.0
    basis = np.stack([np.ones_like(x), x, 1.5 * x * x - 0.5, (2.5 * x * x - 1.5) * x], -1)
    factor = np.linalg.cholesky(basis.T @ basis)
    return [[float(value) for value in row] for row in factor]


SPACES = {"s": pltpu.SMEM, "v": pltpu.VMEM, "h": pltpu.HBM}


def call(kernel, shapes, spaces, scratch=(), limit=8, micros=0):
    cost = pl.CostEstimate(
        flops=int(micros * 1.0e9), transcendentals=0, bytes_accessed=int(micros * 3.0e6)
    )
    run = pl.pallas_call(
        kernel,
        out_shape=shapes,
        in_specs=[pl.BlockSpec(memory_space=SPACES[space]) for space in spaces],
        out_specs=[pl.BlockSpec(memory_space=shape.memory_space) for shape in shapes],
        scratch_shapes=list(scratch),
        compiler_params=pltpu.CompilerParams(vmem_limit_bytes=limit << 20),
        cost_estimate=cost if micros else None,
    )

    def placed(*args):
        return run(
            *(
                arg if space == "s" else pltpu.with_memory_space_constraint(arg, SPACES[space])
                for arg, space in zip(args, spaces, strict=True)
            )
        )

    return placed


def shards(
    visibility,
    model_visibility,
    keep_mask,
    gains_in,
    consensus_in,
    dual_in,
    penalty,
    channel_index,
    first_station,
    second_station,
):
    baselines = visibility.shape[3]
    stations = gains_in.shape[2]
    slots = lax.axis_size("tm")
    channels = lax.axis_size("freq")
    tiles = baselines // LANES
    blocks = stations // LANES
    assert blocks == slots and blocks % 2 == 0 and channel_index.shape == (1,)
    vmem = pltpu.VMEM

    def swap(array, step):
        return lax.ppermute(array, "tm", [(i, i ^ step) for i in range(slots)])

    sizes = [tiles // 2, tiles // 2]
    pieces = call(
        widen_kernel,
        [vmem((2 * size * SUBS, LANES), F32) for size in sizes],
        "hhh",
        [
            vmem((SUBS, baselines), BF16),
            vmem((SUBS, baselines), BF16),
            vmem((1, baselines), jnp.int32),
            pltpu.SemaphoreType.DMA((3,)),
        ],
    )(
        visibility.reshape(SUBS, baselines),
        model_visibility.reshape(SUBS, baselines),
        keep_mask.reshape(1, baselines),
    )
    far = []
    for piece in pieces:
        got = []
        step = slots // 2
        while step > 1:
            got += [swap(array, step) for array in [piece, *got]]
            step //= 2
        far.append(got)
    gains, consensus, dual = (
        array.reshape(SUBS, stations) for array in (gains_in, consensus_in, dual_in)
    )
    products = [vmem((PRODS, size, LANES), F32) for size in sizes]
    terms = [vmem((2, size * TERMS, LANES), F32) for size in sizes]
    seen = vmem((2, SUBS, tiles, LANES), F32)
    station = vmem((tiles, LANES), jnp.int32)
    wide = vmem((SUBS, stations), F32)
    totals = vmem((blocks * 3 * PACK // 2, LANES), F32)
    count = len(sizes)
    tables = call(
        lambda *refs: tables_kernel(count, *refs),
        [
            *products,
            vmem((2 * baselines, LANES), BF16),
            vmem((blocks * 3 * PACK // 2, 2 * baselines), BF16),
            seen,
            vmem(((2 * SUBS + 1) * SUBS, LANES), F32),
            vmem((2 * SUBS, LANES), F32),
            station,
            station,
        ],
        "v" * count + "shhhhhh",
        [wide, wide, wide, vmem((1, stations), F32), pltpu.SemaphoreType.DMA((6,))],
        limit=16,
        micros=1,
    )(
        *pieces,
        channel_index,
        first_station.reshape(tiles, LANES),
        second_station.reshape(tiles, LANES),
        gains,
        consensus,
        dual,
        penalty.reshape(1, stations),
    )
    summed = list(tables[:count])
    hot, mask, found, state, own, first, second = tables[count:]
    pieces, state = lax.optimization_barrier((pieces, state))
    near = [swap(piece, 1) for piece in pieces]
    far[0], state = lax.optimization_barrier((far[0], state))
    last = [[swap(array, 1) for array in far[0]]]
    (summed[0],) = call(more_kernel, [products[0]], "v" * (2 + len(far[0])), micros=0.001)(
        summed[0], near[0], *far[0]
    )
    far[1], last[0], found = lax.optimization_barrier((far[1], last[0], found))
    last.append([swap(array, 1) for array in far[1]])
    (summed[1],) = call(more_kernel, [products[1]], "v" * (2 + len(far[1])), micros=0.001)(
        summed[1], near[1], *far[1]
    )
    summed[0], partial = call(
        lambda *refs: piece_kernel(0, *refs),
        [products[0], totals],
        "v" * (4 + len(last[0])),
        [terms[0]],
        limit=16,
        micros=0.001,
    )(hot, mask, found, summed[0], *last[0])
    part = vmem((SUBS, LANES), F32)
    gain_part, combined, send = call(
        lambda *refs: sweeps_kernel((count, len(last[1])), *refs),
        [part, part, vmem((channels * SENT, LANES), F32)],
        "v" * (10 + len(last[1])),
        [products[1], totals, *terms],
        limit=16,
    )(
        hot,
        mask,
        found,
        state,
        own,
        first,
        second,
        summed[0],
        partial,
        summed[1],
        *last[1],
    )
    parts = lax.all_to_all(send.reshape(channels, 1, SENT * LANES), "freq", 0, 0)
    parts = parts.reshape(channels * SENT, LANES)
    outs = call(
        lambda *refs: fit_kernel(gram_cholesky(channels), *refs),
        [pltpu.HBM((SUBS, LANES), F32)] * 3,
        "vvvv",
        [part, part, pltpu.SemaphoreType.DMA((3,))],
    )(parts, own, gain_part, combined)
    return tuple(array[None] for array in outs)


def solution(mesh):
    placed = (
        P("freq", "tm", None, None),
        P("freq", "tm", None, None),
        P("freq", "tm", None),
        P("freq", None, None),
        P("freq", None, None),
        P("freq", None, None),
        P(),
        P("freq"),
        P(),
        P(),
    )
    return jax.shard_map(
        shards,
        mesh=mesh,
        in_specs=placed,
        out_specs=(P("freq", None, "tm"), P("freq", None, "tm"), P("freq", None, "tm")),
        check_vma=False,
    )
```

```python
import jax
import jax.numpy as jnp
import numpy as np
from jax import lax
from jax.experimental import pallas as pl
from jax.experimental.pallas import tpu as pltpu
from jax.sharding import PartitionSpec as P

SWEEPS = 2
LANES = 128
SUBS = 8
PRODS = 48
TERMS = 24
SENT = 9
PACK = 16
F32 = jnp.float32
BF16 = jnp.bfloat16


def mul_conj(a, b):
    return (a[0] * b[0] + a[1] * b[1], a[1] * b[0] - a[0] * b[1])


def copy_in(pairs, sem):
    copies = [
        pltpu.make_async_copy(source, target, sem.at[index])
        for index, (source, target) in enumerate(pairs)
    ]
    for copy in copies:
        copy.start()
    return copies


def widen_kernel(start, vis_hbm, model_hbm, keep_hbm, out_ref, *refs):
    sem = refs[-1]
    lanes = pl.ds(start * LANES, refs[0].shape[1])
    sources = (hbm.at[:, lanes] for hbm in (vis_hbm, model_hbm, keep_hbm))
    for copy in copy_in(list(zip(sources, refs[:-1], strict=True)), sem):
        copy.wait()
    vis_ref, model_ref, keep_ref = refs[:-1]
    tiles = out_ref.shape[0] // (2 * SUBS)
    for tile in range(tiles):
        lanes = pl.ds(tile * LANES, LANES)
        out_ref[pl.ds(tile * SUBS, SUBS), :] = vis_ref[:, lanes].astype(F32)
        out_ref[pl.ds((tiles + tile) * SUBS, SUBS), :] = model_ref[:, lanes].astype(
            F32
        ) * keep_ref[:, lanes].astype(F32)


def slot_products(slot_ref, group, tiles):
    def load(part, component):
        start = (part * tiles + group * SUBS) * SUBS + component
        return slot_ref[pl.ds(start, SUBS, stride=SUBS), :]

    seen = [(load(0, 2 * e), load(0, 2 * e + 1)) for e in range(4)]
    model = [(load(1, 2 * e), load(1, 2 * e + 1)) for e in range(4)]
    rows = []
    for v in range(4):
        for m in range(4):
            rows.extend(mul_conj(seen[v], model[m]))
    rows.extend(entry[0] * entry[0] + entry[1] * entry[1] for entry in model)
    for left, right in ((0, 1), (2, 3), (0, 2), (1, 3)):
        rows.extend(mul_conj(model[left], model[right]))
    a = mul_conj(model[0], model[3])
    b = mul_conj(model[1], model[2])
    rows.extend((a[0] + b[0], a[0] - b[0], a[1] + b[1], a[1] - b[1]))
    return rows


def add_products(slot_refs, before_ref, out_ref, group):
    tiles = slot_refs[0].shape[0] // (2 * SUBS)
    at = pl.ds(group * SUBS, SUBS)
    total = None
    for slot_ref in slot_refs:
        rows = slot_products(slot_ref, group, tiles)
        total = rows if total is None else [x + y for x, y in zip(total, rows)]
    for index, row in enumerate(total):
        if before_ref is not None:
            row = row + before_ref[index, at, :]
            total[index] = row
        out_ref[index, at, :] = row
    return total


def gain_tables(gains):
    return [
        [jnp.broadcast_to(gain[h : h + 1], (SUBS, LANES)) for h in range(gain.shape[0])]
        for gain in gains
    ]


def gather_gains(tables, station_ref, group):
    station = station_ref[pl.ds(group * SUBS, SUBS), :]
    offset, block = station & (LANES - 1), station >> 7
    values = []
    for table in tables:
        value = None
        for h, row in enumerate(table):
            found = jnp.take_along_axis(row, offset, axis=1, mode="promise_in_bounds")
            value = found if value is None else jnp.where(block == h, found, value)
        values.append(value)
    return values


def tables_kernel(count, *refs):
    slot_refs, channel_ref = refs[:count], refs[count]
    station_hbms, array_hbms = refs[count + 1 : count + 3], refs[count + 3 : count + 7]
    prod_refs = refs[count + 7 : 2 * count + 7]
    outs = refs[2 * count + 7 : -5]
    hot_ref, mask_ref, seen_ref, state_ref, own_ref, first_ref, second_ref = outs
    gains_ref, consensus_ref, dual_ref, penalty_ref, sem = refs[-5:]
    station_refs = (first_ref, second_ref)
    copies = copy_in(
        list(
            zip(
                station_hbms + array_hbms,
                station_refs + (gains_ref, consensus_ref, dual_ref, penalty_ref),
            )
        ),
        sem,
    )
    tiles = first_ref.shape[0]
    for slot_ref, prod_ref in zip(slot_refs, prod_refs, strict=True):
        for group in range(prod_ref.shape[1] // SUBS):
            add_products([slot_ref], None, prod_ref, group)
    for copy in copies:
        copy.wait()
    blocks = gains_ref.shape[1] // LANES
    for h in range(blocks):
        lanes = pl.ds(h * LANES, LANES)
        penalty = penalty_ref[:, lanes]
        gain = gains_ref[:, lanes]
        target = penalty * (consensus_ref[:, lanes] - dual_ref[:, lanes])
        for j in range(SUBS):
            state_ref[pl.ds(j * SUBS + h, 1), :] = gain[j : j + 1]
            state_ref[pl.ds((SUBS + j) * SUBS + h, 1), :] = target[j : j + 1]
        state_ref[pl.ds(2 * SUBS * SUBS + h, 1), :] = penalty
    gains = [state_ref[pl.ds(j * SUBS, blocks), :] for j in range(SUBS)]
    tables = gain_tables(gains)
    for part, station_ref in enumerate(station_refs):
        for group in range(tiles // SUBS):
            for j, value in enumerate(gather_gains(tables, station_ref, group)):
                seen_ref[part, j, pl.ds(group * SUBS, SUBS), :] = value
    place = lax.axis_index("tm")
    own_ref[:SUBS, :] = dual_ref[:, pl.ds(pl.multiple_of(place * LANES, LANES), LANES)]
    own_ref[SUBS:, :] = jnp.full((SUBS, LANES), channel_ref[0].astype(F32))
    row = lax.broadcasted_iota(jnp.int32, (LANES, LANES), 0)
    lower = lax.broadcasted_iota(jnp.int32, (PACK, LANES), 0) >= SUBS
    for part, station_ref in enumerate(station_refs):
        for tile in range(tiles):
            station = station_ref[pl.ds(tile, 1), :]
            offset, block = station & (LANES - 1), station >> 7
            lanes = pl.ds((part * tiles + tile) * LANES, LANES)
            hot_ref[lanes, :] = jnp.where(row == offset, 1.0, 0.0).T.astype(BF16)
            wide = jnp.broadcast_to(block, (PACK, LANES))
            for h in range(blocks):
                mask_ref[pl.ds(h * PACK, PACK), lanes] = jnp.where(wide == h, 1.0, 0.0).astype(
                    BF16
                )
            for pair in range(blocks // 2):
                mine = jnp.where(lower, 2 * pair + 1, 2 * pair)
                mask_ref[pl.ds((blocks + pair) * PACK, PACK), lanes] = jnp.where(
                    wide == mine, 1.0, 0.0
                ).astype(BF16)


def more_kernel(before_ref, *refs):
    for group in range(before_ref.shape[1] // SUBS):
        add_products(refs[:-1], before_ref, refs[-1], group)


def gram(gain):
    entry = [(gain[2 * e], gain[2 * e + 1]) for e in range(4)]
    h00 = sum(part * part for part in entry[0] + entry[2])
    h11 = sum(part * part for part in entry[1] + entry[3])
    top = mul_conj(entry[1], entry[0])
    low = mul_conj(entry[3], entry[2])
    return h00, h11, top[0] + low[0], top[1] + low[1]


def baseline_terms(prod, gain_second, gain_first):
    def num(gain, swap):
        out = []
        for i in range(2):
            for l in range(2):
                real = imag = None
                for j in range(2):
                    for k in range(2):
                        if swap:
                            index = 4 * (2 * j + i) + 2 * k + l
                        else:
                            index = 4 * (2 * i + j) + 2 * l + k
                        tr, ti = prod(2 * index), prod(2 * index + 1)
                        gr, gi = gain[2 * (2 * j + k)], gain[2 * (2 * j + k) + 1]
                        if swap:
                            addr, addi = tr * gr + ti * gi, tr * gi - ti * gr
                        else:
                            addr, addi = tr * gr - ti * gi, tr * gi + ti * gr
                        real = addr if real is None else real + addr
                        imag = addi if imag is None else imag + addi
                out.extend((real, imag))
        return out

    n00, n01, n10, n11, pr, pi, qr, qi, rr, ri, sr, si, apr, amr, api, ami = (
        prod(32 + index) for index in range(16)
    )
    h00, h11, hr, hi = gram(gain_second)
    den_first = [
        n00 * h00 + n01 * h11 + 2.0 * (pr * hr - pi * hi),
        n10 * h00 + n11 * h11 + 2.0 * (qr * hr - qi * hi),
        rr * h00 + sr * h11 + apr * hr - ami * hi,
        ri * h00 + si * h11 + api * hr + amr * hi,
    ]
    h00, h11, hr, hi = gram(gain_first)
    den_second = [
        n00 * h00 + n10 * h11 + 2.0 * (rr * hr + ri * hi),
        n01 * h00 + n11 * h11 + 2.0 * (sr * hr + si * hi),
        pr * h00 + qr * h11 + apr * hr + api * hi,
        amr * hi - pi * h00 - qi * h11 - ami * hr,
    ]
    return num(gain_second, False) + den_first, num(gain_first, True) + den_second


def store_terms(prod, gain_first, gain_second, group, term_ref):
    start = group * SUBS * TERMS
    for part, rows in enumerate(baseline_terms(prod, gain_second, gain_first)):
        for j, row in enumerate(rows):
            where, apart = (start + j, 8) if j < 8 else (start + 8 + j, 4)
            high = row.astype(BF16).astype(F32)
            term_ref[part, pl.ds(where, SUBS, stride=TERMS), :] = high
            term_ref[part, pl.ds(where + apart, SUBS, stride=TERMS), :] = row - high


def scatter_terms(term_ref, hot_ref, mask_ref, group, start, part):
    rows = mask_ref.shape[0]
    tiles = hot_ref.shape[0] // (2 * LANES)
    blocks = rows * 2 // (3 * PACK)
    columns = []
    for tile in range(group * SUBS, (group + 1) * SUBS):
        lanes = pl.ds((part * tiles + start + tile) * LANES, LANES)
        num = term_ref[part, pl.ds(tile * TERMS, PACK), :].astype(BF16)
        den = term_ref[part, pl.ds(tile * TERMS + PACK, SUBS), :]
        den = jnp.concatenate([den, den], axis=0).astype(BF16)
        column = [
            mask_ref[pl.ds(h * PACK, PACK), lanes] * (num if h < blocks else den)
            for h in range(rows // PACK)
        ]
        columns.append(jnp.concatenate(column, axis=0))
    at = pl.ds((part * tiles + start + group * SUBS) * LANES, SUBS * LANES)
    return jnp.dot(
        jnp.concatenate(columns, axis=1), hot_ref[at, :], preferred_element_type=F32
    )


def piece_totals(prod_ref, gains_of, term_ref, hot_ref, mask_ref, start, total):
    for group in range(prod_ref.shape[1] // SUBS):
        at = pl.ds(group * SUBS, SUBS)
        gain_first, gain_second = (gains_of(part, start // SUBS + group) for part in range(2))
        store_terms(
            lambda index: prod_ref[index, at, :], gain_first, gain_second, group, term_ref
        )
        for part in range(2):
            add = scatter_terms(term_ref, hot_ref, mask_ref, group, start, part)
            total = add if total is None else total + add
    return total


def found_gains(found_ref):
    return lambda part, group: [
        found_ref[part, j, pl.ds(group * SUBS, SUBS), :] for j in range(SUBS)
    ]


def piece_kernel(start, hot_ref, mask_ref, found_ref, before_ref, *refs):
    slot_refs = refs[:-3]
    prod_ref, total_ref, term_ref = refs[-3:]
    for group in range(prod_ref.shape[1] // SUBS):
        add_products(slot_refs, before_ref, prod_ref, group)
    total_ref[...] = piece_totals(
        prod_ref, found_gains(found_ref), term_ref, hot_ref, mask_ref, start, None
    )


def solve(num, den, gain, target, penalty):
    rhs = [tuple(num[2 * e + part] + target[2 * e + part] for part in range(2)) for e in range(4)]
    r00, r11, r01 = den[0] + penalty, den[1] + penalty, (den[2], den[3])
    scale = 0.5 / (r00 * r11 - (r01[0] * r01[0] + r01[1] * r01[1]))
    out = []
    for i in range(2):
        a, b = rhs[2 * i], rhs[2 * i + 1]
        cross = mul_conj(b, r01)
        out.extend((a[part] * r11 - cross[part]) * scale for part in range(2))
        out.append((b[0] * r00 - (a[0] * r01[0] - a[1] * r01[1])) * scale)
        out.append((b[1] * r00 - (a[0] * r01[1] + a[1] * r01[0])) * scale)
    return [value + 0.5 * old for value, old in zip(out, gain)]


def own_place():
    return lax.axis_index("tm")


def sweeps_kernel(counts, *refs):
    pieces, slots = counts
    hot_ref, mask_ref, found_ref, state_ref, own_ref, first_ref, second_ref = refs[:7]
    prod_refs, partial_refs = refs[7 : 6 + pieces], refs[6 + pieces : 5 + 2 * pieces]
    before_ref, slot_refs = refs[5 + 2 * pieces], refs[6 + 2 * pieces : 6 + 2 * pieces + slots]
    gain_out_ref, sum_ref, send_ref, last_ref, total_ref = refs[6 + 2 * pieces + slots : -pieces]
    term_refs = refs[-pieces:]
    blocks = mask_ref.shape[0] * 2 // (3 * PACK)
    gains = [state_ref[pl.ds(j * SUBS, blocks), :] for j in range(SUBS)]
    target = [state_ref[pl.ds((SUBS + j) * SUBS, blocks), :] for j in range(SUBS)]
    penalty = state_ref[pl.ds(2 * SUBS * SUBS, blocks), :]
    for group in range(last_ref.shape[1] // SUBS):
        add_products(slot_refs, before_ref, last_ref, group)
    prod_refs = (*prod_refs, last_ref)
    for sweep in range(SWEEPS):
        total = None
        if sweep:
            tables = gain_tables(gains)

            def gains_of(part, group, tables=tables):
                return gather_gains(tables, (first_ref, second_ref)[part], group)

        else:
            gains_of = found_gains(found_ref)
            for partial_ref in partial_refs:
                total = partial_ref[...] if total is None else total + partial_ref[...]
        start = 0
        for prod_ref, term_ref in zip(prod_refs, term_refs, strict=True):
            if sweep or prod_ref is last_ref:
                total = piece_totals(
                    prod_ref, gains_of, term_ref, hot_ref, mask_ref, start, total
                )
            start += prod_ref.shape[1]
        total_ref[...] = total

        def rows(start, stride):
            return total_ref[pl.ds(start, blocks, stride=stride), :]

        num = [rows(j, PACK) + rows(SUBS + j, PACK) for j in range(SUBS)]
        den = [
            rows(blocks * PACK + j, SUBS) + rows(blocks * PACK + 4 + j, SUBS) for j in range(4)
        ]
        gains = solve(num, den, gains, target, penalty)
    for j in range(SUBS):
        total_ref[pl.ds(j, blocks, stride=SUBS), :] = gains[j]
    place = own_place()
    part = total_ref[pl.ds(pl.multiple_of(place * SUBS, SUBS), SUBS), :]
    gain_out_ref[...] = part
    combined, mark = part + own_ref[:SUBS, :], own_ref[SUBS:, :]
    sum_ref[...] = combined
    for channel in range(send_ref.shape[0] // SENT):
        send_ref[pl.ds(channel * SENT, SUBS), :] = combined
        send_ref[pl.ds(channel * SENT + SUBS, 1), :] = mark[:1]


def legendre(position):
    square = position * position
    return [None, position, 1.5 * square - 0.5, (2.5 * square - 1.5) * position]


def fit_kernel(gram_factor, parts_ref, own_ref, gain_ref, sum_ref, *refs):
    gain_hbm, consensus_hbm, dual_hbm, consensus_ref, dual_ref, sem = refs
    gain_copy = pltpu.make_async_copy(gain_ref, gain_hbm, sem.at[0])
    gain_copy.start()
    channels = parts_ref.shape[0] // SENT
    scale = float(channels) - 1.0

    def basis(channel):
        return legendre(2.0 * channel / scale - 1.0)

    moments = [None] * 4
    for channel in range(channels):
        value = parts_ref[pl.ds(channel * SENT, SUBS), :]
        for k, weight in enumerate(basis(parts_ref[pl.ds(channel * SENT + SUBS, 1), :])):
            add = value if weight is None else weight * value
            moments[k] = add if moments[k] is None else moments[k] + add
    middle = []
    for k in range(4):
        rest = moments[k]
        for earlier in range(k):
            rest = rest - gram_factor[k][earlier] * middle[earlier]
        middle.append(rest * (1.0 / gram_factor[k][k]))
    coeffs = [None] * 4
    for k in reversed(range(4)):
        rest = middle[k]
        for later in range(k + 1, 4):
            rest = rest - gram_factor[later][k] * coeffs[later]
        coeffs[k] = rest * (1.0 / gram_factor[k][k])
    own = basis(own_ref[SUBS:, :])
    fitted = coeffs[0]
    for k in range(1, 4):
        fitted = fitted + own[k] * coeffs[k]
    consensus_ref[...] = fitted
    dual_ref[...] = sum_ref[...] - fitted
    consensus_copy = pltpu.make_async_copy(consensus_ref, consensus_hbm, sem.at[1])
    dual_copy = pltpu.make_async_copy(dual_ref, dual_hbm, sem.at[2])
    consensus_copy.start()
    dual_copy.start()
    gain_copy.wait()
    consensus_copy.wait()
    dual_copy.wait()


def gram_cholesky(channels):
    x = 2.0 * np.arange(channels, dtype=np.float64) / (channels - 1.0) - 1.0
    basis = np.stack([np.ones_like(x), x, 1.5 * x * x - 0.5, (2.5 * x * x - 1.5) * x], -1)
    factor = np.linalg.cholesky(basis.T @ basis)
    return [[float(value) for value in row] for row in factor]


SPACES = {"s": pltpu.SMEM, "v": pltpu.VMEM, "h": pltpu.HBM}


def call(kernel, shapes, spaces, scratch=(), limit=8, micros=0):
    cost = pl.CostEstimate(
        flops=int(micros * 1.0e9), transcendentals=0, bytes_accessed=int(micros * 3.0e6)
    )
    run = pl.pallas_call(
        kernel,
        out_shape=shapes,
        in_specs=[pl.BlockSpec(memory_space=SPACES[space]) for space in spaces],
        out_specs=[pl.BlockSpec(memory_space=shape.memory_space) for shape in shapes],
        scratch_shapes=list(scratch),
        compiler_params=pltpu.CompilerParams(vmem_limit_bytes=limit << 20),
        cost_estimate=cost if micros else None,
    )

    def placed(*args):
        return run(
            *(
                arg if space == "s" else pltpu.with_memory_space_constraint(arg, SPACES[space])
                for arg, space in zip(args, spaces, strict=True)
            )
        )

    return placed


def shards(
    visibility,
    model_visibility,
    keep_mask,
    gains_in,
    consensus_in,
    dual_in,
    penalty,
    channel_index,
    first_station,
    second_station,
):
    baselines = visibility.shape[3]
    stations = gains_in.shape[2]
    slots = lax.axis_size("tm")
    channels = lax.axis_size("freq")
    tiles = baselines // LANES
    blocks = stations // LANES
    assert blocks == slots and blocks % 2 == 0 and channel_index.shape == (1,)
    vmem = pltpu.VMEM

    def swap(array, step):
        return lax.ppermute(array, "tm", [(i, i ^ step) for i in range(slots)])

    sizes = [tiles // 2, tiles // 2]
    pieces = []
    for index, size in enumerate(sizes):
        pieces += call(
            lambda *refs, start=sum(sizes[:index]): widen_kernel(start, *refs),
            [vmem((2 * size * SUBS, LANES), F32)],
            "hhh",
            [
                vmem((SUBS, size * LANES), BF16),
                vmem((SUBS, size * LANES), BF16),
                vmem((1, size * LANES), jnp.int32),
                pltpu.SemaphoreType.DMA((3,)),
            ],
            micros=0.001,
        )(
            visibility.reshape(SUBS, baselines),
            model_visibility.reshape(SUBS, baselines),
            keep_mask.reshape(1, baselines),
        )
    far = []
    for piece in pieces:
        got = []
        step = slots // 2
        while step > 1:
            got += [swap(array, step) for array in [piece, *got]]
            step //= 2
        far.append(got)
    gains, consensus, dual = (
        array.reshape(SUBS, stations) for array in (gains_in, consensus_in, dual_in)
    )
    products = [vmem((PRODS, size, LANES), F32) for size in sizes]
    terms = [vmem((2, size * TERMS, LANES), F32) for size in sizes]
    seen = vmem((2, SUBS, tiles, LANES), F32)
    station = vmem((tiles, LANES), jnp.int32)
    wide = vmem((SUBS, stations), F32)
    totals = vmem((blocks * 3 * PACK // 2, LANES), F32)
    count = len(sizes)
    tables = call(
        lambda *refs: tables_kernel(count, *refs),
        [
            *products,
            vmem((2 * baselines, LANES), BF16),
            vmem((blocks * 3 * PACK // 2, 2 * baselines), BF16),
            seen,
            vmem(((2 * SUBS + 1) * SUBS, LANES), F32),
            vmem((2 * SUBS, LANES), F32),
            station,
            station,
        ],
        "v" * count + "shhhhhh",
        [wide, wide, wide, vmem((1, stations), F32), pltpu.SemaphoreType.DMA((6,))],
        limit=16,
        micros=1,
    )(
        *pieces,
        channel_index,
        first_station.reshape(tiles, LANES),
        second_station.reshape(tiles, LANES),
        gains,
        consensus,
        dual,
        penalty.reshape(1, stations),
    )
    summed = list(tables[:count])
    hot, mask, found, state, own, first, second = tables[count:]
    pieces, state = lax.optimization_barrier((pieces, state))
    near = [swap(piece, 1) for piece in pieces]
    far[0], state = lax.optimization_barrier((far[0], state))
    last = [[swap(array, 1) for array in far[0]]]
    (summed[0],) = call(more_kernel, [products[0]], "v" * (2 + len(far[0])), micros=0.001)(
        summed[0], near[0], *far[0]
    )
    far[1], last[0], found = lax.optimization_barrier((far[1], last[0], found))
    last.append([swap(array, 1) for array in far[1]])
    (summed[1],) = call(more_kernel, [products[1]], "v" * (2 + len(far[1])), micros=0.001)(
        summed[1], near[1], *far[1]
    )
    summed[0], partial = call(
        lambda *refs: piece_kernel(0, *refs),
        [products[0], totals],
        "v" * (4 + len(last[0])),
        [terms[0]],
        limit=16,
        micros=0.001,
    )(hot, mask, found, summed[0], *last[0])
    part = vmem((SUBS, LANES), F32)
    gain_part, combined, send = call(
        lambda *refs: sweeps_kernel((count, len(last[1])), *refs),
        [part, part, vmem((channels * SENT, LANES), F32)],
        "v" * (10 + len(last[1])),
        [products[1], totals, *terms],
        limit=16,
    )(
        hot,
        mask,
        found,
        state,
        own,
        first,
        second,
        summed[0],
        partial,
        summed[1],
        *last[1],
    )
    parts = lax.all_to_all(send.reshape(channels, 1, SENT * LANES), "freq", 0, 0)
    parts = parts.reshape(channels * SENT, LANES)
    outs = call(
        lambda *refs: fit_kernel(gram_cholesky(channels), *refs),
        [pltpu.HBM((SUBS, LANES), F32)] * 3,
        "vvvv",
        [part, part, pltpu.SemaphoreType.DMA((3,))],
    )(parts, own, gain_part, combined)
    return tuple(array[None] for array in outs)


def solution(mesh):
    placed = (
        P("freq", "tm", None, None),
        P("freq", "tm", None, None),
        P("freq", "tm", None),
        P("freq", None, None),
        P("freq", None, None),
        P("freq", None, None),
        P(),
        P("freq"),
        P(),
        P(),
    )
    return jax.shard_map(
        shards,
        mesh=mesh,
        in_specs=placed,
        out_specs=(P("freq", None, "tm"), P("freq", None, "tm"), P("freq", None, "tm")),
        check_vma=False,
    )
```

```python
import jax
import jax.numpy as jnp
import numpy as np
from jax import lax
from jax.experimental import pallas as pl
from jax.experimental.pallas import tpu as pltpu
from jax.sharding import PartitionSpec as P

SWEEPS = 2
LANES = 128
SUBS = 8
PRODS = 48
TERMS = 24
SENT = 9
PACK = 16
F32 = jnp.float32
BF16 = jnp.bfloat16


def mul_conj(a, b):
    return (a[0] * b[0] + a[1] * b[1], a[1] * b[0] - a[0] * b[1])


def copy_in(pairs, sem):
    copies = [
        pltpu.make_async_copy(source, target, sem.at[index])
        for index, (source, target) in enumerate(pairs)
    ]
    for copy in copies:
        copy.start()
    return copies


def widen_kernel(start, vis_hbm, model_hbm, keep_hbm, out_ref, *refs):
    sem = refs[-1]
    lanes = pl.ds(start * LANES, refs[0].shape[1])
    sources = (hbm.at[:, lanes] for hbm in (vis_hbm, model_hbm, keep_hbm))
    for copy in copy_in(list(zip(sources, refs[:-1], strict=True)), sem):
        copy.wait()
    vis_ref, model_ref, keep_ref = refs[:-1]
    tiles = out_ref.shape[0] // (2 * SUBS)
    for tile in range(tiles):
        lanes = pl.ds(tile * LANES, LANES)
        out_ref[pl.ds(tile * SUBS, SUBS), :] = vis_ref[:, lanes].astype(F32)
        out_ref[pl.ds((tiles + tile) * SUBS, SUBS), :] = model_ref[:, lanes].astype(
            F32
        ) * keep_ref[:, lanes].astype(F32)


def slot_products(slot_ref, group, tiles):
    def load(part, component):
        start = (part * tiles + group * SUBS) * SUBS + component
        return slot_ref[pl.ds(start, SUBS, stride=SUBS), :]

    seen = [(load(0, 2 * e), load(0, 2 * e + 1)) for e in range(4)]
    model = [(load(1, 2 * e), load(1, 2 * e + 1)) for e in range(4)]
    rows = []
    for v in range(4):
        for m in range(4):
            rows.extend(mul_conj(seen[v], model[m]))
    rows.extend(entry[0] * entry[0] + entry[1] * entry[1] for entry in model)
    for left, right in ((0, 1), (2, 3), (0, 2), (1, 3)):
        rows.extend(mul_conj(model[left], model[right]))
    a = mul_conj(model[0], model[3])
    b = mul_conj(model[1], model[2])
    rows.extend((a[0] + b[0], a[0] - b[0], a[1] + b[1], a[1] - b[1]))
    return rows


def add_products(slot_refs, before_ref, out_ref, group):
    tiles = slot_refs[0].shape[0] // (2 * SUBS)
    at = pl.ds(group * SUBS, SUBS)
    total = None
    for slot_ref in slot_refs:
        rows = slot_products(slot_ref, group, tiles)
        total = rows if total is None else [x + y for x, y in zip(total, rows)]
    for index, row in enumerate(total):
        if before_ref is not None:
            row = row + before_ref[index, at, :]
            total[index] = row
        out_ref[index, at, :] = row
    return total


def gain_tables(gains):
    return [
        [jnp.broadcast_to(gain[h : h + 1], (SUBS, LANES)) for h in range(gain.shape[0])]
        for gain in gains
    ]


def gather_gains(tables, station_ref, group):
    station = station_ref[pl.ds(group * SUBS, SUBS), :]
    offset, block = station & (LANES - 1), station >> 7
    values = []
    for table in tables:
        value = None
        for h, row in enumerate(table):
            found = jnp.take_along_axis(row, offset, axis=1, mode="promise_in_bounds")
            value = found if value is None else jnp.where(block == h, found, value)
        values.append(value)
    return values


def tables_kernel(count, *refs):
    slot_refs, channel_ref = refs[:count], refs[count]
    station_hbms, array_hbms = refs[count + 1 : count + 3], refs[count + 3 : count + 7]
    outs = refs[count + 7 : -5]
    hot_ref, mask_ref, seen_ref, state_ref, own_ref, first_ref, second_ref = outs
    gains_ref, consensus_ref, dual_ref, penalty_ref, sem = refs[-5:]
    station_refs = (first_ref, second_ref)
    copies = copy_in(
        list(
            zip(
                station_hbms + array_hbms,
                station_refs + (gains_ref, consensus_ref, dual_ref, penalty_ref),
            )
        ),
        sem,
    )
    tiles = first_ref.shape[0]
    for copy in copies:
        copy.wait()
    blocks = gains_ref.shape[1] // LANES
    for h in range(blocks):
        lanes = pl.ds(h * LANES, LANES)
        penalty = penalty_ref[:, lanes]
        gain = gains_ref[:, lanes]
        target = penalty * (consensus_ref[:, lanes] - dual_ref[:, lanes])
        for j in range(SUBS):
            state_ref[pl.ds(j * SUBS + h, 1), :] = gain[j : j + 1]
            state_ref[pl.ds((SUBS + j) * SUBS + h, 1), :] = target[j : j + 1]
        state_ref[pl.ds(2 * SUBS * SUBS + h, 1), :] = penalty
    gains = [state_ref[pl.ds(j * SUBS, blocks), :] for j in range(SUBS)]
    tables = gain_tables(gains)
    for part, station_ref in enumerate(station_refs):
        for group in range(tiles // SUBS):
            for j, value in enumerate(gather_gains(tables, station_ref, group)):
                seen_ref[part, j, pl.ds(group * SUBS, SUBS), :] = value
    place = lax.axis_index("tm")
    own_ref[:SUBS, :] = dual_ref[:, pl.ds(pl.multiple_of(place * LANES, LANES), LANES)]
    own_ref[SUBS:, :] = jnp.full((SUBS, LANES), channel_ref[0].astype(F32))
    row = lax.broadcasted_iota(jnp.int32, (LANES, LANES), 0)
    lower = lax.broadcasted_iota(jnp.int32, (PACK, LANES), 0) >= SUBS
    for part, station_ref in enumerate(station_refs):
        for tile in range(tiles):
            station = station_ref[pl.ds(tile, 1), :]
            offset, block = station & (LANES - 1), station >> 7
            lanes = pl.ds((part * tiles + tile) * LANES, LANES)
            hot_ref[lanes, :] = jnp.where(row == offset, 1.0, 0.0).T.astype(BF16)
            wide = jnp.broadcast_to(block, (PACK, LANES))
            for h in range(blocks):
                mask_ref[pl.ds(h * PACK, PACK), lanes] = jnp.where(wide == h, 1.0, 0.0).astype(
                    BF16
                )
            for pair in range(blocks // 2):
                mine = jnp.where(lower, 2 * pair + 1, 2 * pair)
                mask_ref[pl.ds((blocks + pair) * PACK, PACK), lanes] = jnp.where(
                    wide == mine, 1.0, 0.0
                ).astype(BF16)


def more_kernel(*refs):
    for group in range(refs[-1].shape[1] // SUBS):
        add_products(refs[:-1], None, refs[-1], group)


def gram(gain):
    entry = [(gain[2 * e], gain[2 * e + 1]) for e in range(4)]
    h00 = sum(part * part for part in entry[0] + entry[2])
    h11 = sum(part * part for part in entry[1] + entry[3])
    top = mul_conj(entry[1], entry[0])
    low = mul_conj(entry[3], entry[2])
    return h00, h11, top[0] + low[0], top[1] + low[1]


def baseline_terms(prod, gain_second, gain_first):
    def num(gain, swap):
        out = []
        for i in range(2):
            for l in range(2):
                real = imag = None
                for j in range(2):
                    for k in range(2):
                        if swap:
                            index = 4 * (2 * j + i) + 2 * k + l
                        else:
                            index = 4 * (2 * i + j) + 2 * l + k
                        tr, ti = prod(2 * index), prod(2 * index + 1)
                        gr, gi = gain[2 * (2 * j + k)], gain[2 * (2 * j + k) + 1]
                        if swap:
                            addr, addi = tr * gr + ti * gi, tr * gi - ti * gr
                        else:
                            addr, addi = tr * gr - ti * gi, tr * gi + ti * gr
                        real = addr if real is None else real + addr
                        imag = addi if imag is None else imag + addi
                out.extend((real, imag))
        return out

    n00, n01, n10, n11, pr, pi, qr, qi, rr, ri, sr, si, apr, amr, api, ami = (
        prod(32 + index) for index in range(16)
    )
    h00, h11, hr, hi = gram(gain_second)
    den_first = [
        n00 * h00 + n01 * h11 + 2.0 * (pr * hr - pi * hi),
        n10 * h00 + n11 * h11 + 2.0 * (qr * hr - qi * hi),
        rr * h00 + sr * h11 + apr * hr - ami * hi,
        ri * h00 + si * h11 + api * hr + amr * hi,
    ]
    h00, h11, hr, hi = gram(gain_first)
    den_second = [
        n00 * h00 + n10 * h11 + 2.0 * (rr * hr + ri * hi),
        n01 * h00 + n11 * h11 + 2.0 * (sr * hr + si * hi),
        pr * h00 + qr * h11 + apr * hr + api * hi,
        amr * hi - pi * h00 - qi * h11 - ami * hr,
    ]
    return num(gain_second, False) + den_first, num(gain_first, True) + den_second


def store_terms(prod, gain_first, gain_second, group, term_ref):
    start = group * SUBS * TERMS
    for part, rows in enumerate(baseline_terms(prod, gain_second, gain_first)):
        for j, row in enumerate(rows):
            where, apart = (start + j, 8) if j < 8 else (start + 8 + j, 4)
            high = row.astype(BF16).astype(F32)
            term_ref[part, pl.ds(where, SUBS, stride=TERMS), :] = high
            term_ref[part, pl.ds(where + apart, SUBS, stride=TERMS), :] = row - high


def scatter_terms(term_ref, hot_ref, mask_ref, group, start, part):
    rows = mask_ref.shape[0]
    tiles = hot_ref.shape[0] // (2 * LANES)
    blocks = rows * 2 // (3 * PACK)
    columns = []
    for tile in range(group * SUBS, (group + 1) * SUBS):
        lanes = pl.ds((part * tiles + start + tile) * LANES, LANES)
        num = term_ref[part, pl.ds(tile * TERMS, PACK), :].astype(BF16)
        den = term_ref[part, pl.ds(tile * TERMS + PACK, SUBS), :]
        den = jnp.concatenate([den, den], axis=0).astype(BF16)
        column = [
            mask_ref[pl.ds(h * PACK, PACK), lanes] * (num if h < blocks else den)
            for h in range(rows // PACK)
        ]
        columns.append(jnp.concatenate(column, axis=0))
    at = pl.ds((part * tiles + start + group * SUBS) * LANES, SUBS * LANES)
    return jnp.dot(
        jnp.concatenate(columns, axis=1), hot_ref[at, :], preferred_element_type=F32
    )


def piece_totals(prod_ref, gains_of, term_ref, hot_ref, mask_ref, start, total):
    for group in range(prod_ref.shape[1] // SUBS):
        at = pl.ds(group * SUBS, SUBS)
        gain_first, gain_second = (gains_of(part, start // SUBS + group) for part in range(2))
        store_terms(
            lambda index: prod_ref[index, at, :], gain_first, gain_second, group, term_ref
        )
        for part in range(2):
            add = scatter_terms(term_ref, hot_ref, mask_ref, group, start, part)
            total = add if total is None else total + add
    return total


def found_gains(found_ref):
    return lambda part, group: [
        found_ref[part, j, pl.ds(group * SUBS, SUBS), :] for j in range(SUBS)
    ]


def piece_kernel(start, hot_ref, mask_ref, found_ref, before_ref, *refs):
    slot_refs = refs[:-3]
    prod_ref, total_ref, term_ref = refs[-3:]
    for group in range(prod_ref.shape[1] // SUBS):
        add_products(slot_refs, before_ref, prod_ref, group)
    total_ref[...] = piece_totals(
        prod_ref, found_gains(found_ref), term_ref, hot_ref, mask_ref, start, None
    )


def solve(num, den, gain, target, penalty):
    rhs = [tuple(num[2 * e + part] + target[2 * e + part] for part in range(2)) for e in range(4)]
    r00, r11, r01 = den[0] + penalty, den[1] + penalty, (den[2], den[3])
    scale = 0.5 / (r00 * r11 - (r01[0] * r01[0] + r01[1] * r01[1]))
    out = []
    for i in range(2):
        a, b = rhs[2 * i], rhs[2 * i + 1]
        cross = mul_conj(b, r01)
        out.extend((a[part] * r11 - cross[part]) * scale for part in range(2))
        out.append((b[0] * r00 - (a[0] * r01[0] - a[1] * r01[1])) * scale)
        out.append((b[1] * r00 - (a[0] * r01[1] + a[1] * r01[0])) * scale)
    return [value + 0.5 * old for value, old in zip(out, gain)]


def own_place():
    return lax.axis_index("tm")


def sweeps_kernel(counts, *refs):
    pieces, slots = counts
    hot_ref, mask_ref, found_ref, state_ref, own_ref, first_ref, second_ref = refs[:7]
    prod_refs, partial_refs = refs[7 : 6 + pieces], refs[6 + pieces : 5 + 2 * pieces]
    before_ref, slot_refs = refs[5 + 2 * pieces], refs[6 + 2 * pieces : 6 + 2 * pieces + slots]
    gain_out_ref, sum_ref, send_ref, last_ref, total_ref = refs[6 + 2 * pieces + slots : -pieces]
    term_refs = refs[-pieces:]
    blocks = mask_ref.shape[0] * 2 // (3 * PACK)
    gains = [state_ref[pl.ds(j * SUBS, blocks), :] for j in range(SUBS)]
    target = [state_ref[pl.ds((SUBS + j) * SUBS, blocks), :] for j in range(SUBS)]
    penalty = state_ref[pl.ds(2 * SUBS * SUBS, blocks), :]
    for group in range(last_ref.shape[1] // SUBS):
        add_products(slot_refs, before_ref, last_ref, group)
    prod_refs = (*prod_refs, last_ref)
    for sweep in range(SWEEPS):
        total = None
        if sweep:
            tables = gain_tables(gains)

            def gains_of(part, group, tables=tables):
                return gather_gains(tables, (first_ref, second_ref)[part], group)

        else:
            gains_of = found_gains(found_ref)
            for partial_ref in partial_refs:
                total = partial_ref[...] if total is None else total + partial_ref[...]
        start = 0
        for prod_ref, term_ref in zip(prod_refs, term_refs, strict=True):
            if sweep or prod_ref is last_ref:
                total = piece_totals(
                    prod_ref, gains_of, term_ref, hot_ref, mask_ref, start, total
                )
            start += prod_ref.shape[1]
        total_ref[...] = total

        def rows(start, stride):
            return total_ref[pl.ds(start, blocks, stride=stride), :]

        num = [rows(j, PACK) + rows(SUBS + j, PACK) for j in range(SUBS)]
        den = [
            rows(blocks * PACK + j, SUBS) + rows(blocks * PACK + 4 + j, SUBS) for j in range(4)
        ]
        gains = solve(num, den, gains, target, penalty)
    for j in range(SUBS):
        total_ref[pl.ds(j, blocks, stride=SUBS), :] = gains[j]
    place = own_place()
    part = total_ref[pl.ds(pl.multiple_of(place * SUBS, SUBS), SUBS), :]
    gain_out_ref[...] = part
    combined, mark = part + own_ref[:SUBS, :], own_ref[SUBS:, :]
    sum_ref[...] = combined
    for channel in range(send_ref.shape[0] // SENT):
        send_ref[pl.ds(channel * SENT, SUBS), :] = combined
        send_ref[pl.ds(channel * SENT + SUBS, 1), :] = mark[:1]


def legendre(position):
    square = position * position
    return [None, position, 1.5 * square - 0.5, (2.5 * square - 1.5) * position]


def fit_kernel(gram_factor, parts_ref, own_ref, gain_ref, sum_ref, *refs):
    gain_hbm, consensus_hbm, dual_hbm, consensus_ref, dual_ref, sem = refs
    gain_copy = pltpu.make_async_copy(gain_ref, gain_hbm, sem.at[0])
    gain_copy.start()
    channels = parts_ref.shape[0] // SENT
    scale = float(channels) - 1.0

    def basis(channel):
        return legendre(2.0 * channel / scale - 1.0)

    moments = [None] * 4
    for channel in range(channels):
        value = parts_ref[pl.ds(channel * SENT, SUBS), :]
        for k, weight in enumerate(basis(parts_ref[pl.ds(channel * SENT + SUBS, 1), :])):
            add = value if weight is None else weight * value
            moments[k] = add if moments[k] is None else moments[k] + add
    middle = []
    for k in range(4):
        rest = moments[k]
        for earlier in range(k):
            rest = rest - gram_factor[k][earlier] * middle[earlier]
        middle.append(rest * (1.0 / gram_factor[k][k]))
    coeffs = [None] * 4
    for k in reversed(range(4)):
        rest = middle[k]
        for later in range(k + 1, 4):
            rest = rest - gram_factor[later][k] * coeffs[later]
        coeffs[k] = rest * (1.0 / gram_factor[k][k])
    own = basis(own_ref[SUBS:, :])
    fitted = coeffs[0]
    for k in range(1, 4):
        fitted = fitted + own[k] * coeffs[k]
    consensus_ref[...] = fitted
    dual_ref[...] = sum_ref[...] - fitted
    consensus_copy = pltpu.make_async_copy(consensus_ref, consensus_hbm, sem.at[1])
    dual_copy = pltpu.make_async_copy(dual_ref, dual_hbm, sem.at[2])
    consensus_copy.start()
    dual_copy.start()
    gain_copy.wait()
    consensus_copy.wait()
    dual_copy.wait()


def gram_cholesky(channels):
    x = 2.0 * np.arange(channels, dtype=np.float64) / (channels - 1.0) - 1.0
    basis = np.stack([np.ones_like(x), x, 1.5 * x * x - 0.5, (2.5 * x * x - 1.5) * x], -1)
    factor = np.linalg.cholesky(basis.T @ basis)
    return [[float(value) for value in row] for row in factor]


SPACES = {"s": pltpu.SMEM, "v": pltpu.VMEM, "h": pltpu.HBM}


def call(kernel, shapes, spaces, scratch=(), limit=8, micros=0):
    cost = pl.CostEstimate(
        flops=int(micros * 1.0e9), transcendentals=0, bytes_accessed=int(micros * 3.0e6)
    )
    run = pl.pallas_call(
        kernel,
        out_shape=shapes,
        in_specs=[pl.BlockSpec(memory_space=SPACES[space]) for space in spaces],
        out_specs=[pl.BlockSpec(memory_space=shape.memory_space) for shape in shapes],
        scratch_shapes=list(scratch),
        compiler_params=pltpu.CompilerParams(vmem_limit_bytes=limit << 20),
        cost_estimate=cost if micros else None,
    )

    def placed(*args):
        return run(
            *(
                arg if space == "s" else pltpu.with_memory_space_constraint(arg, SPACES[space])
                for arg, space in zip(args, spaces, strict=True)
            )
        )

    return placed


def shards(
    visibility,
    model_visibility,
    keep_mask,
    gains_in,
    consensus_in,
    dual_in,
    penalty,
    channel_index,
    first_station,
    second_station,
):
    baselines = visibility.shape[3]
    stations = gains_in.shape[2]
    slots = lax.axis_size("tm")
    channels = lax.axis_size("freq")
    tiles = baselines // LANES
    blocks = stations // LANES
    assert blocks == slots and blocks % 2 == 0 and channel_index.shape == (1,)
    vmem = pltpu.VMEM

    def swap(array, step):
        return lax.ppermute(array, "tm", [(i, i ^ step) for i in range(slots)])

    sizes = [tiles // 2, tiles // 2]
    pieces = []
    for index, size in enumerate(sizes):
        pieces += call(
            lambda *refs, start=sum(sizes[:index]): widen_kernel(start, *refs),
            [vmem((2 * size * SUBS, LANES), F32)],
            "hhh",
            [
                vmem((SUBS, size * LANES), BF16),
                vmem((SUBS, size * LANES), BF16),
                vmem((1, size * LANES), jnp.int32),
                pltpu.SemaphoreType.DMA((3,)),
            ],
            micros=0.001,
        )(
            visibility.reshape(SUBS, baselines),
            model_visibility.reshape(SUBS, baselines),
            keep_mask.reshape(1, baselines),
        )
    far = []
    for piece in pieces:
        got = []
        step = slots // 2
        while step > 1:
            got += [swap(array, step) for array in [piece, *got]]
            step //= 2
        far.append(got)
    gains, consensus, dual = (
        array.reshape(SUBS, stations) for array in (gains_in, consensus_in, dual_in)
    )
    products = [vmem((PRODS, size, LANES), F32) for size in sizes]
    terms = [vmem((2, size * TERMS, LANES), F32) for size in sizes]
    seen = vmem((2, SUBS, tiles, LANES), F32)
    station = vmem((tiles, LANES), jnp.int32)
    wide = vmem((SUBS, stations), F32)
    totals = vmem((blocks * 3 * PACK // 2, LANES), F32)
    count = len(sizes)
    tables = call(
        lambda *refs: tables_kernel(count, *refs),
        [
            vmem((2 * baselines, LANES), BF16),
            vmem((blocks * 3 * PACK // 2, 2 * baselines), BF16),
            seen,
            vmem(((2 * SUBS + 1) * SUBS, LANES), F32),
            vmem((2 * SUBS, LANES), F32),
            station,
            station,
        ],
        "v" * count + "shhhhhh",
        [wide, wide, wide, vmem((1, stations), F32), pltpu.SemaphoreType.DMA((6,))],
        limit=16,
        micros=1,
    )(
        *pieces,
        channel_index,
        first_station.reshape(tiles, LANES),
        second_station.reshape(tiles, LANES),
        gains,
        consensus,
        dual,
        penalty.reshape(1, stations),
    )
    summed = [None, None]
    hot, mask, found, state, own, first, second = tables
    pieces, state = lax.optimization_barrier((pieces, state))
    near = [swap(piece, 1) for piece in pieces]
    far[0], state = lax.optimization_barrier((far[0], state))
    last = [[swap(array, 1) for array in far[0]]]
    (summed[0],) = call(more_kernel, [products[0]], "v" * (2 + len(far[0])), micros=0.001)(
        pieces[0], near[0], *far[0]
    )
    far[1], last[0], found = lax.optimization_barrier((far[1], last[0], found))
    last.append([swap(array, 1) for array in far[1]])
    (summed[1],) = call(more_kernel, [products[1]], "v" * (2 + len(far[1])), micros=0.001)(
        pieces[1], near[1], *far[1]
    )
    summed[0], partial = call(
        lambda *refs: piece_kernel(0, *refs),
        [products[0], totals],
        "v" * (4 + len(last[0])),
        [terms[0]],
        limit=16,
        micros=0.001,
    )(hot, mask, found, summed[0], *last[0])
    part = vmem((SUBS, LANES), F32)
    gain_part, combined, send = call(
        lambda *refs: sweeps_kernel((count, len(last[1])), *refs),
        [part, part, vmem((channels * SENT, LANES), F32)],
        "v" * (10 + len(last[1])),
        [products[1], totals, *terms],
        limit=16,
    )(
        hot,
        mask,
        found,
        state,
        own,
        first,
        second,
        summed[0],
        partial,
        summed[1],
        *last[1],
    )
    parts = lax.all_to_all(send.reshape(channels, 1, SENT * LANES), "freq", 0, 0)
    parts = parts.reshape(channels * SENT, LANES)
    outs = call(
        lambda *refs: fit_kernel(gram_cholesky(channels), *refs),
        [pltpu.HBM((SUBS, LANES), F32)] * 3,
        "vvvv",
        [part, part, pltpu.SemaphoreType.DMA((3,))],
    )(parts, own, gain_part, combined)
    return tuple(array[None] for array in outs)


def solution(mesh):
    placed = (
        P("freq", "tm", None, None),
        P("freq", "tm", None, None),
        P("freq", "tm", None),
        P("freq", None, None),
        P("freq", None, None),
        P("freq", None, None),
        P(),
        P("freq"),
        P(),
        P(),
    )
    return jax.shard_map(
        shards,
        mesh=mesh,
        in_specs=placed,
        out_specs=(P("freq", None, "tm"), P("freq", None, "tm"), P("freq", None, "tm")),
        check_vma=False,
    )
```
